128 devices in a mesh: feat: 4 (over y), label: 32 (over z, x, core).
Axes of the slice: x: 4, y: 4, z: 4, core: 2. Of those that a mesh axis runs over, the one named last changes fastest.
Arguments:
- documents: bfloat16 [160, 1024], P(None, 'label'), may hold values from -6 to 6
- expand_weight: bfloat16 [1024, 32768], P('label', 'feat'), may hold values from -0.1875 to 0.1875
- sparse_weight: bfloat16 [3072, 16, 128, 128], P(('feat', 'label')), may hold values from -0.125 to 0.125
- feature_lists: int32 [3072, 16], replicated, may hold values from 0 to 255, as said below
- positives: int32 [160, 8], replicated, may hold values from 0 to 393215
Outputs:
- grad_expand: bfloat16 [1024, 32768], P('label', 'feat')
- grad_sparse: bfloat16 [3072, 16, 128, 128], P(('feat', 'label'))
The draws below stay inside these ranges and needn't reach their ends.
Inputs may be any that keep to these rules, and one draw needn't show every extreme that they name: `feature_lists`: within each aligned group of 24 label blocks (taken in order), the entries name exactly 24 distinct feature blocks from each range of 64 consecutive blocks, each named exactly 4 times in the group; the 16 entries of one label block are distinct.
All inputs are finite; a program needn't handle non-finite values.
Results may differ from the reference program's by a relative error of at most 0.014.
Values may be sent and summed in bfloat16 or wider, within the bound.
A program may use at most 192 MiB of HBM per device.

```python
import jax
import jax.numpy as jnp
from jax import lax

D = 1024
BLK = 128
FBLOCKS = 256
SLOTS = 16
LBLK_DEV = 24
CAP = 24
POS = 8
DOCS = 160
H = 32768
LBLKS = 3072
LABELS = 393216
N_FEAT = 4


def draw_feature_lists(key, part):
    groups = LBLKS // LBLK_DEV
    per_owner = FBLOCKS // N_FEAT
    pool_size = N_FEAT * CAP
    repeats = LBLK_DEV * SLOTS // pool_size

    def one_group(group_key):
        owner_keys = jax.random.split(jax.random.fold_in(group_key, 11), N_FEAT)
        chosen = jax.vmap(lambda owner_key: jax.random.permutation(owner_key, per_owner)[:CAP])(owner_keys)
        offsets = (jnp.arange(N_FEAT, dtype=jnp.int32) * per_owner)[:, None]
        pool = (chosen.astype(jnp.int32) + offsets).reshape(-1)
        order_keys = jax.random.split(jax.random.fold_in(group_key, 23), repeats)
        orders = jax.vmap(lambda order_key: jax.random.permutation(order_key, pool))(order_keys)
        return orders.reshape(LBLK_DEV, SLOTS).astype(jnp.int32)
    group_keys = jax.random.split(jax.random.fold_in(key, 5), groups)
    return jax.vmap(one_group)(group_keys).reshape(LBLKS, SLOTS).astype(jnp.int32)


def plant(result, key, low, largest):
    dims = result.shape
    index_at = [jax.random.randint(jax.random.fold_in(key, axis), (), 0, dims[axis]) for axis in range(len(dims))]
    result = result.at[tuple(index_at)].set(low)
    longest = dims.index(max(dims))
    index_at[longest] = (index_at[longest] + 1) % dims[longest]
    return result.at[tuple(index_at)].set(largest)


def block_scale(key, extent, cuts, smallest, top_value):
    def one(position, parts):
        draws = jax.random.uniform(jax.random.fold_in(jax.random.fold_in(key, 6), position), (parts,), jnp.float32, smallest / len(cuts), top_value / len(cuts))
        return jnp.repeat(jnp.exp(draws), extent[position] // parts).reshape((-1,) + (1,) * (len(extent) - position - 1))

    factor_of = one(*cuts[0])
    for cut in cuts[1:]:
        factor_of = factor_of * one(*cut)
    return factor_of


def gaussian(rng, shape, width, reach, cuts=(), held_as=jnp.bfloat16):
    gain = block_scale(rng, shape, cuts, -0.22, 0.18) if cuts else 1.0
    entries = jax.random.normal(rng, shape, jnp.float32) * width * gain
    return jnp.minimum(jnp.maximum(entries, -reach), reach).astype(held_as)


def setup_inputs(seed: int = 0) -> dict:
    key_of = jax.random.split(jax.random.key(seed), 6)
    return {
        "documents": gaussian(key_of[0], (DOCS, D), 1.0, 6.0, ((1, 32),)),
        "expand_weight": gaussian(key_of[1], (D, H), D ** -0.5, 0.1875, ((0, 32), (1, 4))),
        "sparse_weight": gaussian(key_of[2], (LBLKS, SLOTS, BLK, BLK), (SLOTS * BLK) ** -0.5, 0.125, ((0, 128),)),
        "feature_lists": draw_feature_lists(jax.random.fold_in(key_of[5], 71), 0),
        "positives": plant(jax.random.randint(key_of[4], (DOCS, POS), 0, LABELS), jax.random.fold_in(key_of[4], 1), 0, LABELS - 1).astype(jnp.int32),
    }


def reference(documents, expand_weight, sparse_weight, feature_lists, positives):
    expanded = jnp.dot(documents, expand_weight, preferred_element_type=jnp.float32)
    hidden = jnp.maximum(expanded, 0.0).astype(jnp.bfloat16)
    hidden_blocks = hidden.reshape(DOCS, FBLOCKS, BLK).transpose(1, 0, 2)
    groups = LBLKS // LBLK_DEV

    def group_step(carry, group):
        lists = lax.dynamic_slice_in_dim(feature_lists, group * LBLK_DEV, LBLK_DEV, 0)
        weights = lax.dynamic_slice_in_dim(sparse_weight, group * LBLK_DEV, LBLK_DEV, 0)
        picked = jnp.take(hidden_blocks, lists, axis=0)
        logits = jnp.einsum("lsdc,lsce->dle", picked.astype(jnp.float32), weights.astype(jnp.float32))
        label_ids = ((group * LBLK_DEV + jnp.arange(LBLK_DEV, dtype=jnp.int32))[:, None] * BLK
                     + jnp.arange(BLK, dtype=jnp.int32)[None, :]).astype(jnp.int32)
        targets = jnp.any(positives[:, :, None, None] == label_ids[None, None, :, :], axis=1).astype(jnp.float32)
        residual = (jax.nn.sigmoid(logits) - targets).astype(jnp.bfloat16)
        grad_block = jnp.einsum("lsdc,dle->lsce", picked.astype(jnp.float32), residual.astype(jnp.float32)).astype(jnp.bfloat16)
        back = jnp.einsum("dle,lsce->lsdc", residual.astype(jnp.float32), weights.astype(jnp.float32))
        partial_value = jax.ops.segment_sum(back.reshape(LBLK_DEV * SLOTS, DOCS, BLK), lists.reshape(-1), num_segments=FBLOCKS)
        partial_value = partial_value.astype(jnp.bfloat16)
        return carry + partial_value.astype(jnp.float32), grad_block

    start = jnp.zeros((FBLOCKS, DOCS, BLK), jnp.float32)
    block_grad, grad_blocks = lax.scan(group_step, start, jnp.arange(groups, dtype=jnp.int32))
    grad_sparse = grad_blocks.reshape(LBLKS, SLOTS, BLK, BLK)
    grad_hidden = jnp.where(hidden_blocks > 0, block_grad, 0.0).astype(jnp.bfloat16)
    grad_expand = jnp.einsum("dk,bdc->kbc", documents.astype(jnp.float32), grad_hidden.astype(jnp.float32))
    grad_expand = grad_expand.reshape(D, FBLOCKS * BLK).astype(jnp.bfloat16)
    return grad_expand, grad_sparse
```

```python
import functools

import jax
import jax.numpy as jnp
from jax import lax
from jax.experimental import pallas as pl
from jax.experimental.pallas import tpu as pltpu
from jax.sharding import Mesh
from jax.sharding import PartitionSpec as P

BLK = 128
FBLOCKS = 256
SLOTS = 16
LBLK_DEV = 24
POOL = 96
NAMED = 4
POS = 8
DOCS = 160
HALF = 80
SHARD = 320
RING = 4
AXES = ("feat", "label_0", "label_1", "label_2")
LABEL = AXES[1:]
MESH = pl.DeviceIdType.MESH
MIB = 1 << 20

PARTS = (((2, 0, 1), 0, 112), ((0, 1, 2), 112, 112), ((1, 2, 0), 224, 96))
PLANE_PARTS = (((0, 1), 0, 160), ((1, 0), 160, 160))


def hop(m, k):
    return lax.rem(m + k, RING)


def region(part, phase, here, t, half, lead=()):
    order, row, rows = part
    index = list(here)
    cut = rows // 32 * 16
    span = {None: (row, rows), 0: (row, rows - cut), 1: (row + rows - cut, cut)}
    low, size = span[half] if phase == 0 else (row, rows)
    for done in range(phase):
        index[order[done]] = slice(None)
    if phase > 0 and half is not None:
        index[order[phase - 1]] = pl.ds(2 * half, 2)
    index[order[phase]] = t
    return (*index, *lead, pl.ds(low, size), slice(None))


def ring_gather(buf, parts, here, axes, lead, send, recv, first_source, on_phase, on_chunk):
    def copy(p, phase, way, k, source_t, half, source=None):
        axis = parts[p][0][phase]
        at = region(parts[p], phase, here, source_t, half, lead)
        slot = ((p * len(axes) + phase) * 2 + way) * 3 + k
        src = buf.at[at] if source is None else source(p, half)
        return pltpu.make_async_remote_copy(
            src_ref=src,
            dst_ref=buf.at[at],
            send_sem=send.at[slot],
            recv_sem=recv.at[slot],
            device_id={axes[axis]: hop(here[axis], (1, 3)[way])},
            device_id_type=MESH,
        )

    for phase in range(len(axes)):
        source = first_source if phase == 0 else None
        started = []
        for k in range(2):
            for p in range(len(parts)):
                m = here[parts[p][0][phase]]
                for way in range(2):
                    op = copy(p, phase, way, k, m, k if way == 0 else 1 - k, source)
                    op.start()
                    started.append(op)
        on_phase(phase)
        for p in range(len(parts)):
            m = here[parts[p][0][phase]]
            for way in range(2):
                near = hop(m, (3, 1)[way])
                copy(p, phase, way, 0, near, way).wait_recv()
                op = copy(p, phase, way, 2, near, way)
                op.start()
                started.append(op)
        for p in range(len(parts)):
            m = here[parts[p][0][phase]]
            for way in range(2):
                near = hop(m, (3, 1)[way])
                copy(p, phase, way, 1, near, 1 - way).wait_recv()
                on_chunk(p, phase, near)
        for p in range(len(parts)):
            m = here[parts[p][0][phase]]
            for way in range(2):
                copy(p, phase, way, 2, hop(m, 2), way).wait_recv()
            on_chunk(p, phase, hop(m, 2))
        for op in started:
            op.wait_send()


def expand_kernel(
    docs_ref, weight_ref, hid_ref, docs_all, w_all, shard,
    w_send, w_recv, d_send, d_recv, own_sem, send, recv, sib_send, sib_recv,
):
    y, z, x, c = (lax.axis_index(a) for a in AXES)
    me = z * 8 + x * 2 + c
    sibling = {"label_2": 1 - c}

    def peer(l):
        return {
            "label_0": lax.div(l, 8),
            "label_1": lax.rem(lax.div(l, 2), 4),
            "label_2": lax.rem(l, 2),
        }

    barrier = pltpu.get_barrier_semaphore()

    def greet(o, carry):
        pl.semaphore_signal(
            barrier, inc=1, device_id=peer(lax.rem(me + o, 32)), device_id_type=MESH
        )
        return carry

    lax.fori_loop(1, 32, greet, 0)
    for k in (1, 3):
        pl.semaphore_signal(barrier, inc=1, device_id={"feat": hop(y, k)}, device_id_type=MESH)
    pl.semaphore_wait(barrier, 33)

    def rows_of(ref, l):
        return ref.at[pl.ds(pl.multiple_of(l * 32, 32), 32), :]

    def columns_for(l):
        return weight_ref.at[:, pl.ds(pl.multiple_of(l * 256, 256), 256)]

    def docs_copy(to, origin):
        return pltpu.make_async_remote_copy(
            src_ref=docs_ref, dst_ref=rows_of(docs_all, origin),
            send_sem=d_send.at[to], recv_sem=d_recv.at[origin],
            device_id=peer(to), device_id_type=MESH,
        )

    def weight_copy(to, origin):
        return pltpu.make_async_remote_copy(
            src_ref=columns_for(to), dst_ref=rows_of(w_all, origin),
            send_sem=w_send.at[to], recv_sem=w_recv.at[origin],
            device_id=peer(to), device_id_type=MESH,
        )

    def start(o, carry):
        to = lax.rem(me + o, 32)
        weight_copy(to, me).start()
        docs_copy(to, me).start()
        return carry

    lax.fori_loop(1, 32, start, 0)
    own_docs = pltpu.make_async_copy(docs_ref, rows_of(docs_all, me), own_sem.at[0])
    own_weight = pltpu.make_async_copy(columns_for(me), rows_of(w_all, me), own_sem.at[1])
    own_docs.start()
    own_weight.start()
    own_docs.wait()
    own_weight.wait()

    def finish(o, carry):
        other = lax.rem(me + o, 32)
        weight_copy(other, other).wait_recv()
        docs_copy(other, other).wait_recv()
        return carry

    lax.fori_loop(1, 32, finish, 0)
    product = lax.dot_general(
        docs_all[...], w_all[...], (((0,), (0,)), ((), ())), preferred_element_type=jnp.float32
    )
    hidden = jnp.maximum(product, 0.0).astype(jnp.bfloat16)
    shard[0:DOCS, :] = hidden[:DOCS, :BLK]
    shard[DOCS:SHARD, :] = hidden[:DOCS, BLK:]
    own_hidden = pltpu.make_async_copy(shard, hid_ref.at[y, z, x, c], own_sem.at[2])
    own_hidden.start()

    def first_source(p, half):
        return shard.at[region(PARTS[p], 0, (y, z, x), 0, half)[-2:]]

    siblings = []

    def to_sibling(p, k, t):
        at = region(PARTS[p], 2, (y, z, x), t, None, (c,))
        op = pltpu.make_async_remote_copy(
            src_ref=hid_ref.at[at], dst_ref=hid_ref.at[at],
            send_sem=sib_send.at[p * 4 + k], recv_sem=sib_recv.at[p * 4 + k],
            device_id=sibling, device_id_type=MESH,
        )
        op.start()
        siblings.append(op)

    def on_phase(phase):
        if phase == 0:
            own_hidden.wait()
        if phase == 2:
            for p in range(3):
                to_sibling(p, 0, (y, z, x)[PARTS[p][0][2]])

    count = [1, 1, 1]

    def on_chunk(p, phase, t):
        if phase == 2:
            to_sibling(p, count[p], t)
            count[p] += 1

    ring_gather(
        hid_ref, PARTS, (y, z, x), AXES[:3], (c,), send, recv, first_source, on_phase, on_chunk
    )
    for op in siblings:
        op.wait_send()
    for p in range(3):
        m = (y, z, x)[PARTS[p][0][2]]
        for k, t in enumerate((m, hop(m, 3), hop(m, 1), hop(m, 2))):
            at = region(PARTS[p], 2, (y, z, x), t, None, (1 - c,))
            pltpu.make_async_remote_copy(
                src_ref=hid_ref.at[at], dst_ref=hid_ref.at[at],
                send_sem=sib_send.at[p * 4 + k], recv_sem=sib_recv.at[p * 4 + k],
                device_id=sibling, device_id_type=MESH,
            ).wait_recv()

    def drain(o, carry):
        to = lax.rem(me + o, 32)
        weight_copy(to, me).wait_send()
        docs_copy(to, me).wait_send()
        return carry

    lax.fori_loop(1, 32, drain, 0)


def expand(docs_t, expand_weight):
    return pl.pallas_call(
        expand_kernel,
        out_shape=jax.ShapeDtypeStruct((4, 4, 4, 2, SHARD, BLK), jnp.bfloat16),
        in_specs=[pl.BlockSpec(memory_space=pltpu.VMEM), pl.BlockSpec(memory_space=pl.ANY)],
        out_specs=pl.BlockSpec(memory_space=pl.ANY),
        scratch_shapes=[
            pltpu.VMEM((1024, 256), jnp.bfloat16),
            pltpu.VMEM((1024, 256), jnp.bfloat16),
            pltpu.VMEM((SHARD, BLK), jnp.bfloat16),
            pltpu.SemaphoreType.DMA((32,)),
            pltpu.SemaphoreType.DMA((32,)),
            pltpu.SemaphoreType.DMA((32,)),
            pltpu.SemaphoreType.DMA((32,)),
            pltpu.SemaphoreType.DMA((3,)),
            pltpu.SemaphoreType.DMA((54,)),
            pltpu.SemaphoreType.DMA((54,)),
            pltpu.SemaphoreType.DMA((12,)),
            pltpu.SemaphoreType.DMA((12,)),
        ],
        compiler_params=pltpu.CompilerParams(
            collective_id=0, has_side_effects=True, vmem_limit_bytes=16 * MIB
        ),
        name="expand",
    )(docs_t, expand_weight)


def label_kernel(
    lists, blocks, named, base, pos_ref, hid_ref, weight_ref, gs_ref, gp_ref,
    h, h_t, w, res, pos_b, gp, place, h_sem, w_sem, gp_sem,
):
    g = pl.program_id(0)

    def block_copy(p):
        b = blocks[p]
        return pltpu.make_async_copy(hid_ref.at[b], h.at[p], h_sem.at[p])

    def weight_copy(q):
        return pltpu.make_async_copy(weight_ref.at[q], w.at[q], w_sem.at[q])

    @pl.when(g == 0)
    def _():
        def begin(p, carry):
            block_copy(p).start()
            place[blocks[p]] = p
            return carry

        lax.fori_loop(0, POOL, begin, 0)

        def begin_weight(q, carry):
            weight_copy(q).start()
            return carry

        lax.fori_loop(0, LBLK_DEV, begin_weight, 0)
        for k in range(POS):
            pos_b[k] = jnp.broadcast_to(pos_ref[:, k : k + 1], (DOCS, BLK))

        def arrive(p, carry):
            block_copy(p).wait()
            h_t[p] = h[p].T
            return carry

        lax.fori_loop(0, POOL, arrive, 0)

    weight_copy(g).wait()
    where = [place[lists[g * SLOTS + s]] for s in range(SLOTS)]
    logits = jnp.zeros((DOCS, BLK), jnp.float32)
    for s in range(0, SLOTS, 2):
        left = jnp.concatenate([h[where[s]], h[where[s + 1]]], axis=1)
        right = w[g, s : s + 2].reshape(2 * BLK, BLK)
        logits += jnp.dot(left, right, preferred_element_type=jnp.float32)
    ids = (base[0] + g) * BLK + lax.broadcasted_iota(jnp.int32, (DOCS, BLK), 1)
    hit = pos_b[0] == ids
    for k in range(1, POS):
        hit = jnp.logical_or(hit, pos_b[k] == ids)
    residual = (jax.nn.sigmoid(logits) - jnp.where(hit, 1.0, 0.0)).astype(jnp.bfloat16)
    res[g] = residual
    for s in range(SLOTS):
        gs_ref[0, s] = jnp.dot(
            h_t[where[s]], residual, preferred_element_type=jnp.float32
        ).astype(jnp.bfloat16)

    def gp_copy(f):
        return pltpu.make_async_copy(
            gp.at[pl.ds(f * 24, 24)], gp_ref.at[pl.ds(f * 24, 24)], gp_sem.at[f]
        )

    @pl.when(g == LBLK_DEV - 1)
    def _():
        for f in range(4):

            def collect(p, carry):
                slots = [named[p * NAMED + k] for k in range(NAMED)]
                pairs = [(lax.div(i, SLOTS), lax.rem(i, SLOTS)) for i in slots]
                left = jnp.concatenate([res[q] for q, _ in pairs], axis=1)
                right = jnp.concatenate([w[q, s] for q, s in pairs], axis=1)
                gp[p] = lax.dot_general(
                    left, right, (((1,), (1,)), ((), ())), preferred_element_type=jnp.float32
                ).astype(jnp.bfloat16)
                return carry

            lax.fori_loop(f * 24, f * 24 + 24, collect, 0)
            gp_copy(f).start()
        for f in range(4):
            gp_copy(f).wait()


def label_blocks(lists, blocks, named, base, positives, hid, sparse_weight):
    return pl.pallas_call(
        label_kernel,
        out_shape=(
            jax.ShapeDtypeStruct((LBLK_DEV, SLOTS, BLK, BLK), jnp.bfloat16),
            jax.ShapeDtypeStruct((POOL, DOCS, BLK), jnp.bfloat16),
        ),
        grid_spec=pltpu.PrefetchScalarGridSpec(
            num_scalar_prefetch=4,
            grid=(LBLK_DEV,),
            in_specs=[
                pl.BlockSpec((DOCS, POS), lambda g, *_: (0, 0)),
                pl.BlockSpec(memory_space=pl.ANY),
                pl.BlockSpec(memory_space=pl.ANY),
            ],
            out_specs=(
                pl.BlockSpec((1, SLOTS, BLK, BLK), lambda g, *_: (g, 0, 0, 0)),
                pl.BlockSpec(memory_space=pl.ANY),
            ),
            scratch_shapes=[
                pltpu.VMEM((POOL, DOCS, BLK), jnp.bfloat16),
                pltpu.VMEM((POOL, BLK, DOCS), jnp.bfloat16),
                pltpu.VMEM((LBLK_DEV, SLOTS, BLK, BLK), jnp.bfloat16),
                pltpu.VMEM((LBLK_DEV, DOCS, BLK), jnp.bfloat16),
                pltpu.VMEM((POS, DOCS, BLK), jnp.int32),
                pltpu.VMEM((POOL, DOCS, BLK), jnp.bfloat16),
                pltpu.SMEM((FBLOCKS,), jnp.int32),
                pltpu.SemaphoreType.DMA((POOL,)),
                pltpu.SemaphoreType.DMA((LBLK_DEV,)),
                pltpu.SemaphoreType.DMA((4,)),
            ],
        ),
        compiler_params=pltpu.CompilerParams(
            dimension_semantics=("arbitrary",), vmem_limit_bytes=48 * MIB
        ),
        name="label_blocks",
    )(lists, blocks, named, base, positives, hid, sparse_weight)


def reduce_kernel(
    table, gp_ref, hid_ref, docs_ref, out_ref,
    own, sib, acc, mask, full, *rest,
):
    bufs, (pair_sem, mask_sem, send, recv, g_send, g_recv, sib_send, sib_recv) = rest[:36], rest[36:]
    y, z, x, c = (lax.axis_index(a) for a in AXES)
    here = (y, z, x)
    sibling = {"label_2": 1 - c}
    barrier = pltpu.get_barrier_semaphore()
    for axis, m in zip(AXES, here):
        for k in (1, 3):
            pl.semaphore_signal(barrier, inc=1, device_id={axis: hop(m, k)}, device_id_type=MESH)
    pl.semaphore_signal(barrier, inc=1, device_id=sibling, device_id_type=MESH)
    pl.semaphore_wait(barrier, 7)

    def docs_half(k):
        return gp_ref.at[:, pl.ds(pl.multiple_of(k * HALF, 16), HALF), :]

    to_pair = pltpu.make_async_remote_copy(
        src_ref=docs_half(1 - c), dst_ref=sib.at[pl.ds(0, POOL)],
        send_sem=pair_sem.at[0], recv_sem=pair_sem.at[1],
        device_id=sibling, device_id_type=MESH,
    )
    to_pair.start()
    mine = pltpu.make_async_copy(docs_half(c), own.at[pl.ds(0, POOL)], pair_sem.at[2])
    mine.start()
    masks = []
    for blk in range(4):
        op = pltpu.make_async_copy(
            hid_ref.at[y, z, x, blk // 2, pl.ds(pl.multiple_of(blk % 2 * DOCS + c * HALF, 16), HALF), :],
            mask.at[pl.ds(blk * HALF, HALF), :],
            mask_sem.at[blk],
        )
        op.start()
        masks.append(op)
    own[POOL] = jnp.zeros((HALF, BLK), jnp.bfloat16)
    sib[POOL] = jnp.zeros((HALF, BLK), jnp.bfloat16)
    mine.wait()
    to_pair.wait()
    for op in masks:
        op.wait()

    def spread(q, carry):
        at = (lax.div(q, 16), lax.rem(lax.div(q, 4), 4), lax.rem(q, 4))
        for blk in range(4):
            b = q * 4 + blk
            acc[(*at, pl.ds(blk * HALF, HALF), slice(None))] = (
                own[table[b]] + sib[table[FBLOCKS + b]]
            )
        return carry

    lax.fori_loop(0, 64, spread, 0)

    def buf(p, phase, kind):
        return bufs[(p * 3 + phase) * 4 + kind]

    def inner(p, phase, half):
        at = region(PARTS[p], phase, here, 0, half)
        order, row, rows = PARTS[p]
        kept = [at[a] for a in range(3) if a in order[:phase]]
        cut = rows // 32 * 16
        span = (0, rows)
        if phase == 0 and half is not None:
            span = ((0, rows - cut), (rows - cut, cut))[half]
        return (*kept, pl.ds(*span), slice(None))

    def push(p, phase, way, k):
        axis = PARTS[p][0][phase]
        m = here[axis]
        near = hop(m, (1, 3)[way])
        t, half = ((hop(m, 2), way), (near, 1 - way), (near, way))[k]
        dst = buf(p, phase, way) if k == 0 else buf(p, phase, 2 + way).at[inner(p, phase, half)]
        slot = ((p * 3 + phase) * 2 + way) * 3 + k
        return pltpu.make_async_remote_copy(
            src_ref=acc.at[region(PARTS[p], phase, here, t, half)], dst_ref=dst,
            send_sem=send.at[slot], recv_sem=recv.at[slot],
            device_id={AXES[axis]: near}, device_id_type=MESH,
        )

    def tiles(p, phase, half, body):
        at = region(PARTS[p], phase, here, 0, half)
        order = PARTS[p][0]
        dims = [a for a in range(3) if a in order[:phase]]
        starts, sizes = [], []
        for a in dims:
            cut = at[a] if not isinstance(at[a], slice) else pl.ds(0, 4)
            starts.append(cut.start)
            sizes.append(cut.size)
        total = 1
        for size in sizes:
            total *= size

        def one(i, carry):
            local = []
            rest_i = i
            for size in reversed(sizes):
                local.insert(0, lax.rem(rest_i, size))
                rest_i = lax.div(rest_i, size)
            body(dims, starts, local)
            return carry

        if total == 1:
            body(dims, starts, [])
        else:
            lax.fori_loop(0, total, one, 0)

    def add_into(p, phase, t, half, sources):
        at = region(PARTS[p], phase, here, t, half)

        def body(dims, starts, local):
            index = list(at)
            for a, first, i in zip(dims, starts, local):
                index[a] = first + i
            total = acc[tuple(index)].astype(jnp.float32)
            for source, whole in sources:
                lead = [first + i for first, i in zip(starts, local)] if whole else local
                total = total + source[(*lead, slice(None), slice(None))].astype(jnp.float32)
            acc[tuple(index)] = total.astype(jnp.bfloat16)

        tiles(p, phase, half, body)

    for phase in (2, 1, 0):
        started = []
        for k in range(2):
            for p in range(3):
                for way in range(2):
                    op = push(p, phase, way, k)
                    op.start()
                    started.append(op)
        for p in range(3):
            m = here[PARTS[p][0][phase]]
            for way in range(2):
                push(p, phase, way, 0).wait_recv()
                add_into(p, phase, hop(m, (1, 3)[way]), way, [(buf(p, phase, way), False)])
                op = push(p, phase, way, 2)
                op.start()
                started.append(op)
        for p in range(3):
            m = here[PARTS[p][0][phase]]
            for way in range(2):
                push(p, phase, way, 1).wait_recv()
                push(p, phase, way, 2).wait_recv()
            add_into(
                p, phase, m, None, [(buf(p, phase, 2), True), (buf(p, phase, 3), True)]
            )
        for op in started:
            op.wait_send()

    total = acc[y, z, x]
    full[c, z, x] = jnp.where(mask[...] > 0, total, jnp.zeros_like(total))

    plane = (z, x)
    siblings = []

    def to_sibling(p, k, t, core):
        at = (core, *region(PLANE_PARTS[p], 1, plane, t, None))
        return pltpu.make_async_remote_copy(
            src_ref=full.at[at], dst_ref=full.at[at],
            send_sem=sib_send.at[p * 4 + k], recv_sem=sib_recv.at[p * 4 + k],
            device_id=sibling, device_id_type=MESH,
        )

    def on_phase(phase):
        if phase == 1:
            for p in range(2):
                op = to_sibling(p, 0, plane[PLANE_PARTS[p][0][1]], c)
                op.start()
                siblings.append(op)

    count = [1, 1]

    def on_chunk(p, phase, t):
        if phase == 1:
            op = to_sibling(p, count[p], t, c)
            op.start()
            siblings.append(op)
            count[p] += 1

    ring_gather(
        full.at[c], PLANE_PARTS, plane, LABEL[:2], (), g_send, g_recv, None, on_phase, on_chunk
    )
    for op in siblings:
        op.wait_send()
    for p in range(2):
        m = plane[PLANE_PARTS[p][0][1]]
        for k, t in enumerate((m, hop(m, 3), hop(m, 1), hop(m, 2))):
            to_sibling(p, k, t, 1 - c).wait_recv()

    docs = docs_ref[...]

    def last(q, carry):
        at = (lax.div(q, 4), lax.rem(q, 4))
        grads = [
            jnp.concatenate(
                [full[(half, *at, pl.ds(blk * HALF, HALF), slice(None))] for half in range(2)], axis=0
            )
            for blk in range(4)
        ]
        out_ref[:, pl.ds(pl.multiple_of(q * 512, 512), 512)] = jnp.dot(
            docs, jnp.concatenate(grads, axis=1), preferred_element_type=jnp.float32
        ).astype(jnp.bfloat16)
        return carry

    lax.fori_loop(0, 16, last, 0)


def reduce_blocks(table, gp, hid, docs_t):
    received = []
    for order, _, rows in PARTS:
        cut = rows // 32 * 16
        for phase in range(3):
            whole = [4] * phase + [rows, BLK]
            dims = sorted(order[:phase])
            for half in range(2):
                part = list(whole)
                if phase == 0:
                    part[0] = (rows - cut, cut)[half]
                else:
                    part[dims.index(order[phase - 1])] = 2
                received.append(pltpu.VMEM(tuple(part), jnp.bfloat16))
            received.extend([pltpu.VMEM(tuple(whole), jnp.bfloat16)] * 2)
    return pl.pallas_call(
        reduce_kernel,
        out_shape=jax.ShapeDtypeStruct((32, 8192), jnp.bfloat16),
        in_specs=[
            pl.BlockSpec(memory_space=pltpu.SMEM),
            pl.BlockSpec(memory_space=pl.ANY),
            pl.BlockSpec(memory_space=pl.ANY),
            pl.BlockSpec(memory_space=pltpu.VMEM),
        ],
        out_specs=pl.BlockSpec(memory_space=pltpu.VMEM),
        scratch_shapes=[
            pltpu.VMEM((POOL + 1, HALF, BLK), jnp.bfloat16),
            pltpu.VMEM((POOL + 1, HALF, BLK), jnp.bfloat16),
            pltpu.VMEM((4, 4, 4, SHARD, BLK), jnp.bfloat16),
            pltpu.VMEM((SHARD, BLK), jnp.bfloat16),
            pltpu.VMEM((2, 4, 4, SHARD, BLK), jnp.bfloat16),
            *received,
            pltpu.SemaphoreType.DMA((3,)),
            pltpu.SemaphoreType.DMA((4,)),
            pltpu.SemaphoreType.DMA((54,)),
            pltpu.SemaphoreType.DMA((54,)),
            pltpu.SemaphoreType.DMA((24,)),
            pltpu.SemaphoreType.DMA((24,)),
            pltpu.SemaphoreType.DMA((8,)),
            pltpu.SemaphoreType.DMA((8,)),
        ],
        compiler_params=pltpu.CompilerParams(
            collective_id=1, has_side_effects=True, vmem_limit_bytes=48 * MIB
        ),
        name="reduce_blocks",
    )(table, gp, hid, docs_t)


def on_device(documents, expand_weight, sparse_weight, feature_lists, positives):
    core = lax.axis_index("label_2")
    group = lax.axis_index(AXES)
    docs_t = documents.T
    hid = expand(jnp.pad(docs_t, ((0, 0), (0, 256 - DOCS))), expand_weight)
    pair = lax.dynamic_slice_in_dim(feature_lists, (group - core) * LBLK_DEV, 2 * LBLK_DEV, 0)
    pair = pair.reshape(2, LBLK_DEV * SLOTS)
    order = lax.sort(pair * 512 + jnp.arange(LBLK_DEV * SLOTS, dtype=jnp.int32)[None, :], dimension=1)
    blocks = order[:, ::NAMED] // 512
    own = lax.dynamic_index_in_dim(order, core, 0, keepdims=False)
    spots = jnp.arange(POOL, dtype=jnp.int32)[None, :, None] - POOL
    match = blocks[:, :, None] == jnp.arange(FBLOCKS, dtype=jnp.int32)[None, None, :]
    table = POOL + jnp.sum(jnp.where(match, spots, 0), axis=1)
    table = jnp.where(core == 0, table, table[::-1]).reshape(-1)
    grad_sparse, gp = label_blocks(
        lax.dynamic_index_in_dim(pair, core, 0, keepdims=False),
        lax.dynamic_index_in_dim(blocks, core, 0, keepdims=False),
        own % 512,
        (group * LBLK_DEV).astype(jnp.int32).reshape(1),
        positives,
        hid.reshape(FBLOCKS, DOCS, BLK),
        sparse_weight,
    )
    grad_expand = reduce_blocks(table, gp, hid, docs_t)
    return (grad_expand, grad_sparse)


def solution(mesh):
    finer = Mesh(mesh.devices.reshape(mesh.shape["feat"], 4, 4, 2), AXES)
    return jax.shard_map(
        on_device,
        mesh=finer,
        in_specs=(P(None, LABEL), P(LABEL, "feat"), P(AXES, None, None, None), P(), P()),
        out_specs=(P(LABEL, "feat"), P(AXES, None, None, None)),
        check_vma=False,
    )
```

```python
import functools

import jax
import jax.numpy as jnp
from jax import lax
from jax.experimental import pallas as pl
from jax.experimental.pallas import tpu as pltpu
from jax.sharding import Mesh
from jax.sharding import PartitionSpec as P

BLK = 128
FBLOCKS = 256
SLOTS = 16
LBLK_DEV = 24
POOL = 96
STEP = 4
NAMED = 4
POS = 8
DOCS = 160
HALF = 80
SHARD = 320
RING = 4
AXES = ("feat", "label_0", "label_1", "label_2")
LABEL = AXES[1:]
MESH = pl.DeviceIdType.MESH
MIB = 1 << 20

PARTS = (((2, 0, 1), 0, 112), ((0, 1, 2), 112, 112), ((1, 2, 0), 224, 96))


def hop(m, k):
    return lax.rem(m + k, RING)


def label_peer(l):
    return {
        "label_0": lax.div(l, 8),
        "label_1": lax.rem(lax.div(l, 2), 4),
        "label_2": lax.rem(l, 2),
    }


def region(part, phase, here, t, half, lead=()):
    order, row, rows = part
    index = list(here)
    cut = rows // 32 * 16
    span = {None: (row, rows), 0: (row, rows - cut), 1: (row + rows - cut, cut)}
    low, size = span[half] if phase == 0 else (row, rows)
    for done in range(phase):
        index[order[done]] = slice(None)
    if phase > 0 and half is not None:
        index[order[phase - 1]] = pl.ds(2 * half, 2)
    index[order[phase]] = t
    return (*index, *lead, pl.ds(low, size), slice(None))


def ring_gather(buf, parts, here, axes, lead, send, recv, first_source, on_phase, on_chunk):
    def copy(p, phase, way, k, source_t, half, source=None):
        axis = parts[p][0][phase]
        at = region(parts[p], phase, here, source_t, half, lead)
        slot = ((p * len(axes) + phase) * 2 + way) * 3 + k
        src = buf.at[at] if source is None else source(p, half)
        return pltpu.make_async_remote_copy(
            src_ref=src,
            dst_ref=buf.at[at],
            send_sem=send.at[slot],
            recv_sem=recv.at[slot],
            device_id={axes[axis]: hop(here[axis], (1, 3)[way])},
            device_id_type=MESH,
        )

    started = []
    for phase in range(len(axes)):
        source = first_source if phase == 0 else None
        for k in range(2):
            for p in range(len(parts)):
                m = here[parts[p][0][phase]]
                for way in range(2):
                    op = copy(p, phase, way, k, m, k if way == 0 else 1 - k, source)
                    op.start()
                    started.append(op)
        on_phase(phase)
        for p in range(len(parts)):
            m = here[parts[p][0][phase]]
            for way in range(2):
                near = hop(m, (3, 1)[way])
                copy(p, phase, way, 0, near, way).wait_recv()
                op = copy(p, phase, way, 2, near, way)
                op.start()
                started.append(op)
        for p in range(len(parts)):
            m = here[parts[p][0][phase]]
            for way in range(2):
                near = hop(m, (3, 1)[way])
                copy(p, phase, way, 1, near, 1 - way).wait_recv()
                on_chunk(p, phase, near)
        for p in range(len(parts)):
            m = here[parts[p][0][phase]]
            for way in range(2):
                copy(p, phase, way, 2, hop(m, 2), way).wait_recv()
            on_chunk(p, phase, hop(m, 2))
    for op in started:
        op.wait_send()


def expand_kernel(
    docs_ref, weight_ref, hid_ref, docs_all, mask_ref, w_all, shard,
    w_send, w_recv, d_send, d_recv, own_sem, send, recv, sib_send, sib_recv,
):
    y, z, x, c = (lax.axis_index(a) for a in AXES)
    me = z * 8 + x * 2 + c
    sibling = {"label_2": 1 - c}

    peer = label_peer
    barrier = pltpu.get_barrier_semaphore()

    def greet(o, carry):
        pl.semaphore_signal(
            barrier, inc=1, device_id=peer(lax.rem(me + o, 32)), device_id_type=MESH
        )
        return carry

    lax.fori_loop(1, 32, greet, 0)
    for k in (1, 3):
        pl.semaphore_signal(barrier, inc=1, device_id={"feat": hop(y, k)}, device_id_type=MESH)
    pl.semaphore_wait(barrier, 33)

    def rows_of(ref, l):
        return ref.at[lax.div(l, 2), lax.rem(l, 2)]

    def columns_for(l):
        return weight_ref.at[:, pl.ds(pl.multiple_of(l * 256, 256), 256)]

    def docs_copy(to, origin):
        return pltpu.make_async_remote_copy(
            src_ref=docs_ref, dst_ref=rows_of(docs_all, origin),
            send_sem=d_send.at[to], recv_sem=d_recv.at[origin],
            device_id=peer(to), device_id_type=MESH,
        )

    def docs_pair(core):
        return pltpu.make_async_remote_copy(
            src_ref=docs_all.at[:, core], dst_ref=docs_all.at[:, core],
            send_sem=own_sem.at[3], recv_sem=own_sem.at[4],
            device_id=sibling, device_id_type=MESH,
        )

    def weight_copy(to, origin):
        return pltpu.make_async_remote_copy(
            src_ref=columns_for(to), dst_ref=rows_of(w_all, origin),
            send_sem=w_send.at[to], recv_sem=w_recv.at[origin],
            device_id=peer(to), device_id_type=MESH,
        )

    def same_core(o):
        return lax.rem(me + 2 * o, 32)

    def start_docs(o, carry):
        docs_copy(same_core(o), me).start()
        return carry

    def start_weight(o, carry):
        weight_copy(lax.rem(me + o, 32), me).start()
        return carry

    lax.fori_loop(1, 16, start_docs, 0)
    lax.fori_loop(1, 32, start_weight, 0)
    own_docs = pltpu.make_async_copy(docs_ref, rows_of(docs_all, me), own_sem.at[0])
    own_weight = pltpu.make_async_copy(columns_for(me), rows_of(w_all, me), own_sem.at[1])
    own_docs.start()
    own_weight.start()
    own_docs.wait()
    own_weight.wait()

    def finish_docs(o, carry):
        docs_copy(same_core(o), same_core(o)).wait_recv()
        return carry

    def finish_weight(o, carry):
        other = lax.rem(me + o, 32)
        weight_copy(other, other).wait_recv()
        return carry

    lax.fori_loop(1, 16, finish_docs, 0)
    docs_pair(c).start()
    lax.fori_loop(1, 32, finish_weight, 0)
    docs_pair(1 - c).wait_recv()
    product = lax.dot_general(
        docs_all[...].reshape(1024, 256), w_all[...].reshape(1024, 256),
        (((0,), (0,)), ((), ())), preferred_element_type=jnp.float32,
    )
    hidden = jnp.maximum(product, 0.0).astype(jnp.bfloat16)
    shard[0:DOCS, :] = hidden[:DOCS, :BLK]
    shard[DOCS:SHARD, :] = hidden[:DOCS, BLK:]
    own_hidden = pltpu.make_async_copy(shard, hid_ref.at[y, z, x, c], own_sem.at[2])
    own_hidden.start()

    def first_source(p, half):
        return shard.at[region(PARTS[p], 0, (y, z, x), 0, half)[-2:]]

    siblings = []

    def to_sibling(p, k, t):
        at = region(PARTS[p], 2, (y, z, x), t, None, (c,))
        op = pltpu.make_async_remote_copy(
            src_ref=hid_ref.at[at], dst_ref=hid_ref.at[at],
            send_sem=sib_send.at[p * 4 + k], recv_sem=sib_recv.at[p * 4 + k],
            device_id=sibling, device_id_type=MESH,
        )
        op.start()
        siblings.append(op)

    def on_phase(phase):
        if phase == 0:
            own_hidden.wait()
        if phase == 2:
            for p in range(3):
                to_sibling(p, 0, (y, z, x)[PARTS[p][0][2]])

    count = [1, 1, 1]

    def on_chunk(p, phase, t):
        if phase == 2:
            to_sibling(p, count[p], t)
            count[p] += 1

    ring_gather(
        hid_ref, PARTS, (y, z, x), AXES[:3], (c,), send, recv, first_source, on_phase, on_chunk
    )
    for op in siblings:
        op.wait_send()
    for p in range(3):
        m = (y, z, x)[PARTS[p][0][2]]
        for k, t in enumerate((m, hop(m, 3), hop(m, 1), hop(m, 2))):
            at = region(PARTS[p], 2, (y, z, x), t, None, (1 - c,))
            pltpu.make_async_remote_copy(
                src_ref=hid_ref.at[at], dst_ref=hid_ref.at[at],
                send_sem=sib_send.at[p * 4 + k], recv_sem=sib_recv.at[p * 4 + k],
                device_id=sibling, device_id_type=MESH,
            ).wait_recv()

    docs_pair(c).wait_send()
    for blk in range(4):
        op = pltpu.make_async_copy(
            hid_ref.at[
                y, z, x, blk // 2,
                pl.ds(pl.multiple_of(blk % 2 * DOCS + c * HALF, 16), HALF), slice(None),
            ],
            mask_ref.at[pl.ds(blk * HALF, HALF), :],
            own_sem.at[blk],
        )
        op.start()
    for blk in range(4):
        pltpu.make_async_copy(
            mask_ref.at[pl.ds(blk * HALF, HALF), :], mask_ref.at[pl.ds(blk * HALF, HALF), :], own_sem.at[blk]
        ).wait()

    def drain_docs(o, carry):
        docs_copy(same_core(o), me).wait_send()
        return carry

    def drain_weight(o, carry):
        weight_copy(lax.rem(me + o, 32), me).wait_send()
        return carry

    lax.fori_loop(1, 16, drain_docs, 0)
    lax.fori_loop(1, 32, drain_weight, 0)


def expand(docs_t, expand_weight):
    return pl.pallas_call(
        expand_kernel,
        out_shape=(
            jax.ShapeDtypeStruct((4, 4, 4, 2, SHARD, BLK), jnp.bfloat16),
            jax.ShapeDtypeStruct((16, 2, 32, 256), jnp.bfloat16),
            jax.ShapeDtypeStruct((SHARD, BLK), jnp.bfloat16),
        ),
        in_specs=[pl.BlockSpec(memory_space=pltpu.VMEM), pl.BlockSpec(memory_space=pl.ANY)],
        out_specs=(
            pl.BlockSpec(memory_space=pl.ANY),
            pl.BlockSpec(memory_space=pltpu.VMEM),
            pl.BlockSpec(memory_space=pltpu.VMEM),
        ),
        scratch_shapes=[
            pltpu.VMEM((16, 2, 32, 256), jnp.bfloat16),
            pltpu.VMEM((SHARD, BLK), jnp.bfloat16),
            pltpu.SemaphoreType.DMA((32,)),
            pltpu.SemaphoreType.DMA((32,)),
            pltpu.SemaphoreType.DMA((32,)),
            pltpu.SemaphoreType.DMA((32,)),
            pltpu.SemaphoreType.DMA((5,)),
            pltpu.SemaphoreType.DMA((54,)),
            pltpu.SemaphoreType.DMA((54,)),
            pltpu.SemaphoreType.DMA((12,)),
            pltpu.SemaphoreType.DMA((12,)),
        ],
        compiler_params=pltpu.CompilerParams(
            collective_id=0, has_side_effects=True, vmem_limit_bytes=36 * MIB
        ),
        name="expand",
    )(docs_t, expand_weight)


def label_kernel(
    lists, blocks, named, base, pos_ref, hid_ref, weight_ref, gs_ref, gp_ref,
    h, h_t, w, res, pos_b, gp, place, h_sem, w_sem, gp_sem,
):
    g = pl.program_id(0)

    def block_copy(p):
        b = blocks[p]
        return pltpu.make_async_copy(hid_ref.at[b], h.at[p], h_sem.at[p])

    def weight_copy(q):
        return pltpu.make_async_copy(weight_ref.at[q], w.at[q], w_sem.at[q])

    @pl.when(g == 0)
    def _():
        def begin(p, carry):
            block_copy(p).start()
            place[blocks[p]] = p
            return carry

        lax.fori_loop(0, POOL, begin, 0)

        def begin_weight(q, carry):
            weight_copy(q).start()
            return carry

        lax.fori_loop(0, LBLK_DEV, begin_weight, 0)
        for k in range(POS):
            pos_b[k] = jnp.broadcast_to(pos_ref[:, k : k + 1], (DOCS, BLK))

        def arrive(p, carry):
            block_copy(p).wait()
            h_t[p] = h[p].T
            return carry

        lax.fori_loop(0, POOL, arrive, 0, unroll=8)

    rows = [g * STEP + k for k in range(STEP)]
    spots = [[place[lists[q * SLOTS + s]] for s in range(SLOTS)] for q in rows]
    for q in rows:
        weight_copy(q).wait()
    scores = []
    for q, where in zip(rows, spots):
        logits = jnp.zeros((DOCS, BLK), jnp.float32)
        for s in range(0, SLOTS, 2):
            left = jnp.concatenate([h[where[s]], h[where[s + 1]]], axis=1)
            right = w[q, s : s + 2].reshape(2 * BLK, BLK)
            logits += jnp.dot(left, right, preferred_element_type=jnp.float32)
        scores.append(logits)
    residuals = []
    for q, logits in zip(rows, scores):
        ids = (base[0] + q) * BLK + lax.broadcasted_iota(jnp.int32, (DOCS, BLK), 1)
        hit = pos_b[0] == ids
        for k in range(1, POS):
            hit = jnp.logical_or(hit, pos_b[k] == ids)
        residual = (jax.nn.sigmoid(logits) - jnp.where(hit, 1.0, 0.0)).astype(jnp.bfloat16)
        res[q] = residual
        residuals.append(residual)
    for k, (where, residual) in enumerate(zip(spots, residuals)):
        for s in range(SLOTS):
            gs_ref[k, s] = jnp.dot(
                h_t[where[s]], residual, preferred_element_type=jnp.float32
            ).astype(jnp.bfloat16)

    def gp_copy(f):
        return pltpu.make_async_copy(
            gp.at[pl.ds(f * 24, 24)], gp_ref.at[pl.ds(f * 24, 24)], gp_sem.at[f]
        )

    @pl.when(g == LBLK_DEV // STEP - 1)
    def _():
        for f in range(4):

            def collect(p, carry):
                slots = [named[p * NAMED + k] for k in range(NAMED)]
                pairs = [(lax.div(i, SLOTS), lax.rem(i, SLOTS)) for i in slots]
                left = jnp.concatenate([res[q] for q, _ in pairs], axis=1)
                right = jnp.concatenate([w[q, s] for q, s in pairs], axis=1)
                gp[p] = lax.dot_general(
                    left, right, (((1,), (1,)), ((), ())), preferred_element_type=jnp.float32
                ).astype(jnp.bfloat16)
                return carry

            lax.fori_loop(f * 24, f * 24 + 24, collect, 0, unroll=8)
            gp_copy(f).start()
        for f in range(4):
            gp_copy(f).wait()


def label_blocks(lists, blocks, named, base, positives, hid, sparse_weight):
    return pl.pallas_call(
        label_kernel,
        out_shape=(
            jax.ShapeDtypeStruct((LBLK_DEV, SLOTS, BLK, BLK), jnp.bfloat16),
            jax.ShapeDtypeStruct((POOL, DOCS, BLK), jnp.bfloat16),
        ),
        grid_spec=pltpu.PrefetchScalarGridSpec(
            num_scalar_prefetch=4,
            grid=(LBLK_DEV // STEP,),
            in_specs=[
                pl.BlockSpec((DOCS, POS), lambda g, *_: (0, 0)),
                pl.BlockSpec(memory_space=pl.ANY),
                pl.BlockSpec(memory_space=pl.ANY),
            ],
            out_specs=(
                pl.BlockSpec((STEP, SLOTS, BLK, BLK), lambda g, *_: (g, 0, 0, 0)),
                pl.BlockSpec(memory_space=pl.ANY),
            ),
            scratch_shapes=[
                pltpu.VMEM((POOL, DOCS, BLK), jnp.bfloat16),
                pltpu.VMEM((POOL, BLK, DOCS), jnp.bfloat16),
                pltpu.VMEM((LBLK_DEV, SLOTS, BLK, BLK), jnp.bfloat16),
                pltpu.VMEM((LBLK_DEV, DOCS, BLK), jnp.bfloat16),
                pltpu.VMEM((POS, DOCS, BLK), jnp.int32),
                pltpu.VMEM((POOL, DOCS, BLK), jnp.bfloat16),
                pltpu.SMEM((FBLOCKS,), jnp.int32),
                pltpu.SemaphoreType.DMA((POOL,)),
                pltpu.SemaphoreType.DMA((LBLK_DEV,)),
                pltpu.SemaphoreType.DMA((4,)),
            ],
        ),
        compiler_params=pltpu.CompilerParams(
            dimension_semantics=("arbitrary",), vmem_limit_bytes=36 * MIB
        ),
        name="label_blocks",
    )(lists, blocks, named, base, positives, hid, sparse_weight)


def reduce_kernel(
    table, gp_ref, mask, docs_ref, out_ref,
    own, sib, acc, grad, mine_grad, pieces, *rest,
):
    bufs, (pair_sem, mask_sem, send, recv, o_send, o_recv) = rest[:36], rest[36:]
    y, z, x, c = (lax.axis_index(a) for a in AXES)
    here = (y, z, x)
    sibling = {"label_2": 1 - c}
    me = z * 8 + x * 2 + c
    barrier = pltpu.get_barrier_semaphore()

    def greet(o, carry):
        pl.semaphore_signal(
            barrier, inc=1, device_id=label_peer(lax.rem(me + o, 32)), device_id_type=MESH
        )
        return carry

    lax.fori_loop(1, 32, greet, 0)
    for k in (1, 3):
        pl.semaphore_signal(barrier, inc=1, device_id={"feat": hop(y, k)}, device_id_type=MESH)

    def docs_half(k):
        return gp_ref.at[:, pl.ds(pl.multiple_of(k * HALF, 16), HALF), :]

    to_pair = pltpu.make_async_remote_copy(
        src_ref=docs_half(1 - c), dst_ref=sib.at[pl.ds(0, POOL)],
        send_sem=pair_sem.at[0], recv_sem=pair_sem.at[1],
        device_id=sibling, device_id_type=MESH,
    )
    mine = pltpu.make_async_copy(docs_half(c), own.at[pl.ds(0, POOL)], pair_sem.at[2])
    mine.start()
    own[POOL] = jnp.zeros((HALF, BLK), jnp.bfloat16)
    sib[POOL] = jnp.zeros((HALF, BLK), jnp.bfloat16)
    pl.semaphore_wait(barrier, 33)
    to_pair.start()
    mine.wait()
    to_pair.wait()

    def spread(q, carry):
        at = (lax.div(q, 16), lax.rem(lax.div(q, 4), 4), lax.rem(q, 4))
        for blk in range(4):
            b = q * 4 + blk
            acc[(*at, pl.ds(blk * HALF, HALF), slice(None))] = (
                own[table[b]] + sib[table[FBLOCKS + b]]
            )
        return carry

    lax.fori_loop(0, 64, spread, 0)

    def buf(p, phase, kind):
        return bufs[(p * 3 + phase) * 4 + kind]

    def inner(p, phase, half):
        at = region(PARTS[p], phase, here, 0, half)
        order, row, rows = PARTS[p]
        kept = [at[a] for a in range(3) if a in order[:phase]]
        cut = rows // 32 * 16
        span = (0, rows)
        if phase == 0 and half is not None:
            span = ((0, rows - cut), (rows - cut, cut))[half]
        return (*kept, pl.ds(*span), slice(None))

    def push(p, phase, way, k):
        axis = PARTS[p][0][phase]
        m = here[axis]
        near = hop(m, (1, 3)[way])
        t, half = ((hop(m, 2), way), (near, 1 - way), (near, way))[k]
        dst = buf(p, phase, way) if k == 0 else buf(p, phase, 2 + way).at[inner(p, phase, half)]
        slot = ((p * 3 + phase) * 2 + way) * 3 + k
        return pltpu.make_async_remote_copy(
            src_ref=acc.at[region(PARTS[p], phase, here, t, half)], dst_ref=dst,
            send_sem=send.at[slot], recv_sem=recv.at[slot],
            device_id={AXES[axis]: near}, device_id_type=MESH,
        )

    def tiles(p, phase, half, body):
        at = region(PARTS[p], phase, here, 0, half)
        order = PARTS[p][0]
        dims = [a for a in range(3) if a in order[:phase]]
        starts, sizes = [], []
        for a in dims:
            cut = at[a] if not isinstance(at[a], slice) else pl.ds(0, 4)
            starts.append(cut.start)
            sizes.append(cut.size)
        total = 1
        for size in sizes:
            total *= size

        def one(i, carry):
            local = []
            rest_i = i
            for size in reversed(sizes):
                local.insert(0, lax.rem(rest_i, size))
                rest_i = lax.div(rest_i, size)
            body(dims, starts, local)
            return carry

        if total == 1:
            body(dims, starts, [])
        else:
            lax.fori_loop(0, total, one, 0)

    def add_into(p, phase, t, half, sources):
        at = region(PARTS[p], phase, here, t, half)

        def body(dims, starts, local):
            index = list(at)
            for a, first, i in zip(dims, starts, local):
                index[a] = first + i
            total = acc[tuple(index)].astype(jnp.float32)
            for source, whole in sources:
                lead = [first + i for first, i in zip(starts, local)] if whole else local
                total = total + source[(*lead, slice(None), slice(None))].astype(jnp.float32)
            acc[tuple(index)] = total.astype(jnp.bfloat16)

        tiles(p, phase, half, body)

    started = []
    for phase in (2, 1, 0):
        for k in range(2):
            for p in range(3):
                for way in range(2):
                    op = push(p, phase, way, k)
                    op.start()
                    started.append(op)
        for p in range(3):
            m = here[PARTS[p][0][phase]]
            for way in range(2):
                push(p, phase, way, 0).wait_recv()
                add_into(p, phase, hop(m, (1, 3)[way]), way, [(buf(p, phase, way), False)])
                op = push(p, phase, way, 2)
                op.start()
                started.append(op)
        for p in range(3):
            m = here[PARTS[p][0][phase]]
            for way in range(2):
                push(p, phase, way, 1).wait_recv()
                push(p, phase, way, 2).wait_recv()
            add_into(
                p, phase, m, None, [(buf(p, phase, 2), True), (buf(p, phase, 3), True)]
            )

    total = acc[y, z, x]
    grad[...] = jnp.where(mask[...] > 0, total, jnp.zeros_like(total))

    def columns(k):
        return grad.at[pl.ds(pl.multiple_of(k * DOCS, 16), DOCS), :]

    def pair_grad(k, core):
        return pltpu.make_async_remote_copy(
            src_ref=columns(k), dst_ref=mine_grad.at[core],
            send_sem=pair_sem.at[3], recv_sem=pair_sem.at[4],
            device_id=sibling, device_id_type=MESH,
        )

    to_other = pair_grad(1 - c, c)
    to_other.start()
    kept = pltpu.make_async_copy(columns(c), mine_grad.at[c], pair_sem.at[5])
    kept.start()
    kept.wait()
    pair_grad(c, 1 - c).wait_recv()
    sides = [
        jnp.concatenate([mine_grad[half, pl.ds(j * HALF, HALF), :] for half in range(2)], axis=0)
        for j in range(2)
    ]
    right = jnp.concatenate(sides, axis=1)

    def out_columns(l):
        return out_ref.at[:, pl.ds(pl.multiple_of(l * 256, 256), 256)]

    def out_copy(to, origin):
        return pltpu.make_async_remote_copy(
            src_ref=pieces.at[to], dst_ref=out_columns(origin),
            send_sem=o_send.at[to], recv_sem=o_recv.at[origin],
            device_id=label_peer(to), device_id_type=MESH,
        )

    own_out = pltpu.make_async_copy(pieces.at[me], out_columns(me), pair_sem.at[6])
    for k in range(4):
        row = hop(z, k) * 8
        left = docs_ref[pl.ds(hop(z, k) * 4, 4)].reshape(256, 256)[:, :DOCS]
        pieces[pl.ds(row, 8)] = jnp.dot(
            left, right, preferred_element_type=jnp.float32
        ).astype(jnp.bfloat16).reshape(8, 32, 256)

        def deliver(o, carry):
            out_copy(row + lax.rem(x * 2 + c + o, 8), me).start()
            return carry

        lax.fori_loop(1 if k == 0 else 0, 8, deliver, 0)
        if k == 0:
            own_out.start()
    own_out.wait()

    def collect(o, carry):
        other = lax.rem(me + o, 32)
        out_copy(other, other).wait_recv()
        return carry

    def drain(o, carry):
        out_copy(lax.rem(me + o, 32), me).wait_send()
        return carry

    lax.fori_loop(1, 32, collect, 0)
    to_other.wait_send()
    for op in started:
        op.wait_send()
    lax.fori_loop(1, 32, drain, 0)


def reduce_blocks(table, gp, mask, docs_all):
    received = []
    for order, _, rows in PARTS:
        cut = rows // 32 * 16
        for phase in range(3):
            whole = [4] * phase + [rows, BLK]
            dims = sorted(order[:phase])
            for half in range(2):
                part = list(whole)
                if phase == 0:
                    part[0] = (rows - cut, cut)[half]
                else:
                    part[dims.index(order[phase - 1])] = 2
                received.append(pltpu.VMEM(tuple(part), jnp.bfloat16))
            received.extend([pltpu.VMEM(tuple(whole), jnp.bfloat16)] * 2)
    return pl.pallas_call(
        reduce_kernel,
        out_shape=jax.ShapeDtypeStruct((32, 8192), jnp.bfloat16),
        in_specs=[
            pl.BlockSpec(memory_space=pltpu.SMEM),
            pl.BlockSpec(memory_space=pl.ANY),
            pl.BlockSpec(memory_space=pltpu.VMEM),
            pl.BlockSpec(memory_space=pltpu.VMEM),
        ],
        out_specs=pl.BlockSpec(memory_space=pltpu.VMEM),
        scratch_shapes=[
            pltpu.VMEM((POOL + 1, HALF, BLK), jnp.bfloat16),
            pltpu.VMEM((POOL + 1, HALF, BLK), jnp.bfloat16),
            pltpu.VMEM((4, 4, 4, SHARD, BLK), jnp.bfloat16),
            pltpu.VMEM((SHARD, BLK), jnp.bfloat16),
            pltpu.VMEM((2, DOCS, BLK), jnp.bfloat16),
            pltpu.VMEM((32, 32, 256), jnp.bfloat16),
            *received,
            pltpu.SemaphoreType.DMA((7,)),
            pltpu.SemaphoreType.DMA((4,)),
            pltpu.SemaphoreType.DMA((54,)),
            pltpu.SemaphoreType.DMA((54,)),
            pltpu.SemaphoreType.DMA((32,)),
            pltpu.SemaphoreType.DMA((32,)),
        ],
        compiler_params=pltpu.CompilerParams(
            collective_id=1, has_side_effects=True, vmem_limit_bytes=24 * MIB
        ),
        name="reduce_blocks",
    )(table, gp, mask, docs_all)


def on_device(documents, expand_weight, sparse_weight, feature_lists, positives):
    core = lax.axis_index("label_2")
    group = lax.axis_index(AXES)
    docs_t = documents.T
    hid, docs_all, mask = expand(jnp.pad(docs_t, ((0, 0), (0, 256 - DOCS))), expand_weight)
    pair = lax.dynamic_slice_in_dim(feature_lists, (group - core) * LBLK_DEV, 2 * LBLK_DEV, 0)
    pair = pair.reshape(2, LBLK_DEV * SLOTS)
    order = lax.sort(pair * 512 + jnp.arange(LBLK_DEV * SLOTS, dtype=jnp.int32)[None, :], dimension=1)
    blocks = order[:, ::NAMED] // 512
    own = lax.dynamic_index_in_dim(order, core, 0, keepdims=False)
    spots = jnp.arange(POOL, dtype=jnp.int32)[None, :, None] - POOL
    match = blocks[:, :, None] == jnp.arange(FBLOCKS, dtype=jnp.int32)[None, None, :]
    table = POOL + jnp.sum(jnp.where(match, spots, 0), axis=1)
    table = jnp.where(core == 0, table, table[::-1]).reshape(-1)
    grad_sparse, gp = label_blocks(
        lax.dynamic_index_in_dim(pair, core, 0, keepdims=False),
        lax.dynamic_index_in_dim(blocks, core, 0, keepdims=False),
        own % 512,
        (group * LBLK_DEV).astype(jnp.int32).reshape(1),
        positives,
        hid.reshape(FBLOCKS, DOCS, BLK),
        sparse_weight,
    )
    grad_expand = reduce_blocks(table, gp, mask, docs_all)
    return (grad_expand, grad_sparse)


def solution(mesh):
    finer = Mesh(mesh.devices.reshape(mesh.shape["feat"], 4, 4, 2), AXES)
    return jax.shard_map(
        on_device,
        mesh=finer,
        in_specs=(P(None, LABEL), P(LABEL, "feat"), P(AXES, None, None, None), P(), P()),
        out_specs=(P(LABEL, "feat"), P(AXES, None, None, None)),
        check_vma=False,
    )
```

```python
import functools

import jax
import jax.numpy as jnp
from jax import lax
from jax.experimental import pallas as pl
from jax.experimental.pallas import tpu as pltpu
from jax.sharding import Mesh
from jax.sharding import PartitionSpec as P

BLK = 128
FBLOCKS = 256
SLOTS = 16
LBLK_DEV = 24
POOL = 96
STEP = 4
NAMED = 4
POS = 8
DOCS = 160
HALF = 80
SHARD = 320
RING = 4
AXES = ("feat", "label_0", "label_1", "label_2")
LABEL = AXES[1:]
MESH = pl.DeviceIdType.MESH
MIB = 1 << 20

PARTS = (((2, 0, 1), 0, 112), ((0, 1, 2), 112, 112), ((1, 2, 0), 224, 96))
NEAR, BACK = (1, 3, 2), (3, 1, 2)
LINES = (0, 3, 1, 2)


def hop(m, k):
    return lax.rem(m + k, RING)


def label_peer(l):
    return {
        "label_0": lax.div(l, 8),
        "label_1": lax.rem(lax.div(l, 2), 4),
        "label_2": lax.rem(l, 2),
    }


def cell(part, ta, tb, tc, lead=()):
    order, row, rows = part
    index = [None] * 3
    for axis, t in zip(order, (ta, tb, tc)):
        index[axis] = t
    return (*index, *lead, pl.ds(row, rows), slice(None))


def two(half):
    return pl.ds(2 * half, 2)


def rank_tables(keys, tables_ref):
    count = LBLK_DEV * SLOTS
    turned = keys.T
    tables_ref[...] = jnp.zeros((8, count), jnp.int32)
    lanes = lax.broadcasted_iota(jnp.int32, (count, count), 1)
    for r in range(2):
        row, col = keys[r : r + 1, :], turned[:, r : r + 1]
        below = jnp.sum(jnp.where(row < col, 1.0, 0.0), axis=1, keepdims=True).astype(jnp.int32)
        if r == 0:
            sort = jnp.where(below == lanes, col.astype(jnp.float32), 0.0)
            tables_ref[0:1, :] = jnp.sum(sort, axis=0, keepdims=True).astype(jnp.int32)
            above = jnp.sum(jnp.where(col < row, 1.0, 0.0), axis=0, keepdims=True)
            tables_ref[1:2, :] = lax.shift_right_logical(above.astype(jnp.int32), 2)
        place = lax.shift_right_logical(below, 2)
        first = jnp.where(place * NAMED == below, place - POOL, 0).astype(jnp.float32)
        hit = lax.shift_right_logical(col, 9) == lanes[:, :FBLOCKS]
        table = jnp.sum(jnp.where(hit, first, 0.0), axis=0, keepdims=True)
        tables_ref[2 + r : 3 + r, 0:FBLOCKS] = table.astype(jnp.int32) + POOL


def expand_kernel(
    keys_ref, docs_in, weight_ref, hid_ref, docs_all, mask_ref, tables_ref, docs_ref, w_all, shard,
    w_send, w_recv, d_send, d_recv, own_sem, send, recv, sib_send, sib_recv,
):
    y, z, x, c = (lax.axis_index(a) for a in AXES)
    here = (y, z, x)
    me = z * 8 + x * 2 + c
    sibling = {"label_2": 1 - c}
    peer = label_peer
    docs_ref[:, 0:DOCS] = docs_in[...]
    docs_ref[:, DOCS:] = jnp.zeros((32, 256 - DOCS), jnp.bfloat16)
    barrier = pltpu.get_barrier_semaphore()

    def greet(o, carry):
        pl.semaphore_signal(
            barrier, inc=1, device_id=peer(lax.rem(me + o, 32)), device_id_type=MESH
        )
        return carry

    lax.fori_loop(1, 32, greet, 0)
    for k in (1, 2, 3):
        pl.semaphore_signal(barrier, inc=1, device_id={"feat": hop(y, k)}, device_id_type=MESH)
    pl.semaphore_wait(barrier, 34)

    def rows_of(ref, l):
        return ref.at[lax.div(l, 2), lax.rem(l, 2)]

    def columns_for(l):
        return weight_ref.at[:, pl.ds(pl.multiple_of(l * 256, 256), 256)]

    def docs_copy(to, origin):
        return pltpu.make_async_remote_copy(
            src_ref=docs_ref, dst_ref=rows_of(docs_all, origin),
            send_sem=d_send.at[to], recv_sem=d_recv.at[origin],
            device_id=peer(to), device_id_type=MESH,
        )

    def docs_pair(core):
        return pltpu.make_async_remote_copy(
            src_ref=docs_all.at[:, core], dst_ref=docs_all.at[:, core],
            send_sem=own_sem.at[3], recv_sem=own_sem.at[4],
            device_id=sibling, device_id_type=MESH,
        )

    def weight_copy(to, origin):
        return pltpu.make_async_remote_copy(
            src_ref=columns_for(to), dst_ref=rows_of(w_all, origin),
            send_sem=w_send.at[to], recv_sem=w_recv.at[origin],
            device_id=peer(to), device_id_type=MESH,
        )

    def same_core(o):
        return lax.rem(me + 2 * o, 32)

    def start_docs(o, carry):
        docs_copy(same_core(o), me).start()
        return carry

    def start_weight(o, carry):
        weight_copy(lax.rem(me + o, 32), me).start()
        return carry

    lax.fori_loop(1, 16, start_docs, 0)
    lax.fori_loop(1, 32, start_weight, 0)
    own_docs = pltpu.make_async_copy(docs_ref, rows_of(docs_all, me), own_sem.at[0])
    own_weight = pltpu.make_async_copy(columns_for(me), rows_of(w_all, me), own_sem.at[1])
    own_docs.start()
    own_weight.start()
    rank_tables(keys_ref[...], tables_ref)
    own_docs.wait()
    own_weight.wait()

    def finish_docs(o, carry):
        docs_copy(same_core(o), same_core(o)).wait_recv()
        return carry

    def finish_weight(o, carry):
        other = lax.rem(me + o, 32)
        weight_copy(other, other).wait_recv()
        return carry

    lax.fori_loop(1, 16, finish_docs, 0)
    docs_pair(c).start()
    lax.fori_loop(1, 32, finish_weight, 0)
    docs_pair(1 - c).wait_recv()
    product = lax.dot_general(
        docs_all[...].reshape(1024, 256), w_all[...].reshape(1024, 256),
        (((0,), (0,)), ((), ())), preferred_element_type=jnp.float32,
    )
    hidden = jnp.maximum(product, 0.0).astype(jnp.bfloat16)
    shard[0:DOCS, :] = hidden[:DOCS, :BLK]
    shard[DOCS:SHARD, :] = hidden[:DOCS, BLK:]
    own_hidden = pltpu.make_async_copy(shard, hid_ref.at[y, z, x, c], own_sem.at[2])
    own_hidden.start()

    started = []

    def copy(at, slot, axis, k, source=None):
        return pltpu.make_async_remote_copy(
            src_ref=hid_ref.at[at] if source is None else source,
            dst_ref=hid_ref.at[at],
            send_sem=send.at[slot],
            recv_sem=recv.at[slot],
            device_id={AXES[axis]: hop(here[axis], k)},
            device_id_type=MESH,
        )

    def go(op):
        op.start()
        started.append(op)

    def coords(p):
        return tuple(here[axis] for axis in PARTS[p][0])

    def first(p, way, origin, source=None):
        a, b, t = coords(p)
        return copy(
            cell(PARTS[p], origin, b, t, (c,)), p * 3 + way, PARTS[p][0][0], NEAR[way], source
        )

    def second(p, way, k, line, half):
        t = coords(p)[2]
        at = cell(PARTS[p], two(half), line, t, (c,))
        return copy(at, 9 + (p * 2 + way) * 3 + k, PARTS[p][0][1], NEAR[way])

    def third(p, sub, way, k, t, half):
        line = hop(coords(p)[1], LINES[sub])
        at = cell(PARTS[p], two(half), line, t, (c,))
        return copy(at, 27 + ((p * 4 + sub) * 2 + way) * 3 + k, PARTS[p][0][2], NEAR[way])

    def pair_copy(p, k, at):
        return pltpu.make_async_remote_copy(
            src_ref=hid_ref.at[at], dst_ref=hid_ref.at[at],
            send_sem=sib_send.at[p * 13 + k], recv_sem=sib_recv.at[p * 13 + k],
            device_id=sibling, device_id_type=MESH,
        )

    def pair_plane(p, core):
        return pair_copy(p, 0, cell(PARTS[p], slice(None), slice(None), coords(p)[2], (core,)))

    def pair_line(p, sub, way, core):
        _, b, t = coords(p)
        at = cell(PARTS[p], slice(None), hop(b, LINES[sub]), hop(t, BACK[way]), (core,))
        return pair_copy(p, 1 + sub * 3 + way, at)

    def send_line(p, sub):
        for k in range(2):
            for way in range(2):
                go(third(p, sub, way, k, coords(p)[2], way if k == 0 else 1 - way))

    def pass_line(p, sub):
        for way in range(2):
            near = hop(coords(p)[2], BACK[way])
            third(p, sub, way, 0, near, way).wait_recv()
            go(third(p, sub, way, 2, near, way))

    def finish_line(p, sub):
        for way in range(2):
            third(p, sub, way, 1, hop(coords(p)[2], BACK[way]), 1 - way).wait_recv()
            go(pair_line(p, sub, way, c))
        for way in range(2):
            third(p, sub, way, 2, hop(coords(p)[2], 2), way).wait_recv()
        go(pair_line(p, sub, 2, c))

    parts = range(3)
    for way in (2, 0, 1):
        for p in parts:
            _, row, rows = PARTS[p]
            go(first(p, way, coords(p)[0], shard.at[pl.ds(row, rows), :]))
    own_hidden.wait()
    for p in parts:
        a, b, t = coords(p)
        for way in range(3):
            first(p, way, hop(a, BACK[way])).wait_recv()
        for k in range(2):
            for way in range(2):
                go(second(p, way, k, b, way if k == 0 else 1 - way))
        send_line(p, 0)
    for p in parts:
        b = coords(p)[1]
        for way in range(2):
            near = hop(b, BACK[way])
            second(p, way, 0, near, way).wait_recv()
            go(second(p, way, 2, near, way))
    for p in parts:
        pass_line(p, 0)
    for p in parts:
        b = coords(p)[1]
        for way in range(2):
            second(p, way, 1, hop(b, BACK[way]), 1 - way).wait_recv()
            send_line(p, 1 + way)
    for p in parts:
        for way in range(2):
            second(p, way, 2, hop(coords(p)[1], 2), way).wait_recv()
        send_line(p, 3)
        go(pair_plane(p, c))
    for sub in (1, 2):
        for p in parts:
            pass_line(p, sub)
    for p in parts:
        finish_line(p, 0)
    for p in parts:
        pass_line(p, 3)
    for sub in (1, 2, 3):
        for p in parts:
            finish_line(p, sub)
    for p in parts:
        pair_plane(p, 1 - c).wait_recv()
        for sub in range(4):
            for way in range(3):
                pair_line(p, sub, way, 1 - c).wait_recv()
    for op in started:
        op.wait_send()
    docs_pair(c).wait_send()
    for blk in range(4):
        op = pltpu.make_async_copy(
            hid_ref.at[
                y, z, x, blk // 2,
                pl.ds(pl.multiple_of(blk % 2 * DOCS + c * HALF, 16), HALF), slice(None),
            ],
            mask_ref.at[pl.ds(blk * HALF, HALF), :],
            own_sem.at[blk],
        )
        op.start()
    for blk in range(4):
        pltpu.make_async_copy(
            mask_ref.at[pl.ds(blk * HALF, HALF), :], mask_ref.at[pl.ds(blk * HALF, HALF), :], own_sem.at[blk]
        ).wait()

    def drain_docs(o, carry):
        docs_copy(same_core(o), me).wait_send()
        return carry

    def drain_weight(o, carry):
        weight_copy(lax.rem(me + o, 32), me).wait_send()
        return carry

    lax.fori_loop(1, 16, drain_docs, 0)
    lax.fori_loop(1, 32, drain_weight, 0)


def expand(keys, docs_t, expand_weight):
    vmem = pl.BlockSpec(memory_space=pltpu.VMEM)
    return pl.pallas_call(
        expand_kernel,
        out_shape=(
            jax.ShapeDtypeStruct((4, 4, 4, 2, SHARD, BLK), jnp.bfloat16),
            jax.ShapeDtypeStruct((16, 2, 32, 256), jnp.bfloat16),
            jax.ShapeDtypeStruct((SHARD, BLK), jnp.bfloat16),
            jax.ShapeDtypeStruct((8, LBLK_DEV * SLOTS), jnp.int32),
        ),
        in_specs=[vmem, vmem, pl.BlockSpec(memory_space=pltpu.HBM)],
        out_specs=(pl.BlockSpec(memory_space=pl.ANY), vmem, vmem, vmem),
        scratch_shapes=[
            pltpu.VMEM((32, 256), jnp.bfloat16),
            pltpu.VMEM((16, 2, 32, 256), jnp.bfloat16),
            pltpu.VMEM((SHARD, BLK), jnp.bfloat16),
            pltpu.SemaphoreType.DMA((32,)),
            pltpu.SemaphoreType.DMA((32,)),
            pltpu.SemaphoreType.DMA((32,)),
            pltpu.SemaphoreType.DMA((32,)),
            pltpu.SemaphoreType.DMA((5,)),
            pltpu.SemaphoreType.DMA((99,)),
            pltpu.SemaphoreType.DMA((99,)),
            pltpu.SemaphoreType.DMA((39,)),
            pltpu.SemaphoreType.DMA((39,)),
        ],
        compiler_params=pltpu.CompilerParams(
            collective_id=0, has_side_effects=True, vmem_limit_bytes=36 * MIB
        ),
        name="expand",
    )(keys, docs_t, expand_weight)


def label_kernel(
    tables, base, pos_ref, hid_ref, weight_ref, gs_ref, gp_ref,
    h, h_t, w, res, pos_b, gp, h_sem, w_sem, gp_sem,
):
    g = pl.program_id(0)

    def block_copy(p):
        b = lax.div(tables[0, p * NAMED], 512)
        return pltpu.make_async_copy(hid_ref.at[b], h.at[p], h_sem.at[p])

    def weight_copy(q):
        return pltpu.make_async_copy(weight_ref.at[q], w.at[q], w_sem.at[q])

    @pl.when(g == 0)
    def _():
        def begin(p, carry):
            block_copy(p).start()
            return carry

        lax.fori_loop(0, POOL, begin, 0)

        def begin_weight(q, carry):
            weight_copy(q).start()
            return carry

        lax.fori_loop(0, LBLK_DEV, begin_weight, 0)
        turned = pos_ref[...].T
        for k in range(POS):
            pos_b[k] = jnp.broadcast_to(turned[:, k : k + 1], (DOCS, BLK))

        def arrive(p, carry):
            block_copy(p).wait()
            h_t[p] = h[p].T
            return carry

        lax.fori_loop(0, POOL, arrive, 0, unroll=8)

    rows = [g * STEP + k for k in range(STEP)]
    spots = [[tables[1, q * SLOTS + s] for s in range(SLOTS)] for q in rows]
    for q in rows:
        weight_copy(q).wait()
    scores = []
    for q, where in zip(rows, spots):
        logits = jnp.zeros((DOCS, BLK), jnp.float32)
        for s in range(0, SLOTS, 2):
            left = jnp.concatenate([h[where[s]], h[where[s + 1]]], axis=1)
            right = w[q, s : s + 2].reshape(2 * BLK, BLK)
            logits += jnp.dot(left, right, preferred_element_type=jnp.float32)
        scores.append(logits)
    residuals = []
    for q, logits in zip(rows, scores):
        ids = (base[0] + q) * BLK + lax.broadcasted_iota(jnp.int32, (DOCS, BLK), 1)
        hit = pos_b[0] == ids
        for k in range(1, POS):
            hit = jnp.logical_or(hit, pos_b[k] == ids)
        residual = (jax.nn.sigmoid(logits) - jnp.where(hit, 1.0, 0.0)).astype(jnp.bfloat16)
        res[q] = residual
        residuals.append(residual)
    for k, (where, residual) in enumerate(zip(spots, residuals)):
        for s in range(SLOTS):
            gs_ref[k, s] = jnp.dot(
                h_t[where[s]], residual, preferred_element_type=jnp.float32
            ).astype(jnp.bfloat16)

    def gp_copy(f):
        return pltpu.make_async_copy(
            gp.at[pl.ds(f * 24, 24)], gp_ref.at[pl.ds(f * 24, 24)], gp_sem.at[f]
        )

    @pl.when(g == LBLK_DEV // STEP - 1)
    def _():
        for f in range(4):

            def collect(p, carry):
                slots = [lax.rem(tables[0, p * NAMED + k], 512) for k in range(NAMED)]
                pairs = [(lax.div(i, SLOTS), lax.rem(i, SLOTS)) for i in slots]
                left = jnp.concatenate([res[q] for q, _ in pairs], axis=1)
                right = jnp.concatenate([w[q, s] for q, s in pairs], axis=1)
                gp[p] = lax.dot_general(
                    left, right, (((1,), (1,)), ((), ())), preferred_element_type=jnp.float32
                ).astype(jnp.bfloat16)
                return carry

            lax.fori_loop(f * 24, f * 24 + 24, collect, 0, unroll=8)
            gp_copy(f).start()
        for f in range(4):
            gp_copy(f).wait()


def label_blocks(tables, base, positives, hid, sparse_weight):
    return pl.pallas_call(
        label_kernel,
        out_shape=(
            jax.ShapeDtypeStruct((LBLK_DEV, SLOTS, BLK, BLK), jnp.bfloat16),
            jax.ShapeDtypeStruct((POOL, DOCS, BLK), jnp.bfloat16),
        ),
        grid_spec=pltpu.PrefetchScalarGridSpec(
            num_scalar_prefetch=2,
            grid=(LBLK_DEV // STEP,),
            in_specs=[
                pl.BlockSpec((POS, DOCS), lambda g, *_: (0, 0)),
                pl.BlockSpec(memory_space=pl.ANY),
                pl.BlockSpec(memory_space=pl.ANY),
            ],
            out_specs=(
                pl.BlockSpec((STEP, SLOTS, BLK, BLK), lambda g, *_: (g, 0, 0, 0)),
                pl.BlockSpec(memory_space=pl.ANY),
            ),
            scratch_shapes=[
                pltpu.VMEM((POOL, DOCS, BLK), jnp.bfloat16),
                pltpu.VMEM((POOL, BLK, DOCS), jnp.bfloat16),
                pltpu.VMEM((LBLK_DEV, SLOTS, BLK, BLK), jnp.bfloat16),
                pltpu.VMEM((LBLK_DEV, DOCS, BLK), jnp.bfloat16),
                pltpu.VMEM((POS, DOCS, BLK), jnp.int32),
                pltpu.VMEM((POOL, DOCS, BLK), jnp.bfloat16),
                pltpu.SemaphoreType.DMA((POOL,)),
                pltpu.SemaphoreType.DMA((LBLK_DEV,)),
                pltpu.SemaphoreType.DMA((4,)),
            ],
        ),
        compiler_params=pltpu.CompilerParams(
            dimension_semantics=("arbitrary",), vmem_limit_bytes=36 * MIB
        ),
        name="label_blocks",
    )(tables, base, positives, hid, sparse_weight)


def reduce_kernel(
    tables, gp_ref, mask, docs_ref, out_ref,
    own, sib, acc, grad, mine_grad, pieces, *rest,
):
    across2, near2, across1, near1, near0 = (rest[k * 3 : k * 3 + 3] for k in range(5))
    pair_sem, send, recv, o_send, o_recv = rest[15:]
    y, z, x, c = (lax.axis_index(a) for a in AXES)
    here = (y, z, x)
    sibling = {"label_2": 1 - c}
    me = z * 8 + x * 2 + c
    barrier = pltpu.get_barrier_semaphore()

    def greet(o, carry):
        pl.semaphore_signal(
            barrier, inc=1, device_id=label_peer(lax.rem(me + o, 32)), device_id_type=MESH
        )
        return carry

    lax.fori_loop(1, 32, greet, 0)
    for k in (1, 2, 3):
        pl.semaphore_signal(barrier, inc=1, device_id={"feat": hop(y, k)}, device_id_type=MESH)

    def docs_half(k):
        return gp_ref.at[:, pl.ds(pl.multiple_of(k * HALF, 16), HALF), :]

    to_pair = pltpu.make_async_remote_copy(
        src_ref=docs_half(1 - c), dst_ref=sib.at[pl.ds(0, POOL)],
        send_sem=pair_sem.at[0], recv_sem=pair_sem.at[1],
        device_id=sibling, device_id_type=MESH,
    )
    mine = pltpu.make_async_copy(docs_half(c), own.at[pl.ds(0, POOL)], pair_sem.at[2])
    mine.start()
    own[POOL] = jnp.zeros((HALF, BLK), jnp.bfloat16)
    sib[POOL] = jnp.zeros((HALF, BLK), jnp.bfloat16)
    pl.semaphore_wait(barrier, 34)
    to_pair.start()
    mine.wait()
    to_pair.wait()

    parts = range(3)
    started = []

    def coords(p):
        return tuple(here[axis] for axis in PARTS[p][0])

    def spread(p, sub):
        order, row, rows = PARTS[p]
        line = hop(coords(p)[1], LINES[sub])

        def one(i, carry):
            at = cell(PARTS[p], lax.div(i, 4), line, lax.rem(i, 4))
            first_block = ((at[0] * 4 + at[1]) * 4 + at[2]) * 4
            for blk in range(row // HALF, (row + rows - 1) // HALF + 1):
                low, high = max(row, blk * HALF), min(row + rows, blk * HALF + HALF)
                span = pl.ds(low - blk * HALF, high - low)
                b = first_block + blk
                acc[(*at[:3], pl.ds(low, high - low), slice(None))] = (
                    own[tables[2, b], span, :] + sib[tables[3, b], span, :]
                )
            return carry

        lax.fori_loop(0, 16, one, 0)

    def push(source, target, slot, axis, k):
        return pltpu.make_async_remote_copy(
            src_ref=acc.at[source], dst_ref=target, send_sem=send.at[slot], recv_sem=recv.at[slot],
            device_id={AXES[axis]: hop(here[axis], k)}, device_id_type=MESH,
        )

    def go(op):
        op.start()
        started.append(op)

    def third(p, sub, way, k):
        line, t = hop(coords(p)[1], LINES[sub]), coords(p)[2]
        half = 1 - way if k == 1 else way
        source = cell(PARTS[p], two(half), line, hop(t, 2 if k == 0 else NEAR[way]))
        target = across2[p].at[sub, way] if k == 0 else near2[p].at[sub, way, two(half)]
        slot = 27 + ((p * 4 + sub) * 2 + way) * 3 + k
        return push(source, target, slot, PARTS[p][0][2], NEAR[way])

    def second(p, way, k):
        _, b, t = coords(p)
        half = 1 - way if k == 1 else way
        source = cell(PARTS[p], two(half), hop(b, 2 if k == 0 else NEAR[way]), t)
        target = across1[p].at[way] if k == 0 else near1[p].at[way, two(half)]
        return push(source, target, 9 + (p * 2 + way) * 3 + k, PARTS[p][0][1], NEAR[way])

    def first(p, way):
        a, b, t = coords(p)
        source = cell(PARTS[p], hop(a, NEAR[way]), b, t)
        return push(source, near0[p].at[way], p * 3 + way, PARTS[p][0][0], NEAR[way])

    def add(at, *terms):
        total = acc[at].astype(jnp.float32)
        for term in terms:
            total = total + term.astype(jnp.float32)
        acc[at] = total.astype(jnp.bfloat16)

    def send_line(p, sub):
        spread(p, sub)
        for k in range(2):
            for way in range(2):
                go(third(p, sub, way, k))

    def pass_line(p, sub):
        line, t = hop(coords(p)[1], LINES[sub]), coords(p)[2]
        for way in range(2):
            third(p, sub, way, 0).wait_recv()
            for i in range(2):
                add(
                    cell(PARTS[p], 2 * way + i, line, hop(t, NEAR[way])),
                    across2[p][sub, way, i],
                )
            go(third(p, sub, way, 2))

    def finish_line(p, sub):
        line, t = hop(coords(p)[1], LINES[sub]), coords(p)[2]
        for way in range(2):
            third(p, sub, way, 1).wait_recv()
            third(p, sub, way, 2).wait_recv()
        for i in range(4):
            add(cell(PARTS[p], i, line, t), near2[p][sub, 0, i], near2[p][sub, 1, i])

    for p in parts:
        send_line(p, 3)
    for p in parts:
        send_line(p, 1)
    for p in parts:
        pass_line(p, 3)
        send_line(p, 2)
    for p in parts:
        pass_line(p, 1)
        send_line(p, 0)
    for p in parts:
        finish_line(p, 3)
        for way in range(2):
            go(second(p, way, 0))
    for p in parts:
        pass_line(p, 2)
    for p in parts:
        pass_line(p, 0)
    for p in parts:
        finish_line(p, 1)
        finish_line(p, 2)
        for way in range(2):
            go(second(p, way, 1))
    for p in parts:
        _, b, t = coords(p)
        for way in range(2):
            second(p, way, 0).wait_recv()
            for i in range(2):
                add(cell(PARTS[p], 2 * way + i, hop(b, NEAR[way]), t), across1[p][way, i])
            go(second(p, way, 2))
    for p in parts:
        finish_line(p, 0)
    for p in parts:
        _, b, t = coords(p)
        for way in range(2):
            second(p, way, 1).wait_recv()
            second(p, way, 2).wait_recv()
        for i in range(4):
            add(cell(PARTS[p], i, b, t), near1[p][0, i], near1[p][1, i])
        for way in (2, 0, 1):
            go(first(p, way))
    for p in parts:
        for way in range(3):
            first(p, way).wait_recv()
        add(cell(PARTS[p], *coords(p)), *(near0[p][way] for way in range(3)))

    total = acc[y, z, x]
    grad[...] = jnp.where(mask[...] > 0, total, jnp.zeros_like(total))

    def columns(k):
        return grad.at[pl.ds(pl.multiple_of(k * DOCS, 16), DOCS), :]

    def pair_grad(k, core):
        return pltpu.make_async_remote_copy(
            src_ref=columns(k), dst_ref=mine_grad.at[core],
            send_sem=pair_sem.at[3], recv_sem=pair_sem.at[4],
            device_id=sibling, device_id_type=MESH,
        )

    to_other = pair_grad(1 - c, c)
    to_other.start()
    kept = pltpu.make_async_copy(columns(c), mine_grad.at[c], pair_sem.at[5])
    kept.start()
    kept.wait()
    pair_grad(c, 1 - c).wait_recv()
    sides = [
        jnp.concatenate([mine_grad[half, pl.ds(j * HALF, HALF), :] for half in range(2)], axis=0)
        for j in range(2)
    ]
    right = jnp.concatenate(sides, axis=1)

    def out_columns(l):
        return out_ref.at[:, pl.ds(pl.multiple_of(l * 256, 256), 256)]

    def out_copy(to, origin):
        return pltpu.make_async_remote_copy(
            src_ref=pieces.at[to], dst_ref=out_columns(origin),
            send_sem=o_send.at[to], recv_sem=o_recv.at[origin],
            device_id=label_peer(to), device_id_type=MESH,
        )

    own_out = pltpu.make_async_copy(pieces.at[me], out_columns(me), pair_sem.at[6])
    for k in range(4):
        row = hop(z, k) * 8
        left = docs_ref[pl.ds(hop(z, k) * 4, 4)].reshape(256, 256)[:, :DOCS]
        pieces[pl.ds(row, 8)] = jnp.dot(
            left, right, preferred_element_type=jnp.float32
        ).astype(jnp.bfloat16).reshape(8, 32, 256)

        def deliver(o, carry):
            out_copy(row + lax.rem(x * 2 + c + o, 8), me).start()
            return carry

        lax.fori_loop(1 if k == 0 else 0, 8, deliver, 0)
        if k == 0:
            own_out.start()
    own_out.wait()

    def collect(o, carry):
        other = lax.rem(me + o, 32)
        out_copy(other, other).wait_recv()
        return carry

    def drain(o, carry):
        out_copy(lax.rem(me + o, 32), me).wait_send()
        return carry

    lax.fori_loop(1, 32, collect, 0)
    to_other.wait_send()
    for op in started:
        op.wait_send()
    lax.fori_loop(1, 32, drain, 0)


def reduce_blocks(tables, gp, mask, docs_all):
    received = [
        pltpu.VMEM((*lead, rows, BLK), jnp.bfloat16)
        for lead in ((4, 2, 2), (4, 2, 4), (2, 2), (2, 4), (3,))
        for _, _, rows in PARTS
    ]
    return pl.pallas_call(
        reduce_kernel,
        out_shape=jax.ShapeDtypeStruct((32, 8192), jnp.bfloat16),
        in_specs=[
            pl.BlockSpec(memory_space=pltpu.SMEM),
            pl.BlockSpec(memory_space=pl.ANY),
            pl.BlockSpec(memory_space=pltpu.VMEM),
            pl.BlockSpec(memory_space=pltpu.VMEM),
        ],
        out_specs=pl.BlockSpec(memory_space=pltpu.VMEM),
        scratch_shapes=[
            pltpu.VMEM((POOL + 1, HALF, BLK), jnp.bfloat16),
            pltpu.VMEM((POOL + 1, HALF, BLK), jnp.bfloat16),
            pltpu.VMEM((4, 4, 4, SHARD, BLK), jnp.bfloat16),
            pltpu.VMEM((SHARD, BLK), jnp.bfloat16),
            pltpu.VMEM((2, DOCS, BLK), jnp.bfloat16),
            pltpu.VMEM((32, 32, 256), jnp.bfloat16),
            *received,
            pltpu.SemaphoreType.DMA((7,)),
            pltpu.SemaphoreType.DMA((99,)),
            pltpu.SemaphoreType.DMA((99,)),
            pltpu.SemaphoreType.DMA((32,)),
            pltpu.SemaphoreType.DMA((32,)),
        ],
        compiler_params=pltpu.CompilerParams(
            collective_id=1, has_side_effects=True, vmem_limit_bytes=24 * MIB
        ),
        name="reduce_blocks",
    )(tables, gp, mask, docs_all)


def on_device(documents, expand_weight, sparse_weight, feature_lists, positives):
    core = lax.axis_index("label_2")
    group = lax.axis_index(AXES)
    pair = lax.dynamic_slice_in_dim(feature_lists, (group - core) * LBLK_DEV, 2 * LBLK_DEV, 0)
    pair = pair.reshape(2, LBLK_DEV * SLOTS)
    keys = jnp.where(core == 0, pair, pair[::-1]) * 512
    keys = jnp.pad(keys + jnp.arange(LBLK_DEV * SLOTS, dtype=jnp.int32)[None, :], ((0, 6), (0, 0)))
    hid, docs_all, mask, tables = expand(keys, documents.T, expand_weight)
    grad_sparse, gp = label_blocks(
        tables,
        (group * LBLK_DEV).astype(jnp.int32).reshape(1),
        positives.T,
        hid.reshape(FBLOCKS, DOCS, BLK),
        sparse_weight,
    )
    grad_expand = reduce_blocks(tables, gp, mask, docs_all)
    return (grad_expand, grad_sparse)


def solution(mesh):
    finer = Mesh(mesh.devices.reshape(mesh.shape["feat"], 4, 4, 2), AXES)
    return jax.shard_map(
        on_device,
        mesh=finer,
        in_specs=(P(None, LABEL), P(LABEL, "feat"), P(AXES, None, None, None), P(), P()),
        out_specs=(P(LABEL, "feat"), P(AXES, None, None, None)),
        check_vma=False,
    )
```

```python
import functools

import jax
import jax.numpy as jnp
from jax import lax
from jax.experimental import pallas as pl
from jax.experimental.pallas import tpu as pltpu
from jax.sharding import Mesh
from jax.sharding import PartitionSpec as P

BLK = 128
FBLOCKS = 256
SLOTS = 16
LBLK_DEV = 24
POOL = 96
STEP = 4
STEPS = 6
SPAN = 16
NAMED = 4
POS = 8
DOCS = 160
HALF = 80
SHARD = 320
RING = 4
AXES = ("feat", "label_0", "label_1", "label_2")
LABEL = AXES[1:]
MESH = pl.DeviceIdType.MESH
MIB = 1 << 20

PARTS = (((2, 0, 1), 0, 112), ((0, 1, 2), 112, 112), ((1, 2, 0), 224, 96))
NEAR, BACK = (1, 3, 2), (3, 1, 2)
LINES = (0, 3, 1, 2)


def hop(m, k):
    return lax.rem(m + k, RING)


def label_peer(l):
    return {
        "label_0": lax.div(l, 8),
        "label_1": lax.rem(lax.div(l, 2), 4),
        "label_2": lax.rem(l, 2),
    }


def cell(part, ta, tb, tc, lead=()):
    order, row, rows = part
    index = [None] * 3
    for axis, t in zip(order, (ta, tb, tc)):
        index[axis] = t
    return (*index, *lead, pl.ds(row, rows), slice(None))


def two(half):
    return pl.ds(2 * half, 2)


def rank_tables(keys, tables_ref):
    count = LBLK_DEV * SLOTS
    turned = keys.T
    tables_ref[...] = jnp.zeros((8, count), jnp.int32)
    lanes = lax.broadcasted_iota(jnp.int32, (count, count), 1)
    for r in range(2):
        row, col = keys[r : r + 1, :], turned[:, r : r + 1]
        below = jnp.sum(jnp.where(row < col, 1.0, 0.0), axis=1, keepdims=True).astype(jnp.int32)
        if r == 0:
            sort = jnp.where(below == lanes, col.astype(jnp.float32), 0.0)
            tables_ref[0:1, :] = jnp.sum(sort, axis=0, keepdims=True).astype(jnp.int32)
            above = jnp.sum(jnp.where(col < row, 1.0, 0.0), axis=0, keepdims=True)
            tables_ref[1:2, :] = lax.shift_right_logical(above.astype(jnp.int32), 2)
            tables_ref[4:5, :] = lax.shift_right_logical(row, 9)
        place = lax.shift_right_logical(below, 2)
        first = jnp.where(place * NAMED == below, place - POOL, 0).astype(jnp.float32)
        hit = lax.shift_right_logical(col, 9) == lanes[:, :FBLOCKS]
        table = jnp.sum(jnp.where(hit, first, 0.0), axis=0, keepdims=True)
        tables_ref[2 + r : 3 + r, 0:FBLOCKS] = table.astype(jnp.int32) + POOL


def expand_kernel(
    keys_ref, docs_in, weight_ref, hid_ref, docs_all, mask_ref, tables_ref, docs_ref, w_all, shard,
    w_send, w_recv, d_send, d_recv, own_sem, send, recv, sib_send, sib_recv,
):
    y, z, x, c = (lax.axis_index(a) for a in AXES)
    here = (y, z, x)
    me = z * 8 + x * 2 + c
    sibling = {"label_2": 1 - c}
    peer = label_peer
    docs_ref[:, 0:DOCS] = docs_in[...]
    docs_ref[:, DOCS:] = jnp.zeros((32, 256 - DOCS), jnp.bfloat16)
    barrier = pltpu.get_barrier_semaphore()

    def greet(o, carry):
        pl.semaphore_signal(
            barrier, inc=1, device_id=peer(lax.rem(me + o, 32)), device_id_type=MESH
        )
        return carry

    lax.fori_loop(1, 32, greet, 0)
    for k in (1, 2, 3):
        pl.semaphore_signal(barrier, inc=1, device_id={"feat": hop(y, k)}, device_id_type=MESH)
    pl.semaphore_wait(barrier, 34)

    def rows_of(ref, l):
        return ref.at[lax.div(l, 2), lax.rem(l, 2)]

    def columns_for(l):
        return weight_ref.at[:, pl.ds(pl.multiple_of(l * 256, 256), 256)]

    def docs_copy(to, origin):
        return pltpu.make_async_remote_copy(
            src_ref=docs_ref, dst_ref=rows_of(docs_all, origin),
            send_sem=d_send.at[to], recv_sem=d_recv.at[origin],
            device_id=peer(to), device_id_type=MESH,
        )

    def docs_pair(core):
        return pltpu.make_async_remote_copy(
            src_ref=docs_all.at[:, core], dst_ref=docs_all.at[:, core],
            send_sem=own_sem.at[3], recv_sem=own_sem.at[4],
            device_id=sibling, device_id_type=MESH,
        )

    def weight_copy(to, origin):
        return pltpu.make_async_remote_copy(
            src_ref=columns_for(to), dst_ref=rows_of(w_all, origin),
            send_sem=w_send.at[to], recv_sem=w_recv.at[origin],
            device_id=peer(to), device_id_type=MESH,
        )

    def same_core(o):
        return lax.rem(me + 2 * o, 32)

    def start_docs(o, carry):
        docs_copy(same_core(o), me).start()
        return carry

    def start_weight(o, carry):
        weight_copy(lax.rem(me + o, 32), me).start()
        return carry

    lax.fori_loop(1, 16, start_docs, 0)
    lax.fori_loop(1, 32, start_weight, 0)
    own_docs = pltpu.make_async_copy(docs_ref, rows_of(docs_all, me), own_sem.at[0])
    own_weight = pltpu.make_async_copy(columns_for(me), rows_of(w_all, me), own_sem.at[1])
    own_docs.start()
    own_weight.start()
    rank_tables(keys_ref[...], tables_ref)
    own_docs.wait()
    own_weight.wait()

    def finish_docs(o, carry):
        docs_copy(same_core(o), same_core(o)).wait_recv()
        return carry

    def finish_weight(o, carry):
        other = lax.rem(me + o, 32)
        weight_copy(other, other).wait_recv()
        return carry

    lax.fori_loop(1, 16, finish_docs, 0)
    docs_pair(c).start()
    lax.fori_loop(1, 32, finish_weight, 0)
    docs_pair(1 - c).wait_recv()
    product = lax.dot_general(
        docs_all[...].reshape(1024, 256), w_all[...].reshape(1024, 256),
        (((0,), (0,)), ((), ())), preferred_element_type=jnp.float32,
    )
    hidden = jnp.maximum(product, 0.0).astype(jnp.bfloat16)
    shard[0:DOCS, :] = hidden[:DOCS, :BLK]
    shard[DOCS:SHARD, :] = hidden[:DOCS, BLK:]
    own_hidden = pltpu.make_async_copy(shard, hid_ref.at[y, z, x, c], own_sem.at[2])
    own_hidden.start()

    started = []

    def copy(at, slot, axis, k, source=None):
        return pltpu.make_async_remote_copy(
            src_ref=hid_ref.at[at] if source is None else source,
            dst_ref=hid_ref.at[at],
            send_sem=send.at[slot],
            recv_sem=recv.at[slot],
            device_id={AXES[axis]: hop(here[axis], k)},
            device_id_type=MESH,
        )

    def go(op):
        op.start()
        started.append(op)

    def coords(p):
        return tuple(here[axis] for axis in PARTS[p][0])

    def first(p, way, origin, source=None):
        a, b, t = coords(p)
        return copy(
            cell(PARTS[p], origin, b, t, (c,)), p * 3 + way, PARTS[p][0][0], NEAR[way], source
        )

    def second(p, way, k, line, half):
        t = coords(p)[2]
        at = cell(PARTS[p], two(half), line, t, (c,))
        return copy(at, 9 + (p * 2 + way) * 3 + k, PARTS[p][0][1], NEAR[way])

    def third(p, sub, way, k, t, half):
        line = hop(coords(p)[1], LINES[sub])
        at = cell(PARTS[p], two(half), line, t, (c,))
        return copy(at, 27 + ((p * 4 + sub) * 2 + way) * 3 + k, PARTS[p][0][2], NEAR[way])

    def pair_copy(p, k, at):
        return pltpu.make_async_remote_copy(
            src_ref=hid_ref.at[at], dst_ref=hid_ref.at[at],
            send_sem=sib_send.at[p * 13 + k], recv_sem=sib_recv.at[p * 13 + k],
            device_id=sibling, device_id_type=MESH,
        )

    def pair_plane(p, core):
        return pair_copy(p, 0, cell(PARTS[p], slice(None), slice(None), coords(p)[2], (core,)))

    def pair_line(p, sub, way, core):
        _, b, t = coords(p)
        at = cell(PARTS[p], slice(None), hop(b, LINES[sub]), hop(t, BACK[way]), (core,))
        return pair_copy(p, 1 + sub * 3 + way, at)

    def send_line(p, sub):
        for k in range(2):
            for way in range(2):
                go(third(p, sub, way, k, coords(p)[2], way if k == 0 else 1 - way))

    def pass_line(p, sub):
        for way in range(2):
            near = hop(coords(p)[2], BACK[way])
            third(p, sub, way, 0, near, way).wait_recv()
            go(third(p, sub, way, 2, near, way))

    def finish_line(p, sub):
        for way in range(2):
            third(p, sub, way, 1, hop(coords(p)[2], BACK[way]), 1 - way).wait_recv()
            go(pair_line(p, sub, way, c))
        for way in range(2):
            third(p, sub, way, 2, hop(coords(p)[2], 2), way).wait_recv()
        go(pair_line(p, sub, 2, c))

    parts = range(3)
    for way in (2, 0, 1):
        for p in parts:
            _, row, rows = PARTS[p]
            go(first(p, way, coords(p)[0], shard.at[pl.ds(row, rows), :]))
    own_hidden.wait()
    for p in parts:
        a, b, t = coords(p)
        for way in range(3):
            first(p, way, hop(a, BACK[way])).wait_recv()
        for k in range(2):
            for way in range(2):
                go(second(p, way, k, b, way if k == 0 else 1 - way))
        send_line(p, 0)
    for p in parts:
        b = coords(p)[1]
        for way in range(2):
            near = hop(b, BACK[way])
            second(p, way, 0, near, way).wait_recv()
            go(second(p, way, 2, near, way))
    for p in parts:
        pass_line(p, 0)
    for p in parts:
        b = coords(p)[1]
        for way in range(2):
            second(p, way, 1, hop(b, BACK[way]), 1 - way).wait_recv()
            send_line(p, 1 + way)
    for p in parts:
        for way in range(2):
            second(p, way, 2, hop(coords(p)[1], 2), way).wait_recv()
        send_line(p, 3)
        go(pair_plane(p, c))
    for sub in (1, 2):
        for p in parts:
            pass_line(p, sub)
    for p in parts:
        finish_line(p, 0)
    for p in parts:
        pass_line(p, 3)
    for sub in (1, 2, 3):
        for p in parts:
            finish_line(p, sub)
    for p in parts:
        pair_plane(p, 1 - c).wait_recv()
        for sub in range(4):
            for way in range(3):
                pair_line(p, sub, way, 1 - c).wait_recv()
    for op in started:
        op.wait_send()
    docs_pair(c).wait_send()
    for blk in range(4):
        op = pltpu.make_async_copy(
            hid_ref.at[
                y, z, x, blk // 2,
                pl.ds(pl.multiple_of(blk % 2 * DOCS + c * HALF, 16), HALF), slice(None),
            ],
            mask_ref.at[pl.ds(blk * HALF, HALF), :],
            own_sem.at[blk],
        )
        op.start()
    for blk in range(4):
        pltpu.make_async_copy(
            mask_ref.at[pl.ds(blk * HALF, HALF), :], mask_ref.at[pl.ds(blk * HALF, HALF), :], own_sem.at[blk]
        ).wait()

    def drain_docs(o, carry):
        docs_copy(same_core(o), me).wait_send()
        return carry

    def drain_weight(o, carry):
        weight_copy(lax.rem(me + o, 32), me).wait_send()
        return carry

    lax.fori_loop(1, 16, drain_docs, 0)
    lax.fori_loop(1, 32, drain_weight, 0)


def expand(keys, docs_t, expand_weight):
    vmem = pl.BlockSpec(memory_space=pltpu.VMEM)
    return pl.pallas_call(
        expand_kernel,
        out_shape=(
            jax.ShapeDtypeStruct((4, 4, 4, 2, SHARD, BLK), jnp.bfloat16),
            jax.ShapeDtypeStruct((16, 2, 32, 256), jnp.bfloat16),
            jax.ShapeDtypeStruct((SHARD, BLK), jnp.bfloat16),
            jax.ShapeDtypeStruct((8, LBLK_DEV * SLOTS), jnp.int32),
        ),
        in_specs=[vmem, vmem, pl.BlockSpec(memory_space=pltpu.HBM)],
        out_specs=(pl.BlockSpec(memory_space=pl.ANY), vmem, vmem, vmem),
        scratch_shapes=[
            pltpu.VMEM((32, 256), jnp.bfloat16),
            pltpu.VMEM((16, 2, 32, 256), jnp.bfloat16),
            pltpu.VMEM((SHARD, BLK), jnp.bfloat16),
            pltpu.SemaphoreType.DMA((32,)),
            pltpu.SemaphoreType.DMA((32,)),
            pltpu.SemaphoreType.DMA((32,)),
            pltpu.SemaphoreType.DMA((32,)),
            pltpu.SemaphoreType.DMA((5,)),
            pltpu.SemaphoreType.DMA((99,)),
            pltpu.SemaphoreType.DMA((99,)),
            pltpu.SemaphoreType.DMA((39,)),
            pltpu.SemaphoreType.DMA((39,)),
        ],
        compiler_params=pltpu.CompilerParams(
            collective_id=0, has_side_effects=True, vmem_limit_bytes=36 * MIB
        ),
        name="expand",
    )(keys, docs_t, expand_weight)


def label_kernel(
    tables, base, pos_ref, hid, weight_ref, gs_ref, gp_ref, h_t, w, res, pos_b, gp, w_sem, gp_sem,
):
    step = pl.program_id(0)

    def weight_copy(k):
        part = pl.ds(k * STEP, STEP)
        return pltpu.make_async_copy(weight_ref.at[part], w.at[part], w_sem.at[k])

    def gp_copy(k):
        part = pl.ds(k * SPAN, SPAN)
        return pltpu.make_async_copy(gp.at[part], gp_ref.at[part], gp_sem.at[k])

    @pl.when(step == 0)
    def _():
        for k in range(STEPS):
            weight_copy(k).start()
        turned = pos_ref[...].T
        for k in range(POS):
            pos_b[k] = jnp.broadcast_to(turned[:, k : k + 1], (DOCS, BLK))

    def listed(place):
        return hid[lax.div(tables[0, place * NAMED], 512)]

    @pl.when(step < STEPS)
    def _():
        weight_copy(step).wait()
        for k in range(STEP):
            q = step * STEP + k
            logits = jnp.zeros((DOCS, BLK), jnp.float32)
            for s in range(0, SLOTS, 2):
                left = jnp.concatenate(
                    [hid[tables[4, q * SLOTS + s + i]] for i in range(2)], axis=1
                )
                right = w[q, s : s + 2].reshape(2 * BLK, BLK)
                logits += jnp.dot(left, right, preferred_element_type=jnp.float32)
            ids = (base[0] + q) * BLK + lax.broadcasted_iota(jnp.int32, (DOCS, BLK), 1)
            hit = pos_b[0] == ids
            for i in range(1, POS):
                hit = jnp.logical_or(hit, pos_b[i] == ids)
            res[q] = (jax.nn.sigmoid(logits) - jnp.where(hit, 1.0, 0.0)).astype(jnp.bfloat16)
        for k in range(SPAN):
            place = step * SPAN + k
            h_t[place] = listed(place).T

    @pl.when(step >= STEPS)
    def _():
        late = step - STEPS
        for k in range(STEP):
            q = late * STEP + k
            residual = res[q]
            for s in range(SLOTS):
                gs_ref[k, s] = jnp.dot(
                    h_t[tables[1, q * SLOTS + s]], residual, preferred_element_type=jnp.float32
                ).astype(jnp.bfloat16)
        for k in range(SPAN):
            place = late * SPAN + k
            slots = [lax.rem(tables[0, place * NAMED + i], 512) for i in range(NAMED)]
            pairs = [(lax.div(i, SLOTS), lax.rem(i, SLOTS)) for i in slots]
            left = jnp.concatenate([res[q] for q, _ in pairs], axis=1)
            right = jnp.concatenate([w[q, s] for q, s in pairs], axis=1)
            gp[place] = lax.dot_general(
                left, right, (((1,), (1,)), ((), ())), preferred_element_type=jnp.float32
            ).astype(jnp.bfloat16)
        gp_copy(late).start()

    @pl.when(step == 2 * STEPS - 1)
    def _():
        for k in range(STEPS):
            gp_copy(k).wait()


def label_blocks(tables, base, positives, hid, sparse_weight):
    return pl.pallas_call(
        label_kernel,
        out_shape=(
            jax.ShapeDtypeStruct((LBLK_DEV, SLOTS, BLK, BLK), jnp.bfloat16),
            jax.ShapeDtypeStruct((POOL, DOCS, BLK), jnp.bfloat16),
        ),
        grid_spec=pltpu.PrefetchScalarGridSpec(
            num_scalar_prefetch=2,
            grid=(2 * STEPS,),
            in_specs=[
                pl.BlockSpec((POS, DOCS), lambda g, *_: (0, 0)),
                pl.BlockSpec(memory_space=pltpu.VMEM),
                pl.BlockSpec(memory_space=pl.ANY),
            ],
            out_specs=(
                pl.BlockSpec(
                    (STEP, SLOTS, BLK, BLK), lambda g, *_: (jnp.maximum(g - STEPS, 0), 0, 0, 0)
                ),
                pl.BlockSpec(memory_space=pl.ANY),
            ),
            scratch_shapes=[
                pltpu.VMEM((POOL, BLK, DOCS), jnp.bfloat16),
                pltpu.VMEM((LBLK_DEV, SLOTS, BLK, BLK), jnp.bfloat16),
                pltpu.VMEM((LBLK_DEV, DOCS, BLK), jnp.bfloat16),
                pltpu.VMEM((POS, DOCS, BLK), jnp.int32),
                pltpu.VMEM((POOL, DOCS, BLK), jnp.bfloat16),
                pltpu.SemaphoreType.DMA((STEPS,)),
                pltpu.SemaphoreType.DMA((STEPS,)),
            ],
        ),
        compiler_params=pltpu.CompilerParams(
            dimension_semantics=("arbitrary",), vmem_limit_bytes=36 * MIB
        ),
        name="label_blocks",
    )(tables, base, positives, hid, sparse_weight)


def reduce_kernel(
    tables, gp_ref, mask, docs_ref, out_ref,
    own, sib, acc, grad, mine_grad, pieces, *rest,
):
    across2, near2, across1, near1, near0 = (rest[k * 3 : k * 3 + 3] for k in range(5))
    pair_sem, send, recv, o_send, o_recv = rest[15:]
    y, z, x, c = (lax.axis_index(a) for a in AXES)
    here = (y, z, x)
    sibling = {"label_2": 1 - c}
    me = z * 8 + x * 2 + c
    barrier = pltpu.get_barrier_semaphore()

    def greet(o, carry):
        pl.semaphore_signal(
            barrier, inc=1, device_id=label_peer(lax.rem(me + o, 32)), device_id_type=MESH
        )
        return carry

    lax.fori_loop(1, 32, greet, 0)
    for k in (1, 2, 3):
        pl.semaphore_signal(barrier, inc=1, device_id={"feat": hop(y, k)}, device_id_type=MESH)

    def docs_half(k):
        return gp_ref.at[:, pl.ds(pl.multiple_of(k * HALF, 16), HALF), :]

    to_pair = pltpu.make_async_remote_copy(
        src_ref=docs_half(1 - c), dst_ref=sib.at[pl.ds(0, POOL)],
        send_sem=pair_sem.at[0], recv_sem=pair_sem.at[1],
        device_id=sibling, device_id_type=MESH,
    )
    mine = pltpu.make_async_copy(docs_half(c), own.at[pl.ds(0, POOL)], pair_sem.at[2])
    mine.start()
    own[POOL] = jnp.zeros((HALF, BLK), jnp.bfloat16)
    sib[POOL] = jnp.zeros((HALF, BLK), jnp.bfloat16)
    pl.semaphore_wait(barrier, 34)
    to_pair.start()
    mine.wait()
    to_pair.wait()

    parts = range(3)
    started = []

    def coords(p):
        return tuple(here[axis] for axis in PARTS[p][0])

    def spread(p, sub):
        order, row, rows = PARTS[p]
        line = hop(coords(p)[1], LINES[sub])

        def one(i, carry):
            at = cell(PARTS[p], lax.div(i, 4), line, lax.rem(i, 4))
            first_block = ((at[0] * 4 + at[1]) * 4 + at[2]) * 4
            for blk in range(row // HALF, (row + rows - 1) // HALF + 1):
                low, high = max(row, blk * HALF), min(row + rows, blk * HALF + HALF)
                span = pl.ds(low - blk * HALF, high - low)
                b = first_block + blk
                acc[(*at[:3], pl.ds(low, high - low), slice(None))] = (
                    own[tables[2, b], span, :] + sib[tables[3, b], span, :]
                )
            return carry

        lax.fori_loop(0, 16, one, 0)

    def push(source, target, slot, axis, k):
        return pltpu.make_async_remote_copy(
            src_ref=acc.at[source], dst_ref=target, send_sem=send.at[slot], recv_sem=recv.at[slot],
            device_id={AXES[axis]: hop(here[axis], k)}, device_id_type=MESH,
        )

    def go(op):
        op.start()
        started.append(op)

    def third(p, sub, way, k):
        line, t = hop(coords(p)[1], LINES[sub]), coords(p)[2]
        half = 1 - way if k == 1 else way
        source = cell(PARTS[p], two(half), line, hop(t, 2 if k == 0 else NEAR[way]))
        target = across2[p].at[sub, way] if k == 0 else near2[p].at[sub, way, two(half)]
        slot = 27 + ((p * 4 + sub) * 2 + way) * 3 + k
        return push(source, target, slot, PARTS[p][0][2], NEAR[way])

    def second(p, way, k):
        _, b, t = coords(p)
        half = 1 - way if k == 1 else way
        source = cell(PARTS[p], two(half), hop(b, 2 if k == 0 else NEAR[way]), t)
        target = across1[p].at[way] if k == 0 else near1[p].at[way, two(half)]
        return push(source, target, 9 + (p * 2 + way) * 3 + k, PARTS[p][0][1], NEAR[way])

    def first(p, way):
        a, b, t = coords(p)
        source = cell(PARTS[p], hop(a, NEAR[way]), b, t)
        return push(source, near0[p].at[way], p * 3 + way, PARTS[p][0][0], NEAR[way])

    def add(at, *terms):
        total = acc[at].astype(jnp.float32)
        for term in terms:
            total = total + term.astype(jnp.float32)
        acc[at] = total.astype(jnp.bfloat16)

    def send_line(p, sub):
        spread(p, sub)
        for k in range(2):
            for way in range(2):
                go(third(p, sub, way, k))

    def pass_line(p, sub):
        line, t = hop(coords(p)[1], LINES[sub]), coords(p)[2]
        for way in range(2):
            third(p, sub, way, 0).wait_recv()
            for i in range(2):
                add(
                    cell(PARTS[p], 2 * way + i, line, hop(t, NEAR[way])),
                    across2[p][sub, way, i],
                )
            go(third(p, sub, way, 2))

    def finish_line(p, sub):
        line, t = hop(coords(p)[1], LINES[sub]), coords(p)[2]
        for way in range(2):
            third(p, sub, way, 1).wait_recv()
            third(p, sub, way, 2).wait_recv()
        for i in range(4):
            add(cell(PARTS[p], i, line, t), near2[p][sub, 0, i], near2[p][sub, 1, i])

    for p in parts:
        send_line(p, 3)
    for p in parts:
        send_line(p, 1)
    for p in parts:
        pass_line(p, 3)
        send_line(p, 2)
    for p in parts:
        pass_line(p, 1)
        send_line(p, 0)
    for p in parts:
        finish_line(p, 3)
        for way in range(2):
            go(second(p, way, 0))
    for p in parts:
        pass_line(p, 2)
    for p in parts:
        pass_line(p, 0)
    for p in parts:
        finish_line(p, 1)
        finish_line(p, 2)
        for way in range(2):
            go(second(p, way, 1))
    for p in parts:
        _, b, t = coords(p)
        for way in range(2):
            second(p, way, 0).wait_recv()
            for i in range(2):
                add(cell(PARTS[p], 2 * way + i, hop(b, NEAR[way]), t), across1[p][way, i])
            go(second(p, way, 2))
    for p in parts:
        finish_line(p, 0)
    for p in parts:
        _, b, t = coords(p)
        for way in range(2):
            second(p, way, 1).wait_recv()
            second(p, way, 2).wait_recv()
        for i in range(4):
            add(cell(PARTS[p], i, b, t), near1[p][0, i], near1[p][1, i])
        for way in (2, 0, 1):
            go(first(p, way))
    for p in parts:
        for way in range(3):
            first(p, way).wait_recv()
        add(cell(PARTS[p], *coords(p)), *(near0[p][way] for way in range(3)))

    total = acc[y, z, x]
    grad[...] = jnp.where(mask[...] > 0, total, jnp.zeros_like(total))

    def columns(k):
        return grad.at[pl.ds(pl.multiple_of(k * DOCS, 16), DOCS), :]

    def pair_grad(k, core):
        return pltpu.make_async_remote_copy(
            src_ref=columns(k), dst_ref=mine_grad.at[core],
            send_sem=pair_sem.at[3], recv_sem=pair_sem.at[4],
            device_id=sibling, device_id_type=MESH,
        )

    to_other = pair_grad(1 - c, c)
    to_other.start()
    kept = pltpu.make_async_copy(columns(c), mine_grad.at[c], pair_sem.at[5])
    kept.start()
    kept.wait()
    pair_grad(c, 1 - c).wait_recv()
    sides = [
        jnp.concatenate([mine_grad[half, pl.ds(j * HALF, HALF), :] for half in range(2)], axis=0)
        for j in range(2)
    ]
    right = jnp.concatenate(sides, axis=1)

    def out_columns(l):
        return out_ref.at[:, pl.ds(pl.multiple_of(l * 256, 256), 256)]

    def out_copy(to, origin):
        return pltpu.make_async_remote_copy(
            src_ref=pieces.at[to], dst_ref=out_columns(origin),
            send_sem=o_send.at[to], recv_sem=o_recv.at[origin],
            device_id=label_peer(to), device_id_type=MESH,
        )

    own_out = pltpu.make_async_copy(pieces.at[me], out_columns(me), pair_sem.at[6])
    for k in range(4):
        row = hop(z, k) * 8
        left = docs_ref[pl.ds(hop(z, k) * 4, 4)].reshape(256, 256)[:, :DOCS]
        pieces[pl.ds(row, 8)] = jnp.dot(
            left, right, preferred_element_type=jnp.float32
        ).astype(jnp.bfloat16).reshape(8, 32, 256)

        def deliver(o, carry):
            out_copy(row + lax.rem(x * 2 + c + o, 8), me).start()
            return carry

        lax.fori_loop(1 if k == 0 else 0, 8, deliver, 0)
        if k == 0:
            own_out.start()
    own_out.wait()

    def collect(o, carry):
        other = lax.rem(me + o, 32)
        out_copy(other, other).wait_recv()
        return carry

    def drain(o, carry):
        out_copy(lax.rem(me + o, 32), me).wait_send()
        return carry

    lax.fori_loop(1, 32, collect, 0)
    to_other.wait_send()
    for op in started:
        op.wait_send()
    lax.fori_loop(1, 32, drain, 0)


def reduce_blocks(tables, gp, mask, docs_all):
    received = [
        pltpu.VMEM((*lead, rows, BLK), jnp.bfloat16)
        for lead in ((4, 2, 2), (4, 2, 4), (2, 2), (2, 4), (3,))
        for _, _, rows in PARTS
    ]
    return pl.pallas_call(
        reduce_kernel,
        out_shape=jax.ShapeDtypeStruct((32, 8192), jnp.bfloat16),
        in_specs=[
            pl.BlockSpec(memory_space=pltpu.SMEM),
            pl.BlockSpec(memory_space=pl.ANY),
            pl.BlockSpec(memory_space=pltpu.VMEM),
            pl.BlockSpec(memory_space=pltpu.VMEM),
        ],
        out_specs=pl.BlockSpec(memory_space=pltpu.VMEM),
        scratch_shapes=[
            pltpu.VMEM((POOL + 1, HALF, BLK), jnp.bfloat16),
            pltpu.VMEM((POOL + 1, HALF, BLK), jnp.bfloat16),
            pltpu.VMEM((4, 4, 4, SHARD, BLK), jnp.bfloat16),
            pltpu.VMEM((SHARD, BLK), jnp.bfloat16),
            pltpu.VMEM((2, DOCS, BLK), jnp.bfloat16),
            pltpu.VMEM((32, 32, 256), jnp.bfloat16),
            *received,
            pltpu.SemaphoreType.DMA((7,)),
            pltpu.SemaphoreType.DMA((99,)),
            pltpu.SemaphoreType.DMA((99,)),
            pltpu.SemaphoreType.DMA((32,)),
            pltpu.SemaphoreType.DMA((32,)),
        ],
        compiler_params=pltpu.CompilerParams(
            collective_id=1, has_side_effects=True, vmem_limit_bytes=24 * MIB
        ),
        name="reduce_blocks",
    )(tables, gp, mask, docs_all)


def on_device(documents, expand_weight, sparse_weight, feature_lists, positives):
    core = lax.axis_index("label_2")
    group = lax.axis_index(AXES)
    pair = lax.dynamic_slice_in_dim(feature_lists, (group - core) * LBLK_DEV, 2 * LBLK_DEV, 0)
    pair = pair.reshape(2, LBLK_DEV * SLOTS)
    keys = jnp.where(core == 0, pair, pair[::-1]) * 512
    keys = jnp.pad(keys + jnp.arange(LBLK_DEV * SLOTS, dtype=jnp.int32)[None, :], ((0, 6), (0, 0)))
    hid, docs_all, mask, tables = expand(keys, documents.T, expand_weight)
    grad_sparse, gp = label_blocks(
        tables,
        (group * LBLK_DEV).astype(jnp.int32).reshape(1),
        positives.T,
        hid.reshape(FBLOCKS, DOCS, BLK),
        sparse_weight,
    )
    grad_expand = reduce_blocks(tables, gp, mask, docs_all)
    return (grad_expand, grad_sparse)


def solution(mesh):
    finer = Mesh(mesh.devices.reshape(mesh.shape["feat"], 4, 4, 2), AXES)
    return jax.shard_map(
        on_device,
        mesh=finer,
        in_specs=(P(None, LABEL), P(LABEL, "feat"), P(AXES, None, None, None), P(), P()),
        out_specs=(P(LABEL, "feat"), P(AXES, None, None, None)),
        check_vma=False,
    )
```

```python
import functools

import jax
import jax.numpy as jnp
from jax import lax
from jax.experimental import pallas as pl
from jax.experimental.pallas import tpu as pltpu
from jax.sharding import Mesh
from jax.sharding import PartitionSpec as P

BLK = 128
FBLOCKS = 256
SLOTS = 16
LBLK_DEV = 24
POOL = 96
STEP = 4
STEPS = 6
SPAN = 16
NAMED = 4
POS = 8
DOCS = 160
HALF = 80
SHARD = 320
RING = 4
AXES = ("feat", "label_0", "label_1", "label_2")
LABEL = AXES[1:]
MESH = pl.DeviceIdType.MESH
MIB = 1 << 20

PARTS = (((2, 0, 1), 0, 112), ((0, 1, 2), 112, 112), ((1, 2, 0), 224, 96))
NEAR, BACK = (1, 3, 2), (3, 1, 2)
LINES = (0, 3, 1, 2)


def hop(m, k):
    return lax.rem(m + k, RING)


def label_peer(l):
    return {
        "label_0": lax.div(l, 8),
        "label_1": lax.rem(lax.div(l, 2), 4),
        "label_2": lax.rem(l, 2),
    }


def cell(part, ta, tb, tc, lead=()):
    order, row, rows = part
    index = [None] * 3
    for axis, t in zip(order, (ta, tb, tc)):
        index[axis] = t
    return (*index, *lead, pl.ds(row, rows), slice(None))


def two(half):
    return pl.ds(2 * half, 2)


def rank_tables(keys, tables_ref):
    count = LBLK_DEV * SLOTS
    turned = keys.T
    tables_ref[...] = jnp.zeros((8, count), jnp.int32)
    lanes = lax.broadcasted_iota(jnp.int32, (count, count), 1)
    for r in range(2):
        row, col = keys[r : r + 1, :], turned[:, r : r + 1]
        below = jnp.sum(jnp.where(row < col, 1.0, 0.0), axis=1, keepdims=True).astype(jnp.int32)
        if r == 0:
            sort = jnp.where(below == lanes, col.astype(jnp.float32), 0.0)
            tables_ref[0:1, :] = jnp.sum(sort, axis=0, keepdims=True).astype(jnp.int32)
            above = jnp.sum(jnp.where(col < row, 1.0, 0.0), axis=0, keepdims=True)
            tables_ref[1:2, :] = lax.shift_right_logical(above.astype(jnp.int32), 2)
            tables_ref[4:5, :] = lax.shift_right_logical(row, 9)
        place = lax.shift_right_logical(below, 2)
        first = jnp.where(place * NAMED == below, place - POOL, 0).astype(jnp.float32)
        hit = lax.shift_right_logical(col, 9) == lanes[:, :FBLOCKS]
        table = jnp.sum(jnp.where(hit, first, 0.0), axis=0, keepdims=True)
        tables_ref[2 + r : 3 + r, 0:FBLOCKS] = table.astype(jnp.int32) + POOL


def expand_kernel(
    keys_ref, docs_in, weight_ref, hid_ref, docs_all, mask_ref, tables_ref, docs_ref, w_all, shard,
    w_send, w_recv, d_send, d_recv, own_sem, send, recv, sib_send, sib_recv,
):
    y, z, x, c = (lax.axis_index(a) for a in AXES)
    here = (y, z, x)
    me = z * 8 + x * 2 + c
    sibling = {"label_2": 1 - c}
    peer = label_peer
    docs_ref[:, 0:DOCS] = docs_in[...]
    docs_ref[:, DOCS:] = jnp.zeros((32, 256 - DOCS), jnp.bfloat16)
    barrier = pltpu.get_barrier_semaphore()

    def greet(o, carry):
        pl.semaphore_signal(
            barrier, inc=1, device_id=peer(lax.rem(me + o, 32)), device_id_type=MESH
        )
        return carry

    lax.fori_loop(1, 32, greet, 0)
    for k in (1, 2, 3):
        pl.semaphore_signal(barrier, inc=1, device_id={"feat": hop(y, k)}, device_id_type=MESH)
    pl.semaphore_wait(barrier, 34)

    def rows_of(ref, l):
        return ref.at[lax.div(l, 2), lax.rem(l, 2)]

    def columns_for(l):
        return weight_ref.at[:, pl.ds(pl.multiple_of(l * 256, 256), 256)]

    def docs_copy(to, origin):
        return pltpu.make_async_remote_copy(
            src_ref=docs_ref, dst_ref=rows_of(docs_all, origin),
            send_sem=d_send.at[to], recv_sem=d_recv.at[origin],
            device_id=peer(to), device_id_type=MESH,
        )

    def docs_pair(core):
        return pltpu.make_async_remote_copy(
            src_ref=docs_all.at[:, core], dst_ref=docs_all.at[:, core],
            send_sem=own_sem.at[3], recv_sem=own_sem.at[4],
            device_id=sibling, device_id_type=MESH,
        )

    def weight_copy(to, origin):
        return pltpu.make_async_remote_copy(
            src_ref=columns_for(to), dst_ref=rows_of(w_all, origin),
            send_sem=w_send.at[to], recv_sem=w_recv.at[origin],
            device_id=peer(to), device_id_type=MESH,
        )

    def same_core(o):
        return lax.rem(me + 2 * o, 32)

    def start_docs(o, carry):
        docs_copy(same_core(o), me).start()
        return carry

    def start_weight(o, carry):
        weight_copy(lax.rem(me + o, 32), me).start()
        return carry

    lax.fori_loop(1, 16, start_docs, 0)
    lax.fori_loop(1, 32, start_weight, 0)
    own_docs = pltpu.make_async_copy(docs_ref, rows_of(docs_all, me), own_sem.at[0])
    own_weight = pltpu.make_async_copy(columns_for(me), rows_of(w_all, me), own_sem.at[1])
    own_docs.start()
    own_weight.start()
    rank_tables(keys_ref[...], tables_ref)
    own_docs.wait()
    own_weight.wait()

    def finish_docs(o, carry):
        docs_copy(same_core(o), same_core(o)).wait_recv()
        return carry

    def finish_weight(o, carry):
        other = lax.rem(me + o, 32)
        weight_copy(other, other).wait_recv()
        return carry

    lax.fori_loop(1, 16, finish_docs, 0)
    docs_pair(c).start()
    lax.fori_loop(1, 32, finish_weight, 0)
    docs_pair(1 - c).wait_recv()
    product = lax.dot_general(
        docs_all[...].reshape(1024, 256), w_all[...].reshape(1024, 256),
        (((0,), (0,)), ((), ())), preferred_element_type=jnp.float32,
    )
    hidden = jnp.maximum(product, 0.0).astype(jnp.bfloat16)
    shard[0:DOCS, :] = hidden[:DOCS, :BLK]
    shard[DOCS:SHARD, :] = hidden[:DOCS, BLK:]
    own_hidden = pltpu.make_async_copy(shard, hid_ref.at[y, z, x, c], own_sem.at[2])
    own_hidden.start()

    started = []

    def copy(at, slot, axis, k, source=None):
        return pltpu.make_async_remote_copy(
            src_ref=hid_ref.at[at] if source is None else source,
            dst_ref=hid_ref.at[at],
            send_sem=send.at[slot],
            recv_sem=recv.at[slot],
            device_id={AXES[axis]: hop(here[axis], k)},
            device_id_type=MESH,
        )

    def go(op):
        op.start()
        started.append(op)

    def coords(p):
        return tuple(here[axis] for axis in PARTS[p][0])

    def first(p, way, origin, source=None):
        a, b, t = coords(p)
        return copy(
            cell(PARTS[p], origin, b, t, (c,)), p * 3 + way, PARTS[p][0][0], NEAR[way], source
        )

    def second(p, way, k, line, half):
        t = coords(p)[2]
        at = cell(PARTS[p], two(half), line, t, (c,))
        return copy(at, 9 + (p * 2 + way) * 3 + k, PARTS[p][0][1], NEAR[way])

    def third(p, sub, way, k, t, half):
        line = hop(coords(p)[1], LINES[sub])
        at = cell(PARTS[p], two(half), line, t, (c,))
        return copy(at, 27 + ((p * 4 + sub) * 2 + way) * 3 + k, PARTS[p][0][2], NEAR[way])

    def pair_copy(p, k, at):
        return pltpu.make_async_remote_copy(
            src_ref=hid_ref.at[at], dst_ref=hid_ref.at[at],
            send_sem=sib_send.at[p * 13 + k], recv_sem=sib_recv.at[p * 13 + k],
            device_id=sibling, device_id_type=MESH,
        )

    def pair_plane(p, core):
        return pair_copy(p, 0, cell(PARTS[p], slice(None), slice(None), coords(p)[2], (core,)))

    def pair_line(p, sub, way, core):
        _, b, t = coords(p)
        at = cell(PARTS[p], slice(None), hop(b, LINES[sub]), hop(t, BACK[way]), (core,))
        return pair_copy(p, 1 + sub * 3 + way, at)

    def send_line(p, sub):
        for k in range(2):
            for way in range(2):
                go(third(p, sub, way, k, coords(p)[2], way if k == 0 else 1 - way))

    def pass_line(p, sub):
        for way in range(2):
            near = hop(coords(p)[2], BACK[way])
            third(p, sub, way, 0, near, way).wait_recv()
            go(third(p, sub, way, 2, near, way))

    def finish_line(p, sub):
        for way in range(2):
            third(p, sub, way, 1, hop(coords(p)[2], BACK[way]), 1 - way).wait_recv()
            go(pair_line(p, sub, way, c))
        for way in range(2):
            third(p, sub, way, 2, hop(coords(p)[2], 2), way).wait_recv()
        go(pair_line(p, sub, 2, c))

    parts = range(3)
    for way in (2, 0, 1):
        for p in parts:
            _, row, rows = PARTS[p]
            go(first(p, way, coords(p)[0], shard.at[pl.ds(row, rows), :]))
    own_hidden.wait()
    for p in parts:
        a, b, t = coords(p)
        for way in range(3):
            first(p, way, hop(a, BACK[way])).wait_recv()
        for k in range(2):
            for way in range(2):
                go(second(p, way, k, b, way if k == 0 else 1 - way))
        send_line(p, 0)
    for p in parts:
        b = coords(p)[1]
        for way in range(2):
            near = hop(b, BACK[way])
            second(p, way, 0, near, way).wait_recv()
            go(second(p, way, 2, near, way))
    for p in parts:
        pass_line(p, 0)
    for p in parts:
        b = coords(p)[1]
        for way in range(2):
            second(p, way, 1, hop(b, BACK[way]), 1 - way).wait_recv()
            send_line(p, 1 + way)
    for p in parts:
        for way in range(2):
            second(p, way, 2, hop(coords(p)[1], 2), way).wait_recv()
        send_line(p, 3)
        go(pair_plane(p, c))
    for sub in (1, 2):
        for p in parts:
            pass_line(p, sub)
    for p in parts:
        finish_line(p, 0)
    for p in parts:
        pass_line(p, 3)
    for sub in (1, 2, 3):
        for p in parts:
            finish_line(p, sub)
    for p in parts:
        pair_plane(p, 1 - c).wait_recv()
    for blk in range(4):
        op = pltpu.make_async_copy(
            hid_ref.at[
                y, z, x, blk // 2,
                pl.ds(pl.multiple_of(blk % 2 * DOCS + c * HALF, 16), HALF), slice(None),
            ],
            mask_ref.at[pl.ds(blk * HALF, HALF), :],
            own_sem.at[5 + blk],
        )
        op.start()
    for p in parts:
        for sub in range(4):
            for way in range(3):
                pair_line(p, sub, way, 1 - c).wait_recv()
    for op in started:
        op.wait_send()
    for blk in range(4):
        pltpu.make_async_copy(
            mask_ref.at[pl.ds(blk * HALF, HALF), :], mask_ref.at[pl.ds(blk * HALF, HALF), :], own_sem.at[5 + blk]
        ).wait()
    docs_pair(c).wait_send()
    def drain_docs(o, carry):
        docs_copy(same_core(o), me).wait_send()
        return carry

    def drain_weight(o, carry):
        weight_copy(lax.rem(me + o, 32), me).wait_send()
        return carry

    lax.fori_loop(1, 16, drain_docs, 0)
    lax.fori_loop(1, 32, drain_weight, 0)


def expand(keys, docs_t, expand_weight):
    vmem = pl.BlockSpec(memory_space=pltpu.VMEM)
    return pl.pallas_call(
        expand_kernel,
        out_shape=(
            jax.ShapeDtypeStruct((4, 4, 4, 2, SHARD, BLK), jnp.bfloat16),
            jax.ShapeDtypeStruct((16, 2, 32, 256), jnp.bfloat16),
            jax.ShapeDtypeStruct((SHARD, BLK), jnp.bfloat16),
            jax.ShapeDtypeStruct((8, LBLK_DEV * SLOTS), jnp.int32),
        ),
        in_specs=[vmem, vmem, pl.BlockSpec(memory_space=pltpu.HBM)],
        out_specs=(pl.BlockSpec(memory_space=pl.ANY), vmem, vmem, vmem),
        scratch_shapes=[
            pltpu.VMEM((32, 256), jnp.bfloat16),
            pltpu.VMEM((16, 2, 32, 256), jnp.bfloat16),
            pltpu.VMEM((SHARD, BLK), jnp.bfloat16),
            pltpu.SemaphoreType.DMA((32,)),
            pltpu.SemaphoreType.DMA((32,)),
            pltpu.SemaphoreType.DMA((32,)),
            pltpu.SemaphoreType.DMA((32,)),
            pltpu.SemaphoreType.DMA((9,)),
            pltpu.SemaphoreType.DMA((99,)),
            pltpu.SemaphoreType.DMA((99,)),
            pltpu.SemaphoreType.DMA((39,)),
            pltpu.SemaphoreType.DMA((39,)),
        ],
        compiler_params=pltpu.CompilerParams(
            collective_id=0, has_side_effects=True, vmem_limit_bytes=36 * MIB
        ),
        name="expand",
    )(keys, docs_t, expand_weight)


def label_kernel(
    tables, base, pos_ref, hid, weight_ref, gs_ref, gp_ref, h_t, w, res, pos_b, gp, w_sem, gp_sem,
):
    step = pl.program_id(0)

    def weight_copy(k):
        part = pl.ds(k * STEP, STEP)
        return pltpu.make_async_copy(weight_ref.at[part], w.at[part], w_sem.at[k])

    def gp_copy(k):
        part = pl.ds(k * SPAN, SPAN)
        return pltpu.make_async_copy(gp.at[part], gp_ref.at[part], gp_sem.at[k])

    @pl.when(step == 0)
    def _():
        for k in range(STEPS):
            weight_copy(k).start()
        turned = pos_ref[...].T
        for k in range(POS):
            pos_b[k] = jnp.broadcast_to(turned[:, k : k + 1], (DOCS, BLK))

    def listed(place):
        return hid[lax.div(tables[0, place * NAMED], 512)]

    @pl.when(step < STEPS)
    def _():
        weight_copy(step).wait()
        for k in range(STEP):
            q = step * STEP + k
            logits = jnp.zeros((DOCS, BLK), jnp.float32)
            for s in range(0, SLOTS, 2):
                left = jnp.concatenate(
                    [hid[tables[4, q * SLOTS + s + i]] for i in range(2)], axis=1
                )
                right = w[q, s : s + 2].reshape(2 * BLK, BLK)
                logits += jnp.dot(left, right, preferred_element_type=jnp.float32)
            ids = (base[0] + q) * BLK + lax.broadcasted_iota(jnp.int32, (DOCS, BLK), 1)
            hit = pos_b[0] == ids
            for i in range(1, POS):
                hit = jnp.logical_or(hit, pos_b[i] == ids)
            res[q] = (jax.nn.sigmoid(logits) - jnp.where(hit, 1.0, 0.0)).astype(jnp.bfloat16)
        for k in range(SPAN):
            place = step * SPAN + k
            h_t[place] = listed(place).T

    @pl.when(step >= STEPS)
    def _():
        late = step - STEPS
        for k in range(STEP):
            q = late * STEP + k
            residual = res[q]
            for s in range(SLOTS):
                gs_ref[k, s] = jnp.dot(
                    h_t[tables[1, q * SLOTS + s]], residual, preferred_element_type=jnp.float32
                ).astype(jnp.bfloat16)
        for k in range(SPAN):
            place = late * SPAN + k
            slots = [lax.rem(tables[0, place * NAMED + i], 512) for i in range(NAMED)]
            pairs = [(lax.div(i, SLOTS), lax.rem(i, SLOTS)) for i in slots]
            left = jnp.concatenate([res[q] for q, _ in pairs], axis=1)
            right = jnp.concatenate([w[q, s] for q, s in pairs], axis=1)
            gp[place] = lax.dot_general(
                left, right, (((1,), (1,)), ((), ())), preferred_element_type=jnp.float32
            ).astype(jnp.bfloat16)
        gp_copy(late).start()

    @pl.when(step == 2 * STEPS - 1)
    def _():
        for k in range(STEPS):
            gp_copy(k).wait()


def label_blocks(tables, base, positives, hid, sparse_weight):
    return pl.pallas_call(
        label_kernel,
        out_shape=(
            jax.ShapeDtypeStruct((LBLK_DEV, SLOTS, BLK, BLK), jnp.bfloat16),
            jax.ShapeDtypeStruct((POOL, DOCS, BLK), jnp.bfloat16),
        ),
        grid_spec=pltpu.PrefetchScalarGridSpec(
            num_scalar_prefetch=2,
            grid=(2 * STEPS,),
            in_specs=[
                pl.BlockSpec((POS, DOCS), lambda g, *_: (0, 0)),
                pl.BlockSpec(memory_space=pltpu.VMEM),
                pl.BlockSpec(memory_space=pl.ANY),
            ],
            out_specs=(
                pl.BlockSpec(
                    (STEP, SLOTS, BLK, BLK), lambda g, *_: (jnp.maximum(g - STEPS, 0), 0, 0, 0)
                ),
                pl.BlockSpec(memory_space=pl.ANY),
            ),
            scratch_shapes=[
                pltpu.VMEM((POOL, BLK, DOCS), jnp.bfloat16),
                pltpu.VMEM((LBLK_DEV, SLOTS, BLK, BLK), jnp.bfloat16),
                pltpu.VMEM((LBLK_DEV, DOCS, BLK), jnp.bfloat16),
                pltpu.VMEM((POS, DOCS, BLK), jnp.int32),
                pltpu.VMEM((POOL, DOCS, BLK), jnp.bfloat16),
                pltpu.SemaphoreType.DMA((STEPS,)),
                pltpu.SemaphoreType.DMA((STEPS,)),
            ],
        ),
        compiler_params=pltpu.CompilerParams(
            dimension_semantics=("arbitrary",), vmem_limit_bytes=36 * MIB
        ),
        name="label_blocks",
    )(tables, base, positives, hid, sparse_weight)


def reduce_kernel(
    tables, gp_ref, mask, docs_ref, out_ref,
    own, sib, acc, grad, mine_grad, pieces, *rest,
):
    across2, near2, across1, near1, near0 = (rest[k * 3 : k * 3 + 3] for k in range(5))
    pair_sem, send, recv, o_send, o_recv = rest[15:]
    y, z, x, c = (lax.axis_index(a) for a in AXES)
    here = (y, z, x)
    sibling = {"label_2": 1 - c}
    me = z * 8 + x * 2 + c
    barrier = pltpu.get_barrier_semaphore()

    for axis, m in zip(AXES, here):
        for k in (1, 3):
            pl.semaphore_signal(barrier, inc=1, device_id={axis: hop(m, k)}, device_id_type=MESH)
    pl.semaphore_signal(barrier, inc=1, device_id=sibling, device_id_type=MESH)

    def docs_half(k):
        return gp_ref.at[:, pl.ds(pl.multiple_of(k * HALF, 16), HALF), :]

    to_pair = pltpu.make_async_remote_copy(
        src_ref=docs_half(1 - c), dst_ref=sib.at[pl.ds(0, POOL)],
        send_sem=pair_sem.at[0], recv_sem=pair_sem.at[1],
        device_id=sibling, device_id_type=MESH,
    )
    mine = pltpu.make_async_copy(docs_half(c), own.at[pl.ds(0, POOL)], pair_sem.at[2])
    mine.start()
    own[POOL] = jnp.zeros((HALF, BLK), jnp.bfloat16)
    sib[POOL] = jnp.zeros((HALF, BLK), jnp.bfloat16)
    pl.semaphore_wait(barrier, 7)
    to_pair.start()
    mine.wait()
    to_pair.wait()

    parts = range(3)
    started = []

    def coords(p):
        return tuple(here[axis] for axis in PARTS[p][0])

    def spread(p, sub):
        order, row, rows = PARTS[p]
        line = hop(coords(p)[1], LINES[sub])

        def one(i, carry):
            at = cell(PARTS[p], lax.div(i, 4), line, lax.rem(i, 4))
            first_block = ((at[0] * 4 + at[1]) * 4 + at[2]) * 4
            for blk in range(row // HALF, (row + rows - 1) // HALF + 1):
                low, high = max(row, blk * HALF), min(row + rows, blk * HALF + HALF)
                span = pl.ds(low - blk * HALF, high - low)
                b = first_block + blk
                acc[(*at[:3], pl.ds(low, high - low), slice(None))] = (
                    own[tables[2, b], span, :] + sib[tables[3, b], span, :]
                )
            return carry

        lax.fori_loop(0, 16, one, 0)

    def push(source, target, slot, axis, k):
        return pltpu.make_async_remote_copy(
            src_ref=acc.at[source], dst_ref=target, send_sem=send.at[slot], recv_sem=recv.at[slot],
            device_id={AXES[axis]: hop(here[axis], k)}, device_id_type=MESH,
        )

    def go(op):
        op.start()
        started.append(op)

    def third(p, sub, way, k):
        line, t = hop(coords(p)[1], LINES[sub]), coords(p)[2]
        half = 1 - way if k == 1 else way
        source = cell(PARTS[p], two(half), line, hop(t, 2 if k == 0 else NEAR[way]))
        target = across2[p].at[sub, way] if k == 0 else near2[p].at[sub, way, two(half)]
        slot = 27 + ((p * 4 + sub) * 2 + way) * 3 + k
        return push(source, target, slot, PARTS[p][0][2], NEAR[way])

    def second(p, way, k):
        _, b, t = coords(p)
        half = 1 - way if k == 1 else way
        source = cell(PARTS[p], two(half), hop(b, 2 if k == 0 else NEAR[way]), t)
        target = across1[p].at[way] if k == 0 else near1[p].at[way, two(half)]
        return push(source, target, 9 + (p * 2 + way) * 3 + k, PARTS[p][0][1], NEAR[way])

    def first(p, way):
        a, b, t = coords(p)
        source = cell(PARTS[p], hop(a, NEAR[way]), b, t)
        return push(source, near0[p].at[way], p * 3 + way, PARTS[p][0][0], NEAR[way])

    def add(at, *terms):
        total = acc[at].astype(jnp.float32)
        for term in terms:
            total = total + term.astype(jnp.float32)
        acc[at] = total.astype(jnp.bfloat16)

    def send_line(p, sub):
        spread(p, sub)
        for k in range(2):
            for way in range(2):
                go(third(p, sub, way, k))

    def pass_line(p, sub):
        line, t = hop(coords(p)[1], LINES[sub]), coords(p)[2]
        for way in range(2):
            third(p, sub, way, 0).wait_recv()
            for i in range(2):
                add(
                    cell(PARTS[p], 2 * way + i, line, hop(t, NEAR[way])),
                    across2[p][sub, way, i],
                )
            go(third(p, sub, way, 2))

    def finish_line(p, sub):
        line, t = hop(coords(p)[1], LINES[sub]), coords(p)[2]
        for way in range(2):
            third(p, sub, way, 1).wait_recv()
            third(p, sub, way, 2).wait_recv()
        for i in range(4):
            add(cell(PARTS[p], i, line, t), near2[p][sub, 0, i], near2[p][sub, 1, i])

    for p in parts:
        send_line(p, 3)
    for p in parts:
        send_line(p, 1)
    for p in parts:
        pass_line(p, 3)
        send_line(p, 2)
    for p in parts:
        pass_line(p, 1)
        send_line(p, 0)
    for p in parts:
        finish_line(p, 3)
        for way in range(2):
            go(second(p, way, 0))
    for p in parts:
        pass_line(p, 2)
    for p in parts:
        pass_line(p, 0)
    for p in parts:
        finish_line(p, 1)
        finish_line(p, 2)
        for way in range(2):
            go(second(p, way, 1))
    for p in parts:
        _, b, t = coords(p)
        for way in range(2):
            second(p, way, 0).wait_recv()
            for i in range(2):
                add(cell(PARTS[p], 2 * way + i, hop(b, NEAR[way]), t), across1[p][way, i])
            go(second(p, way, 2))
    for p in parts:
        finish_line(p, 0)
    for p in parts:
        _, b, t = coords(p)
        for way in range(2):
            second(p, way, 1).wait_recv()
            second(p, way, 2).wait_recv()
        for i in range(4):
            add(cell(PARTS[p], i, b, t), near1[p][0, i], near1[p][1, i])
        for way in (2, 0, 1):
            go(first(p, way))
    for p in parts:
        for way in range(3):
            first(p, way).wait_recv()
        add(cell(PARTS[p], *coords(p)), *(near0[p][way] for way in range(3)))

    total = acc[y, z, x]
    grad[...] = jnp.where(mask[...] > 0, total, jnp.zeros_like(total))

    def columns(k):
        return grad.at[pl.ds(pl.multiple_of(k * DOCS, 16), DOCS), :]

    def pair_grad(k, core):
        return pltpu.make_async_remote_copy(
            src_ref=columns(k), dst_ref=mine_grad.at[core],
            send_sem=pair_sem.at[3], recv_sem=pair_sem.at[4],
            device_id=sibling, device_id_type=MESH,
        )

    to_other = pair_grad(1 - c, c)
    to_other.start()
    kept = pltpu.make_async_copy(columns(c), mine_grad.at[c], pair_sem.at[5])
    kept.start()
    kept.wait()
    pair_grad(c, 1 - c).wait_recv()
    sides = [
        jnp.concatenate([mine_grad[half, pl.ds(j * HALF, HALF), :] for half in range(2)], axis=0)
        for j in range(2)
    ]
    right = jnp.concatenate(sides, axis=1)

    def out_columns(l):
        return out_ref.at[:, pl.ds(pl.multiple_of(l * 256, 256), 256)]

    def out_copy(to, origin):
        return pltpu.make_async_remote_copy(
            src_ref=pieces.at[to], dst_ref=out_columns(origin),
            send_sem=o_send.at[to], recv_sem=o_recv.at[origin],
            device_id=label_peer(to), device_id_type=MESH,
        )

    own_out = pltpu.make_async_copy(pieces.at[me], out_columns(me), pair_sem.at[6])
    for k in range(4):
        row = hop(z, k) * 8
        left = docs_ref[pl.ds(hop(z, k) * 4, 4)].reshape(256, 256)[:, :DOCS]
        pieces[pl.ds(row, 8)] = jnp.dot(
            left, right, preferred_element_type=jnp.float32
        ).astype(jnp.bfloat16).reshape(8, 32, 256)

        def deliver(o, carry):
            out_copy(row + lax.rem(x * 2 + c + o, 8), me).start()
            return carry

        lax.fori_loop(1 if k == 0 else 0, 8, deliver, 0)
        if k == 0:
            own_out.start()
    own_out.wait()

    def collect(o, carry):
        other = lax.rem(me + o, 32)
        out_copy(other, other).wait_recv()
        return carry

    def drain(o, carry):
        out_copy(lax.rem(me + o, 32), me).wait_send()
        return carry

    lax.fori_loop(1, 32, collect, 0)
    to_other.wait_send()
    for op in started:
        op.wait_send()
    lax.fori_loop(1, 32, drain, 0)


def reduce_blocks(tables, gp, mask, docs_all):
    received = [
        pltpu.VMEM((*lead, rows, BLK), jnp.bfloat16)
        for lead in ((4, 2, 2), (4, 2, 4), (2, 2), (2, 4), (3,))
        for _, _, rows in PARTS
    ]
    return pl.pallas_call(
        reduce_kernel,
        out_shape=jax.ShapeDtypeStruct((32, 8192), jnp.bfloat16),
        in_specs=[
            pl.BlockSpec(memory_space=pltpu.SMEM),
            pl.BlockSpec(memory_space=pl.ANY),
            pl.BlockSpec(memory_space=pltpu.VMEM),
            pl.BlockSpec(memory_space=pltpu.VMEM),
        ],
        out_specs=pl.BlockSpec(memory_space=pltpu.VMEM),
        scratch_shapes=[
            pltpu.VMEM((POOL + 1, HALF, BLK), jnp.bfloat16),
            pltpu.VMEM((POOL + 1, HALF, BLK), jnp.bfloat16),
            pltpu.VMEM((4, 4, 4, SHARD, BLK), jnp.bfloat16),
            pltpu.VMEM((SHARD, BLK), jnp.bfloat16),
            pltpu.VMEM((2, DOCS, BLK), jnp.bfloat16),
            pltpu.VMEM((32, 32, 256), jnp.bfloat16),
            *received,
            pltpu.SemaphoreType.DMA((7,)),
            pltpu.SemaphoreType.DMA((99,)),
            pltpu.SemaphoreType.DMA((99,)),
            pltpu.SemaphoreType.DMA((32,)),
            pltpu.SemaphoreType.DMA((32,)),
        ],
        compiler_params=pltpu.CompilerParams(
            collective_id=1, has_side_effects=True, vmem_limit_bytes=24 * MIB
        ),
        name="reduce_blocks",
    )(tables, gp, mask, docs_all)


def on_device(documents, expand_weight, sparse_weight, feature_lists, positives):
    core = lax.axis_index("label_2")
    group = lax.axis_index(AXES)
    pair = lax.dynamic_slice_in_dim(feature_lists, (group - core) * LBLK_DEV, 2 * LBLK_DEV, 0)
    pair = pair.reshape(2, LBLK_DEV * SLOTS)
    keys = jnp.where(core == 0, pair, pair[::-1]) * 512
    keys = jnp.pad(keys + jnp.arange(LBLK_DEV * SLOTS, dtype=jnp.int32)[None, :], ((0, 6), (0, 0)))
    weight = pltpu.with_memory_space_constraint(expand_weight, pltpu.HBM)
    hid, docs_all, mask, tables = expand(keys, documents.T, weight)
    grad_sparse, gp = label_blocks(
        tables,
        (group * LBLK_DEV).astype(jnp.int32).reshape(1),
        positives.T,
        hid.reshape(FBLOCKS, DOCS, BLK),
        sparse_weight,
    )
    grad_expand = reduce_blocks(tables, gp, mask, docs_all)
    return (grad_expand, grad_sparse)


def solution(mesh):
    finer = Mesh(mesh.devices.reshape(mesh.shape["feat"], 4, 4, 2), AXES)
    return jax.shard_map(
        on_device,
        mesh=finer,
        in_specs=(P(None, LABEL), P(LABEL, "feat"), P(AXES, None, None, None), P(), P()),
        out_specs=(P(LABEL, "feat"), P(AXES, None, None, None)),
        check_vma=False,
    )
```

```python
import functools

import jax
import jax.numpy as jnp
from jax import lax
from jax.experimental import pallas as pl
from jax.experimental.pallas import tpu as pltpu
from jax.sharding import Mesh
from jax.sharding import PartitionSpec as P

BLK = 128
FBLOCKS = 256
SLOTS = 16
LBLK_DEV = 24
POOL = 96
STEP = 4
STEPS = 6
SPAN = 16
NAMED = 4
POS = 8
DOCS = 160
HALF = 80
SHARD = 320
RING = 4
AXES = ("feat", "label_0", "label_1", "label_2")
LABEL = AXES[1:]
MESH = pl.DeviceIdType.MESH
MIB = 1 << 20

PARTS = (((2, 0, 1), 0, 112), ((0, 1, 2), 112, 112), ((1, 2, 0), 224, 96))
NEAR, BACK = (1, 3, 2), (3, 1, 2)
LINES = (0, 3, 1, 2)


def hop(m, k):
    return lax.rem(m + k, RING)


def label_peer(l):
    return {
        "label_0": lax.div(l, 8),
        "label_1": lax.rem(lax.div(l, 2), 4),
        "label_2": lax.rem(l, 2),
    }


def cell(part, ta, tb, tc, lead=()):
    order, row, rows = part
    index = [None] * 3
    for axis, t in zip(order, (ta, tb, tc)):
        index[axis] = t
    return (*index, *lead, pl.ds(row, rows), slice(None))


def two(half):
    return pl.ds(2 * half, 2)


def rank_tables(keys, tables_ref):
    count = LBLK_DEV * SLOTS
    turned = keys.T
    tables_ref[...] = jnp.zeros((8, count), jnp.int32)
    lanes = lax.broadcasted_iota(jnp.int32, (count, count), 1)
    for r in range(2):
        row, col = keys[r : r + 1, :], turned[:, r : r + 1]
        below = jnp.sum(jnp.where(row < col, 1.0, 0.0), axis=1, keepdims=True).astype(jnp.int32)
        if r == 0:
            sort = jnp.where(below == lanes, col.astype(jnp.float32), 0.0)
            tables_ref[0:1, :] = jnp.sum(sort, axis=0, keepdims=True).astype(jnp.int32)
            above = jnp.sum(jnp.where(col < row, 1.0, 0.0), axis=0, keepdims=True)
            tables_ref[1:2, :] = lax.shift_right_logical(above.astype(jnp.int32), 2)
            tables_ref[4:5, :] = lax.shift_right_logical(row, 9)
        place = lax.shift_right_logical(below, 2)
        first = jnp.where(place * NAMED == below, place - POOL, 0).astype(jnp.float32)
        hit = lax.shift_right_logical(col, 9) == lanes[:, :FBLOCKS]
        table = jnp.sum(jnp.where(hit, first, 0.0), axis=0, keepdims=True)
        tables_ref[2 + r : 3 + r, 0:FBLOCKS] = table.astype(jnp.int32) + POOL


def expand_kernel(
    keys_ref, docs_in, weight_ref, hid_ref, docs_all, mask_ref, tables_ref, docs_small, docs_ref, w_all, shard,
    w_send, w_recv, d_send, d_recv, own_sem, send, recv, sib_send, sib_recv,
):
    y, z, x, c = (lax.axis_index(a) for a in AXES)
    here = (y, z, x)
    me = z * 8 + x * 2 + c
    sibling = {"label_2": 1 - c}
    peer = label_peer
    load = pltpu.make_async_copy(docs_in, docs_small, own_sem.at[9])
    load.start()
    barrier = pltpu.get_barrier_semaphore()

    def greet(o, carry):
        pl.semaphore_signal(
            barrier, inc=1, device_id=peer(lax.rem(me + o, 32)), device_id_type=MESH
        )
        return carry

    lax.fori_loop(1, 32, greet, 0)
    for k in (1, 2, 3):
        pl.semaphore_signal(barrier, inc=1, device_id={"feat": hop(y, k)}, device_id_type=MESH)
    load.wait()
    docs_ref[:, 0:DOCS] = docs_small[...]
    docs_ref[:, DOCS:] = jnp.zeros((32, 256 - DOCS), jnp.bfloat16)
    pl.semaphore_wait(barrier, 34)

    def rows_of(ref, l):
        return ref.at[lax.div(l, 2), lax.rem(l, 2)]

    def columns_for(l):
        return weight_ref.at[:, pl.ds(pl.multiple_of(l * 256, 256), 256)]

    def docs_copy(to, origin):
        return pltpu.make_async_remote_copy(
            src_ref=docs_ref, dst_ref=rows_of(docs_all, origin),
            send_sem=d_send.at[to], recv_sem=d_recv.at[origin],
            device_id=peer(to), device_id_type=MESH,
        )

    def docs_pair(core):
        return pltpu.make_async_remote_copy(
            src_ref=docs_all.at[:, core], dst_ref=docs_all.at[:, core],
            send_sem=own_sem.at[3], recv_sem=own_sem.at[4],
            device_id=sibling, device_id_type=MESH,
        )

    def weight_copy(to, origin):
        return pltpu.make_async_remote_copy(
            src_ref=columns_for(to), dst_ref=rows_of(w_all, origin),
            send_sem=w_send.at[to], recv_sem=w_recv.at[origin],
            device_id=peer(to), device_id_type=MESH,
        )

    def same_core(o):
        return lax.rem(me + 2 * o, 32)

    def start_docs(o, carry):
        docs_copy(same_core(o), me).start()
        return carry

    def start_weight(o, carry):
        weight_copy(lax.rem(me + o, 32), me).start()
        return carry

    lax.fori_loop(1, 16, start_docs, 0)
    lax.fori_loop(1, 32, start_weight, 0)
    own_docs = pltpu.make_async_copy(docs_ref, rows_of(docs_all, me), own_sem.at[0])
    own_weight = pltpu.make_async_copy(columns_for(me), rows_of(w_all, me), own_sem.at[1])
    own_docs.start()
    own_weight.start()
    rank_tables(keys_ref[...], tables_ref)
    own_docs.wait()
    own_weight.wait()

    def finish_docs(o, carry):
        docs_copy(same_core(o), same_core(o)).wait_recv()
        return carry

    def finish_weight(o, carry):
        other = lax.rem(me + o, 32)
        weight_copy(other, other).wait_recv()
        return carry

    lax.fori_loop(1, 16, finish_docs, 0)
    docs_pair(c).start()
    lax.fori_loop(1, 32, finish_weight, 0)
    docs_pair(1 - c).wait_recv()
    product = lax.dot_general(
        docs_all[...].reshape(1024, 256), w_all[...].reshape(1024, 256),
        (((0,), (0,)), ((), ())), preferred_element_type=jnp.float32,
    )
    hidden = jnp.maximum(product, 0.0).astype(jnp.bfloat16)
    shard[0:DOCS, :] = hidden[:DOCS, :BLK]
    shard[DOCS:SHARD, :] = hidden[:DOCS, BLK:]
    own_hidden = pltpu.make_async_copy(shard, hid_ref.at[y, z, x, c], own_sem.at[2])
    own_hidden.start()

    started = []

    def copy(at, slot, axis, k, source=None):
        return pltpu.make_async_remote_copy(
            src_ref=hid_ref.at[at] if source is None else source,
            dst_ref=hid_ref.at[at],
            send_sem=send.at[slot],
            recv_sem=recv.at[slot],
            device_id={AXES[axis]: hop(here[axis], k)},
            device_id_type=MESH,
        )

    def go(op):
        op.start()
        started.append(op)

    def coords(p):
        return tuple(here[axis] for axis in PARTS[p][0])

    def first(p, way, origin, source=None):
        a, b, t = coords(p)
        return copy(
            cell(PARTS[p], origin, b, t, (c,)), p * 3 + way, PARTS[p][0][0], NEAR[way], source
        )

    def second(p, way, k, line, half):
        t = coords(p)[2]
        at = cell(PARTS[p], two(half), line, t, (c,))
        return copy(at, 9 + (p * 2 + way) * 3 + k, PARTS[p][0][1], NEAR[way])

    def third(p, sub, way, k, t, half):
        line = hop(coords(p)[1], LINES[sub])
        at = cell(PARTS[p], two(half), line, t, (c,))
        return copy(at, 27 + ((p * 4 + sub) * 2 + way) * 3 + k, PARTS[p][0][2], NEAR[way])

    def pair_copy(p, k, at):
        return pltpu.make_async_remote_copy(
            src_ref=hid_ref.at[at], dst_ref=hid_ref.at[at],
            send_sem=sib_send.at[p * 13 + k], recv_sem=sib_recv.at[p * 13 + k],
            device_id=sibling, device_id_type=MESH,
        )

    def pair_plane(p, core):
        return pair_copy(p, 0, cell(PARTS[p], slice(None), slice(None), coords(p)[2], (core,)))

    def pair_line(p, sub, way, core):
        _, b, t = coords(p)
        at = cell(PARTS[p], slice(None), hop(b, LINES[sub]), hop(t, BACK[way]), (core,))
        return pair_copy(p, 1 + sub * 3 + way, at)

    def send_line(p, sub):
        for k in range(2):
            for way in range(2):
                go(third(p, sub, way, k, coords(p)[2], way if k == 0 else 1 - way))

    def pass_line(p, sub):
        for way in range(2):
            near = hop(coords(p)[2], BACK[way])
            third(p, sub, way, 0, near, way).wait_recv()
            go(third(p, sub, way, 2, near, way))

    def finish_line(p, sub):
        for way in range(2):
            third(p, sub, way, 1, hop(coords(p)[2], BACK[way]), 1 - way).wait_recv()
            go(pair_line(p, sub, way, c))
        for way in range(2):
            third(p, sub, way, 2, hop(coords(p)[2], 2), way).wait_recv()
        go(pair_line(p, sub, 2, c))

    parts = range(3)
    for way in (2, 0, 1):
        for p in parts:
            _, row, rows = PARTS[p]
            go(first(p, way, coords(p)[0], shard.at[pl.ds(row, rows), :]))
    own_hidden.wait()
    for p in parts:
        a, b, t = coords(p)
        for way in range(3):
            first(p, way, hop(a, BACK[way])).wait_recv()
        for k in range(2):
            for way in range(2):
                go(second(p, way, k, b, way if k == 0 else 1 - way))
        send_line(p, 0)
    for p in parts:
        b = coords(p)[1]
        for way in range(2):
            near = hop(b, BACK[way])
            second(p, way, 0, near, way).wait_recv()
            go(second(p, way, 2, near, way))
    for p in parts:
        pass_line(p, 0)
    for p in parts:
        b = coords(p)[1]
        for way in range(2):
            second(p, way, 1, hop(b, BACK[way]), 1 - way).wait_recv()
            send_line(p, 1 + way)
    for p in parts:
        for way in range(2):
            second(p, way, 2, hop(coords(p)[1], 2), way).wait_recv()
        send_line(p, 3)
        go(pair_plane(p, c))
    for sub in (1, 2):
        for p in parts:
            pass_line(p, sub)
    for p in parts:
        finish_line(p, 0)
    for p in parts:
        pass_line(p, 3)
    for sub in (1, 2, 3):
        for p in parts:
            finish_line(p, sub)
    for p in parts:
        pair_plane(p, 1 - c).wait_recv()
    for blk in range(4):
        op = pltpu.make_async_copy(
            hid_ref.at[
                y, z, x, blk // 2,
                pl.ds(pl.multiple_of(blk % 2 * DOCS + c * HALF, 16), HALF), slice(None),
            ],
            mask_ref.at[pl.ds(blk * HALF, HALF), :],
            own_sem.at[5 + blk],
        )
        op.start()
    for p in parts:
        for sub in range(4):
            for way in range(3):
                pair_line(p, sub, way, 1 - c).wait_recv()
    for op in started:
        op.wait_send()
    for blk in range(4):
        pltpu.make_async_copy(
            mask_ref.at[pl.ds(blk * HALF, HALF), :], mask_ref.at[pl.ds(blk * HALF, HALF), :], own_sem.at[5 + blk]
        ).wait()
    docs_pair(c).wait_send()
    def drain_docs(o, carry):
        docs_copy(same_core(o), me).wait_send()
        return carry

    def drain_weight(o, carry):
        weight_copy(lax.rem(me + o, 32), me).wait_send()
        return carry

    lax.fori_loop(1, 16, drain_docs, 0)
    lax.fori_loop(1, 32, drain_weight, 0)


def expand(keys, docs_t, expand_weight):
    vmem = pl.BlockSpec(memory_space=pltpu.VMEM)
    return pl.pallas_call(
        expand_kernel,
        out_shape=(
            jax.ShapeDtypeStruct((4, 4, 4, 2, SHARD, BLK), jnp.bfloat16),
            jax.ShapeDtypeStruct((16, 2, 32, 256), jnp.bfloat16),
            jax.ShapeDtypeStruct((SHARD, BLK), jnp.bfloat16),
            jax.ShapeDtypeStruct((8, LBLK_DEV * SLOTS), jnp.int32),
        ),
        in_specs=[vmem, pl.BlockSpec(memory_space=pl.ANY), pl.BlockSpec(memory_space=pl.ANY)],
        out_specs=(pl.BlockSpec(memory_space=pl.ANY), vmem, vmem, vmem),
        scratch_shapes=[
            pltpu.VMEM((32, DOCS), jnp.bfloat16),
            pltpu.VMEM((32, 256), jnp.bfloat16),
            pltpu.VMEM((16, 2, 32, 256), jnp.bfloat16),
            pltpu.VMEM((SHARD, BLK), jnp.bfloat16),
            pltpu.SemaphoreType.DMA((32,)),
            pltpu.SemaphoreType.DMA((32,)),
            pltpu.SemaphoreType.DMA((32,)),
            pltpu.SemaphoreType.DMA((32,)),
            pltpu.SemaphoreType.DMA((10,)),
            pltpu.SemaphoreType.DMA((99,)),
            pltpu.SemaphoreType.DMA((99,)),
            pltpu.SemaphoreType.DMA((39,)),
            pltpu.SemaphoreType.DMA((39,)),
        ],
        compiler_params=pltpu.CompilerParams(
            collective_id=0, has_side_effects=True, vmem_limit_bytes=36 * MIB
        ),
        name="expand",
    )(keys, docs_t, expand_weight)


def label_kernel(
    tables, base, pos_ref, hid, weight_ref, gs_ref, gp_ref,
    pos, h_t, w, res, pos_b, gp, w_sem, gp_sem, pos_sem,
):
    step = pl.program_id(0)

    def weight_copy(k):
        part = pl.ds(k * STEP, STEP)
        return pltpu.make_async_copy(weight_ref.at[part], w.at[part], w_sem.at[k])

    def gp_copy(k):
        part = pl.ds(k * SPAN, SPAN)
        return pltpu.make_async_copy(gp.at[part], gp_ref.at[part], gp_sem.at[k])

    @pl.when(step == 0)
    def _():
        load = pltpu.make_async_copy(pos_ref, pos, pos_sem)
        load.start()
        for k in range(STEPS):
            weight_copy(k).start()
        load.wait()
        turned = pos[...].T
        for k in range(POS):
            pos_b[k] = jnp.broadcast_to(turned[:, k : k + 1], (DOCS, BLK))

    def listed(place):
        return hid[lax.div(tables[0, place * NAMED], 512)]

    @pl.when(step < STEPS)
    def _():
        weight_copy(step).wait()
        for k in range(STEP):
            q = step * STEP + k
            logits = jnp.zeros((DOCS, BLK), jnp.float32)
            for s in range(0, SLOTS, 2):
                left = jnp.concatenate(
                    [hid[tables[4, q * SLOTS + s + i]] for i in range(2)], axis=1
                )
                right = w[q, s : s + 2].reshape(2 * BLK, BLK)
                logits += jnp.dot(left, right, preferred_element_type=jnp.float32)
            ids = (base[0] + q) * BLK + lax.broadcasted_iota(jnp.int32, (DOCS, BLK), 1)
            hit = pos_b[0] == ids
            for i in range(1, POS):
                hit = jnp.logical_or(hit, pos_b[i] == ids)
            res[q] = (jax.nn.sigmoid(logits) - jnp.where(hit, 1.0, 0.0)).astype(jnp.bfloat16)
        for k in range(SPAN):
            place = step * SPAN + k
            h_t[place] = listed(place).T

    @pl.when(step >= STEPS)
    def _():
        late = step - STEPS
        for k in range(STEP):
            q = late * STEP + k
            residual = res[q]
            for s in range(SLOTS):
                gs_ref[k, s] = jnp.dot(
                    h_t[tables[1, q * SLOTS + s]], residual, preferred_element_type=jnp.float32
                ).astype(jnp.bfloat16)
        for k in range(SPAN):
            place = late * SPAN + k
            slots = [lax.rem(tables[0, place * NAMED + i], 512) for i in range(NAMED)]
            pairs = [(lax.div(i, SLOTS), lax.rem(i, SLOTS)) for i in slots]
            left = jnp.concatenate([res[q] for q, _ in pairs], axis=1)
            right = jnp.concatenate([w[q, s] for q, s in pairs], axis=1)
            gp[place] = lax.dot_general(
                left, right, (((1,), (1,)), ((), ())), preferred_element_type=jnp.float32
            ).astype(jnp.bfloat16)
        gp_copy(late).start()

    @pl.when(step == 2 * STEPS - 1)
    def _():
        for k in range(STEPS):
            gp_copy(k).wait()


def label_blocks(tables, base, positives, hid, sparse_weight):
    return pl.pallas_call(
        label_kernel,
        out_shape=(
            jax.ShapeDtypeStruct((LBLK_DEV, SLOTS, BLK, BLK), jnp.bfloat16),
            jax.ShapeDtypeStruct((POOL, DOCS, BLK), jnp.bfloat16),
        ),
        grid_spec=pltpu.PrefetchScalarGridSpec(
            num_scalar_prefetch=2,
            grid=(2 * STEPS,),
            in_specs=[
                pl.BlockSpec(memory_space=pl.ANY),
                pl.BlockSpec(memory_space=pltpu.VMEM),
                pl.BlockSpec(memory_space=pl.ANY),
            ],
            out_specs=(
                pl.BlockSpec(
                    (STEP, SLOTS, BLK, BLK), lambda g, *_: (jnp.maximum(g - STEPS, 0), 0, 0, 0)
                ),
                pl.BlockSpec(memory_space=pl.ANY),
            ),
            scratch_shapes=[
                pltpu.VMEM((POS, DOCS), jnp.int32),
                pltpu.VMEM((POOL, BLK, DOCS), jnp.bfloat16),
                pltpu.VMEM((LBLK_DEV, SLOTS, BLK, BLK), jnp.bfloat16),
                pltpu.VMEM((LBLK_DEV, DOCS, BLK), jnp.bfloat16),
                pltpu.VMEM((POS, DOCS, BLK), jnp.int32),
                pltpu.VMEM((POOL, DOCS, BLK), jnp.bfloat16),
                pltpu.SemaphoreType.DMA((STEPS,)),
                pltpu.SemaphoreType.DMA((STEPS,)),
                pltpu.SemaphoreType.DMA,
            ],
        ),
        compiler_params=pltpu.CompilerParams(
            dimension_semantics=("arbitrary",), vmem_limit_bytes=36 * MIB
        ),
        name="label_blocks",
    )(tables, base, positives, hid, sparse_weight)


def reduce_kernel(
    tables, gp_ref, mask, docs_ref, out_ref,
    own, sib, acc, grad, mine_grad, pieces, *rest,
):
    across2, near2, across1, near1, near0 = (rest[k * 3 : k * 3 + 3] for k in range(5))
    pair_sem, send, recv, o_send, o_recv = rest[15:]
    y, z, x, c = (lax.axis_index(a) for a in AXES)
    here = (y, z, x)
    sibling = {"label_2": 1 - c}
    me = z * 8 + x * 2 + c
    barrier = pltpu.get_barrier_semaphore()

    for axis, m in zip(AXES, here):
        for k in (1, 3):
            pl.semaphore_signal(barrier, inc=1, device_id={axis: hop(m, k)}, device_id_type=MESH)
    pl.semaphore_signal(barrier, inc=1, device_id=sibling, device_id_type=MESH)

    def docs_half(k):
        return gp_ref.at[:, pl.ds(pl.multiple_of(k * HALF, 16), HALF), :]

    to_pair = pltpu.make_async_remote_copy(
        src_ref=docs_half(1 - c), dst_ref=sib.at[pl.ds(0, POOL)],
        send_sem=pair_sem.at[0], recv_sem=pair_sem.at[1],
        device_id=sibling, device_id_type=MESH,
    )
    mine = pltpu.make_async_copy(docs_half(c), own.at[pl.ds(0, POOL)], pair_sem.at[2])
    mine.start()
    own[POOL] = jnp.zeros((HALF, BLK), jnp.bfloat16)
    sib[POOL] = jnp.zeros((HALF, BLK), jnp.bfloat16)
    pl.semaphore_wait(barrier, 7)
    to_pair.start()
    mine.wait()
    to_pair.wait()

    parts = range(3)
    started = []

    def coords(p):
        return tuple(here[axis] for axis in PARTS[p][0])

    def spread(p, sub):
        order, row, rows = PARTS[p]
        line = hop(coords(p)[1], LINES[sub])

        def one(i, carry):
            at = cell(PARTS[p], lax.div(i, 4), line, lax.rem(i, 4))
            first_block = ((at[0] * 4 + at[1]) * 4 + at[2]) * 4
            for blk in range(row // HALF, (row + rows - 1) // HALF + 1):
                low, high = max(row, blk * HALF), min(row + rows, blk * HALF + HALF)
                span = pl.ds(low - blk * HALF, high - low)
                b = first_block + blk
                acc[(*at[:3], pl.ds(low, high - low), slice(None))] = (
                    own[tables[2, b], span, :] + sib[tables[3, b], span, :]
                )
            return carry

        lax.fori_loop(0, 16, one, 0)

    def push(source, target, slot, axis, k):
        return pltpu.make_async_remote_copy(
            src_ref=acc.at[source], dst_ref=target, send_sem=send.at[slot], recv_sem=recv.at[slot],
            device_id={AXES[axis]: hop(here[axis], k)}, device_id_type=MESH,
        )

    def go(op):
        op.start()
        started.append(op)

    def third(p, sub, way, k):
        line, t = hop(coords(p)[1], LINES[sub]), coords(p)[2]
        half = 1 - way if k == 1 else way
        source = cell(PARTS[p], two(half), line, hop(t, 2 if k == 0 else NEAR[way]))
        target = across2[p].at[sub, way] if k == 0 else near2[p].at[sub, way, two(half)]
        slot = 27 + ((p * 4 + sub) * 2 + way) * 3 + k
        return push(source, target, slot, PARTS[p][0][2], NEAR[way])

    def second(p, way, k):
        _, b, t = coords(p)
        half = 1 - way if k == 1 else way
        source = cell(PARTS[p], two(half), hop(b, 2 if k == 0 else NEAR[way]), t)
        target = across1[p].at[way] if k == 0 else near1[p].at[way, two(half)]
        return push(source, target, 9 + (p * 2 + way) * 3 + k, PARTS[p][0][1], NEAR[way])

    def first(p, way):
        a, b, t = coords(p)
        source = cell(PARTS[p], hop(a, NEAR[way]), b, t)
        return push(source, near0[p].at[way], p * 3 + way, PARTS[p][0][0], NEAR[way])

    def add(at, *terms):
        total = acc[at].astype(jnp.float32)
        for term in terms:
            total = total + term.astype(jnp.float32)
        acc[at] = total.astype(jnp.bfloat16)

    def send_line(p, sub):
        spread(p, sub)
        for k in range(2):
            for way in range(2):
                go(third(p, sub, way, k))

    def pass_line(p, sub):
        line, t = hop(coords(p)[1], LINES[sub]), coords(p)[2]
        for way in range(2):
            third(p, sub, way, 0).wait_recv()
            for i in range(2):
                add(
                    cell(PARTS[p], 2 * way + i, line, hop(t, NEAR[way])),
                    across2[p][sub, way, i],
                )
            go(third(p, sub, way, 2))

    def finish_line(p, sub):
        line, t = hop(coords(p)[1], LINES[sub]), coords(p)[2]
        for way in range(2):
            third(p, sub, way, 1).wait_recv()
            third(p, sub, way, 2).wait_recv()
        for i in range(4):
            add(cell(PARTS[p], i, line, t), near2[p][sub, 0, i], near2[p][sub, 1, i])

    for p in parts:
        send_line(p, 3)
    for p in parts:
        send_line(p, 1)
    for p in parts:
        pass_line(p, 3)
        send_line(p, 2)
    for p in parts:
        pass_line(p, 1)
        send_line(p, 0)
    for p in parts:
        finish_line(p, 3)
        for way in range(2):
            go(second(p, way, 0))
    for p in parts:
        pass_line(p, 2)
    for p in parts:
        pass_line(p, 0)
    for p in parts:
        finish_line(p, 1)
        finish_line(p, 2)
        for way in range(2):
            go(second(p, way, 1))
    for p in parts:
        _, b, t = coords(p)
        for way in range(2):
            second(p, way, 0).wait_recv()
            for i in range(2):
                add(cell(PARTS[p], 2 * way + i, hop(b, NEAR[way]), t), across1[p][way, i])
            go(second(p, way, 2))
    for p in parts:
        finish_line(p, 0)
    for p in parts:
        _, b, t = coords(p)
        for way in range(2):
            second(p, way, 1).wait_recv()
            second(p, way, 2).wait_recv()
        for i in range(4):
            add(cell(PARTS[p], i, b, t), near1[p][0, i], near1[p][1, i])
        for way in (2, 0, 1):
            go(first(p, way))
    for p in parts:
        for way in range(3):
            first(p, way).wait_recv()
        add(cell(PARTS[p], *coords(p)), *(near0[p][way] for way in range(3)))

    total = acc[y, z, x]
    grad[...] = jnp.where(mask[...] > 0, total, jnp.zeros_like(total))

    def columns(k):
        return grad.at[pl.ds(pl.multiple_of(k * DOCS, 16), DOCS), :]

    def pair_grad(k, core):
        return pltpu.make_async_remote_copy(
            src_ref=columns(k), dst_ref=mine_grad.at[core],
            send_sem=pair_sem.at[3], recv_sem=pair_sem.at[4],
            device_id=sibling, device_id_type=MESH,
        )

    to_other = pair_grad(1 - c, c)
    to_other.start()
    kept = pltpu.make_async_copy(columns(c), mine_grad.at[c], pair_sem.at[5])
    kept.start()
    kept.wait()
    pair_grad(c, 1 - c).wait_recv()
    sides = [
        jnp.concatenate([mine_grad[half, pl.ds(j * HALF, HALF), :] for half in range(2)], axis=0)
        for j in range(2)
    ]
    right = jnp.concatenate(sides, axis=1)

    def out_columns(l):
        return out_ref.at[:, pl.ds(pl.multiple_of(l * 256, 256), 256)]

    def out_copy(to, origin):
        return pltpu.make_async_remote_copy(
            src_ref=pieces.at[to], dst_ref=out_columns(origin),
            send_sem=o_send.at[to], recv_sem=o_recv.at[origin],
            device_id=label_peer(to), device_id_type=MESH,
        )

    own_out = pltpu.make_async_copy(pieces.at[me], out_columns(me), pair_sem.at[6])
    for k in range(4):
        row = hop(z, k) * 8
        left = docs_ref[pl.ds(hop(z, k) * 4, 4)].reshape(256, 256)[:, :DOCS]
        pieces[pl.ds(row, 8)] = jnp.dot(
            left, right, preferred_element_type=jnp.float32
        ).astype(jnp.bfloat16).reshape(8, 32, 256)

        def deliver(o, carry):
            out_copy(row + lax.rem(x * 2 + c + o, 8), me).start()
            return carry

        lax.fori_loop(1 if k == 0 else 0, 8, deliver, 0)
        if k == 0:
            own_out.start()
    own_out.wait()

    def collect(o, carry):
        other = lax.rem(me + o, 32)
        out_copy(other, other).wait_recv()
        return carry

    def drain(o, carry):
        out_copy(lax.rem(me + o, 32), me).wait_send()
        return carry

    lax.fori_loop(1, 32, collect, 0)
    to_other.wait_send()
    for op in started:
        op.wait_send()
    lax.fori_loop(1, 32, drain, 0)


def reduce_blocks(tables, gp, mask, docs_all):
    received = [
        pltpu.VMEM((*lead, rows, BLK), jnp.bfloat16)
        for lead in ((4, 2, 2), (4, 2, 4), (2, 2), (2, 4), (3,))
        for _, _, rows in PARTS
    ]
    return pl.pallas_call(
        reduce_kernel,
        out_shape=jax.ShapeDtypeStruct((32, 8192), jnp.bfloat16),
        in_specs=[
            pl.BlockSpec(memory_space=pltpu.SMEM),
            pl.BlockSpec(memory_space=pl.ANY),
            pl.BlockSpec(memory_space=pltpu.VMEM),
            pl.BlockSpec(memory_space=pltpu.VMEM),
        ],
        out_specs=pl.BlockSpec(memory_space=pltpu.VMEM),
        scratch_shapes=[
            pltpu.VMEM((POOL + 1, HALF, BLK), jnp.bfloat16),
            pltpu.VMEM((POOL + 1, HALF, BLK), jnp.bfloat16),
            pltpu.VMEM((4, 4, 4, SHARD, BLK), jnp.bfloat16),
            pltpu.VMEM((SHARD, BLK), jnp.bfloat16),
            pltpu.VMEM((2, DOCS, BLK), jnp.bfloat16),
            pltpu.VMEM((32, 32, 256), jnp.bfloat16),
            *received,
            pltpu.SemaphoreType.DMA((7,)),
            pltpu.SemaphoreType.DMA((99,)),
            pltpu.SemaphoreType.DMA((99,)),
            pltpu.SemaphoreType.DMA((32,)),
            pltpu.SemaphoreType.DMA((32,)),
        ],
        compiler_params=pltpu.CompilerParams(
            collective_id=1, has_side_effects=True, vmem_limit_bytes=24 * MIB
        ),
        name="reduce_blocks",
    )(tables, gp, mask, docs_all)


def on_device(documents, expand_weight, sparse_weight, feature_lists, positives):
    core = lax.axis_index("label_2")
    group = lax.axis_index(AXES)
    pair = lax.dynamic_slice_in_dim(feature_lists, (group - core) * LBLK_DEV, 2 * LBLK_DEV, 0)
    pair = pair.reshape(2, LBLK_DEV * SLOTS)
    keys = jnp.where(core == 0, pair, pair[::-1]) * 512
    keys = jnp.pad(keys + jnp.arange(LBLK_DEV * SLOTS, dtype=jnp.int32)[None, :], ((0, 6), (0, 0)))
    weight = pltpu.with_memory_space_constraint(expand_weight, pltpu.HBM)
    docs_t = pltpu.with_memory_space_constraint(documents.T, pltpu.HBM)
    hid, docs_all, mask, tables = expand(keys, docs_t, weight)
    grad_sparse, gp = label_blocks(
        tables,
        (group * LBLK_DEV).astype(jnp.int32).reshape(1),
        pltpu.with_memory_space_constraint(positives.T, pltpu.HBM),
        hid.reshape(FBLOCKS, DOCS, BLK),
        sparse_weight,
    )
    grad_expand = reduce_blocks(tables, gp, mask, docs_all)
    return (grad_expand, grad_sparse)


def solution(mesh):
    finer = Mesh(mesh.devices.reshape(mesh.shape["feat"], 4, 4, 2), AXES)
    return jax.shard_map(
        on_device,
        mesh=finer,
        in_specs=(P(None, LABEL), P(LABEL, "feat"), P(AXES, None, None, None), P(), P()),
        out_specs=(P(LABEL, "feat"), P(AXES, None, None, None)),
        check_vma=False,
    )
```

```python
import functools

import jax
import jax.numpy as jnp
from jax import lax
from jax.experimental import pallas as pl
from jax.experimental.pallas import tpu as pltpu
from jax.sharding import Mesh
from jax.sharding import PartitionSpec as P

BLK = 128
FBLOCKS = 256
SLOTS = 16
LBLK_DEV = 24
POOL = 96
STEP = 4
STEPS = 6
SPAN = 16
NAMED = 4
POS = 8
DOCS = 160
HALF = 80
SHARD = 320
RING = 4
AXES = ("feat", "label_0", "label_1", "label_2")
LABEL = AXES[1:]
MESH = pl.DeviceIdType.MESH
MIB = 1 << 20

PARTS = (((2, 0, 1), 0, 112), ((0, 1, 2), 112, 112), ((1, 2, 0), 224, 96))
NEAR, BACK = (1, 3, 2), (3, 1, 2)
LINES = (0, 3, 1, 2)


def hop(m, k):
    return lax.rem(m + k, RING)


def label_peer(l):
    return {
        "label_0": lax.div(l, 8),
        "label_1": lax.rem(lax.div(l, 2), 4),
        "label_2": lax.rem(l, 2),
    }


def cell(part, ta, tb, tc, lead=()):
    order, row, rows = part
    index = [None] * 3
    for axis, t in zip(order, (ta, tb, tc)):
        index[axis] = t
    return (*index, *lead, pl.ds(row, rows), slice(None))


def two(half):
    return pl.ds(2 * half, 2)


def rank_tables(keys, tables_ref):
    count = LBLK_DEV * SLOTS
    turned = keys.T
    tables_ref[...] = jnp.zeros((8, count), jnp.int32)
    lanes = lax.broadcasted_iota(jnp.int32, (count, count), 1)
    for r in range(2):
        row, col = keys[r : r + 1, :], turned[:, r : r + 1]
        below = jnp.sum(jnp.where(row < col, 1.0, 0.0), axis=1, keepdims=True).astype(jnp.int32)
        if r == 0:
            sort = jnp.where(below == lanes, col.astype(jnp.float32), 0.0)
            tables_ref[0:1, :] = jnp.sum(sort, axis=0, keepdims=True).astype(jnp.int32)
            above = jnp.sum(jnp.where(col < row, 1.0, 0.0), axis=0, keepdims=True)
            tables_ref[1:2, :] = lax.shift_right_logical(above.astype(jnp.int32), 2)
            tables_ref[4:5, :] = lax.shift_right_logical(row, 9)
        place = lax.shift_right_logical(below, 2)
        first = jnp.where(place * NAMED == below, place - POOL, 0).astype(jnp.float32)
        hit = lax.shift_right_logical(col, 9) == lanes[:, :FBLOCKS]
        table = jnp.sum(jnp.where(hit, first, 0.0), axis=0, keepdims=True)
        tables_ref[2 + r : 3 + r, 0:FBLOCKS] = table.astype(jnp.int32) + POOL


def expand_kernel(
    keys_ref, docs_in, weight_ref, hid_ref, docs_all, mask_ref, tables_ref, docs_small, docs_ref, w_all, shard,
    w_send, w_recv, d_send, d_recv, own_sem, send, recv, sib_send, sib_recv,
):
    y, z, x, c = (lax.axis_index(a) for a in AXES)
    here = (y, z, x)
    me = z * 8 + x * 2 + c
    sibling = {"label_2": 1 - c}
    peer = label_peer
    load = pltpu.make_async_copy(docs_in, docs_small, own_sem.at[9])
    load.start()
    barrier = pltpu.get_barrier_semaphore()

    def greet(o, carry):
        pl.semaphore_signal(
            barrier, inc=1, device_id=peer(lax.rem(me + o, 32)), device_id_type=MESH
        )
        return carry

    lax.fori_loop(1, 32, greet, 0)
    for k in (1, 2, 3):
        pl.semaphore_signal(barrier, inc=1, device_id={"feat": hop(y, k)}, device_id_type=MESH)
    load.wait()
    docs_ref[:, 0:DOCS] = docs_small[...]
    docs_ref[:, DOCS:] = jnp.zeros((32, 256 - DOCS), jnp.bfloat16)
    pl.semaphore_wait(barrier, 34)

    def rows_of(ref, l):
        return ref.at[lax.div(l, 2), lax.rem(l, 2)]

    def columns_for(l):
        return weight_ref.at[:, pl.ds(pl.multiple_of(l * 256, 256), 256)]

    def docs_copy(to, origin):
        return pltpu.make_async_remote_copy(
            src_ref=docs_ref, dst_ref=rows_of(docs_all, origin),
            send_sem=d_send.at[to], recv_sem=d_recv.at[origin],
            device_id=peer(to), device_id_type=MESH,
        )

    def docs_pair(core):
        return pltpu.make_async_remote_copy(
            src_ref=docs_all.at[:, core], dst_ref=docs_all.at[:, core],
            send_sem=own_sem.at[3], recv_sem=own_sem.at[4],
            device_id=sibling, device_id_type=MESH,
        )

    def weight_copy(to, origin):
        return pltpu.make_async_remote_copy(
            src_ref=columns_for(to), dst_ref=rows_of(w_all, origin),
            send_sem=w_send.at[to], recv_sem=w_recv.at[origin],
            device_id=peer(to), device_id_type=MESH,
        )

    def same_core(o):
        return lax.rem(me + 2 * o, 32)

    def start_docs(o, carry):
        docs_copy(same_core(o), me).start()
        return carry

    def start_weight(o, carry):
        weight_copy(lax.rem(me + o, 32), me).start()
        return carry

    lax.fori_loop(1, 16, start_docs, 0)
    lax.fori_loop(1, 32, start_weight, 0)
    own_docs = pltpu.make_async_copy(docs_ref, rows_of(docs_all, me), own_sem.at[0])
    own_weight = pltpu.make_async_copy(columns_for(me), rows_of(w_all, me), own_sem.at[1])
    own_docs.start()
    own_weight.start()
    rank_tables(keys_ref[...], tables_ref)
    own_docs.wait()
    own_weight.wait()

    def finish_docs(o, carry):
        docs_copy(same_core(o), same_core(o)).wait_recv()
        return carry

    def finish_weight(o, carry):
        other = lax.rem(me + o, 32)
        weight_copy(other, other).wait_recv()
        return carry

    lax.fori_loop(1, 16, finish_docs, 0)
    docs_pair(c).start()
    lax.fori_loop(1, 32, finish_weight, 0)
    docs_pair(1 - c).wait_recv()
    product = lax.dot_general(
        docs_all[...].reshape(1024, 256), w_all[...].reshape(1024, 256),
        (((0,), (0,)), ((), ())), preferred_element_type=jnp.float32,
    )
    hidden = jnp.maximum(product, 0.0).astype(jnp.bfloat16)
    shard[0:DOCS, :] = hidden[:DOCS, :BLK]
    shard[DOCS:SHARD, :] = hidden[:DOCS, BLK:]
    own_hidden = pltpu.make_async_copy(shard, hid_ref.at[y, z, x, c], own_sem.at[2])
    own_hidden.start()

    started = []

    def copy(at, slot, axis, k, source=None):
        return pltpu.make_async_remote_copy(
            src_ref=hid_ref.at[at] if source is None else source,
            dst_ref=hid_ref.at[at],
            send_sem=send.at[slot],
            recv_sem=recv.at[slot],
            device_id={AXES[axis]: hop(here[axis], k)},
            device_id_type=MESH,
        )

    def go(op):
        op.start()
        started.append(op)

    def coords(p):
        return tuple(here[axis] for axis in PARTS[p][0])

    def first(p, way, origin, source=None):
        a, b, t = coords(p)
        return copy(
            cell(PARTS[p], origin, b, t, (c,)), p * 3 + way, PARTS[p][0][0], NEAR[way], source
        )

    def second(p, way, k, line, half):
        t = coords(p)[2]
        at = cell(PARTS[p], two(half), line, t, (c,))
        return copy(at, 9 + (p * 2 + way) * 3 + k, PARTS[p][0][1], NEAR[way])

    def third(p, sub, way, k, t, half):
        line = hop(coords(p)[1], LINES[sub])
        at = cell(PARTS[p], two(half), line, t, (c,))
        return copy(at, 27 + ((p * 4 + sub) * 2 + way) * 3 + k, PARTS[p][0][2], NEAR[way])

    def pair_copy(p, k, at):
        return pltpu.make_async_remote_copy(
            src_ref=hid_ref.at[at], dst_ref=hid_ref.at[at],
            send_sem=sib_send.at[p * 13 + k], recv_sem=sib_recv.at[p * 13 + k],
            device_id=sibling, device_id_type=MESH,
        )

    def pair_plane(p, core):
        return pair_copy(p, 0, cell(PARTS[p], slice(None), slice(None), coords(p)[2], (core,)))

    def pair_line(p, sub, way, core):
        _, b, t = coords(p)
        at = cell(PARTS[p], slice(None), hop(b, LINES[sub]), hop(t, BACK[way]), (core,))
        return pair_copy(p, 1 + sub * 3 + way, at)

    def send_line(p, sub):
        for k in range(2):
            for way in range(2):
                go(third(p, sub, way, k, coords(p)[2], way if k == 0 else 1 - way))

    def pass_line(p, sub):
        for way in range(2):
            near = hop(coords(p)[2], BACK[way])
            third(p, sub, way, 0, near, way).wait_recv()
            go(third(p, sub, way, 2, near, way))

    def finish_line(p, sub):
        for way in range(2):
            third(p, sub, way, 1, hop(coords(p)[2], BACK[way]), 1 - way).wait_recv()
            go(pair_line(p, sub, way, c))
        for way in range(2):
            third(p, sub, way, 2, hop(coords(p)[2], 2), way).wait_recv()
        go(pair_line(p, sub, 2, c))

    parts = range(3)
    for way in (2, 0, 1):
        for p in parts:
            _, row, rows = PARTS[p]
            go(first(p, way, coords(p)[0], shard.at[pl.ds(row, rows), :]))
    own_hidden.wait()
    for p in parts:
        a, b, t = coords(p)
        for way in range(3):
            first(p, way, hop(a, BACK[way])).wait_recv()
        for k in range(2):
            for way in range(2):
                go(second(p, way, k, b, way if k == 0 else 1 - way))
        send_line(p, 0)
    for p in parts:
        b = coords(p)[1]
        for way in range(2):
            near = hop(b, BACK[way])
            second(p, way, 0, near, way).wait_recv()
            go(second(p, way, 2, near, way))
    for p in parts:
        pass_line(p, 0)
    for p in parts:
        b = coords(p)[1]
        for way in range(2):
            second(p, way, 1, hop(b, BACK[way]), 1 - way).wait_recv()
            send_line(p, 1 + way)
    for p in parts:
        for way in range(2):
            second(p, way, 2, hop(coords(p)[1], 2), way).wait_recv()
        send_line(p, 3)
        go(pair_plane(p, c))
    for sub in (1, 2):
        for p in parts:
            pass_line(p, sub)
    for p in parts:
        finish_line(p, 0)
    for p in parts:
        pass_line(p, 3)
    for sub in (1, 2, 3):
        for p in parts:
            finish_line(p, sub)
    for p in parts:
        pair_plane(p, 1 - c).wait_recv()
    for blk in range(4):
        op = pltpu.make_async_copy(
            hid_ref.at[
                y, z, x, blk // 2,
                pl.ds(pl.multiple_of(blk % 2 * DOCS + c * HALF, 16), HALF), slice(None),
            ],
            mask_ref.at[pl.ds(blk * HALF, HALF), :],
            own_sem.at[5 + blk],
        )
        op.start()
    for p in parts:
        for sub in range(4):
            for way in range(3):
                pair_line(p, sub, way, 1 - c).wait_recv()
    for op in started:
        op.wait_send()
    for blk in range(4):
        pltpu.make_async_copy(
            mask_ref.at[pl.ds(blk * HALF, HALF), :], mask_ref.at[pl.ds(blk * HALF, HALF), :], own_sem.at[5 + blk]
        ).wait()
    docs_pair(c).wait_send()
    def drain_docs(o, carry):
        docs_copy(same_core(o), me).wait_send()
        return carry

    def drain_weight(o, carry):
        weight_copy(lax.rem(me + o, 32), me).wait_send()
        return carry

    lax.fori_loop(1, 16, drain_docs, 0)
    lax.fori_loop(1, 32, drain_weight, 0)


def expand(keys, docs_t, expand_weight):
    vmem = pl.BlockSpec(memory_space=pltpu.VMEM)
    return pl.pallas_call(
        expand_kernel,
        out_shape=(
            jax.ShapeDtypeStruct((4, 4, 4, 2, SHARD, BLK), jnp.bfloat16),
            jax.ShapeDtypeStruct((16, 2, 32, 256), jnp.bfloat16),
            jax.ShapeDtypeStruct((SHARD, BLK), jnp.bfloat16),
            jax.ShapeDtypeStruct((8, LBLK_DEV * SLOTS), jnp.int32),
        ),
        in_specs=[vmem, pl.BlockSpec(memory_space=pl.ANY), pl.BlockSpec(memory_space=pl.ANY)],
        out_specs=(pl.BlockSpec(memory_space=pl.ANY), vmem, vmem, vmem),
        scratch_shapes=[
            pltpu.VMEM((32, DOCS), jnp.bfloat16),
            pltpu.VMEM((32, 256), jnp.bfloat16),
            pltpu.VMEM((16, 2, 32, 256), jnp.bfloat16),
            pltpu.VMEM((SHARD, BLK), jnp.bfloat16),
            pltpu.SemaphoreType.DMA((32,)),
            pltpu.SemaphoreType.DMA((32,)),
            pltpu.SemaphoreType.DMA((32,)),
            pltpu.SemaphoreType.DMA((32,)),
            pltpu.SemaphoreType.DMA((10,)),
            pltpu.SemaphoreType.DMA((99,)),
            pltpu.SemaphoreType.DMA((99,)),
            pltpu.SemaphoreType.DMA((39,)),
            pltpu.SemaphoreType.DMA((39,)),
        ],
        compiler_params=pltpu.CompilerParams(
            collective_id=0, has_side_effects=True, vmem_limit_bytes=36 * MIB
        ),
        name="expand",
    )(keys, docs_t, expand_weight)


def label_kernel(
    tables, base, pos_ref, hid, weight_ref, gs_ref, gp_ref, h_t, w, res, pos_b, gp, w_sem, gp_sem,
):
    step = pl.program_id(0)

    def weight_copy(k):
        part = pl.ds(k * STEP, STEP)
        return pltpu.make_async_copy(weight_ref.at[part], w.at[part], w_sem.at[k])

    def gp_copy(k):
        part = pl.ds(k * SPAN, SPAN)
        return pltpu.make_async_copy(gp.at[part], gp_ref.at[part], gp_sem.at[k])

    @pl.when(step == 0)
    def _():
        for k in range(STEPS):
            weight_copy(k).start()
        turned = pos_ref[...].T
        for k in range(POS):
            pos_b[k] = jnp.broadcast_to(turned[:, k : k + 1], (DOCS, BLK))

    def listed(place):
        return hid[lax.div(tables[0, place * NAMED], 512)]

    @pl.when(step < STEPS)
    def _():
        weight_copy(step).wait()
        for k in range(STEP):
            q = step * STEP + k
            logits = jnp.zeros((DOCS, BLK), jnp.float32)
            for s in range(0, SLOTS, 2):
                left = jnp.concatenate(
                    [hid[tables[4, q * SLOTS + s + i]] for i in range(2)], axis=1
                )
                right = w[q, s : s + 2].reshape(2 * BLK, BLK)
                logits += jnp.dot(left, right, preferred_element_type=jnp.float32)
            ids = (base[0] + q) * BLK + lax.broadcasted_iota(jnp.int32, (DOCS, BLK), 1)
            hit = pos_b[0] == ids
            for i in range(1, POS):
                hit = jnp.logical_or(hit, pos_b[i] == ids)
            res[q] = (jax.nn.sigmoid(logits) - jnp.where(hit, 1.0, 0.0)).astype(jnp.bfloat16)
        for k in range(SPAN):
            place = step * SPAN + k
            h_t[place] = listed(place).T

    @pl.when(step >= STEPS)
    def _():
        late = step - STEPS
        for k in range(STEP):
            q = late * STEP + k
            residual = res[q]
            for s in range(SLOTS):
                gs_ref[k, s] = jnp.dot(
                    h_t[tables[1, q * SLOTS + s]], residual, preferred_element_type=jnp.float32
                ).astype(jnp.bfloat16)
        for k in range(SPAN):
            place = late * SPAN + k
            slots = [lax.rem(tables[0, place * NAMED + i], 512) for i in range(NAMED)]
            pairs = [(lax.div(i, SLOTS), lax.rem(i, SLOTS)) for i in slots]
            left = jnp.concatenate([res[q] for q, _ in pairs], axis=1)
            right = jnp.concatenate([w[q, s] for q, s in pairs], axis=1)
            gp[place] = lax.dot_general(
                left, right, (((1,), (1,)), ((), ())), preferred_element_type=jnp.float32
            ).astype(jnp.bfloat16)
        gp_copy(late).start()

    @pl.when(step == 2 * STEPS - 1)
    def _():
        for k in range(STEPS):
            gp_copy(k).wait()


def label_blocks(tables, base, positives, hid, sparse_weight):
    return pl.pallas_call(
        label_kernel,
        out_shape=(
            jax.ShapeDtypeStruct((LBLK_DEV, SLOTS, BLK, BLK), jnp.bfloat16),
            jax.ShapeDtypeStruct((POOL, DOCS, BLK), jnp.bfloat16),
        ),
        grid_spec=pltpu.PrefetchScalarGridSpec(
            num_scalar_prefetch=2,
            grid=(2 * STEPS,),
            in_specs=[
                pl.BlockSpec((POS, DOCS), lambda g, *_: (0, 0)),
                pl.BlockSpec(memory_space=pltpu.VMEM),
                pl.BlockSpec(memory_space=pl.ANY),
            ],
            out_specs=(
                pl.BlockSpec(
                    (STEP, SLOTS, BLK, BLK), lambda g, *_: (jnp.maximum(g - STEPS, 0), 0, 0, 0)
                ),
                pl.BlockSpec(memory_space=pl.ANY),
            ),
            scratch_shapes=[
                pltpu.VMEM((POOL, BLK, DOCS), jnp.bfloat16),
                pltpu.VMEM((LBLK_DEV, SLOTS, BLK, BLK), jnp.bfloat16),
                pltpu.VMEM((LBLK_DEV, DOCS, BLK), jnp.bfloat16),
                pltpu.VMEM((POS, DOCS, BLK), jnp.int32),
                pltpu.VMEM((POOL, DOCS, BLK), jnp.bfloat16),
                pltpu.SemaphoreType.DMA((STEPS,)),
                pltpu.SemaphoreType.DMA((STEPS,)),
            ],
        ),
        compiler_params=pltpu.CompilerParams(
            dimension_semantics=("arbitrary",), vmem_limit_bytes=36 * MIB
        ),
        name="label_blocks",
    )(tables, base, positives, hid, sparse_weight)


def reduce_kernel(
    tables, gp_ref, mask, docs_ref, out_ref,
    own, sib, acc, grad, mine_grad, pieces, *rest,
):
    across2, near2, across1, near1, near0 = (rest[k * 3 : k * 3 + 3] for k in range(5))
    pair_sem, send, recv, o_send, o_recv = rest[15:]
    y, z, x, c = (lax.axis_index(a) for a in AXES)
    here = (y, z, x)
    sibling = {"label_2": 1 - c}
    me = z * 8 + x * 2 + c
    barrier = pltpu.get_barrier_semaphore()

    for axis, m in zip(AXES, here):
        for k in (1, 3):
            pl.semaphore_signal(barrier, inc=1, device_id={axis: hop(m, k)}, device_id_type=MESH)
    pl.semaphore_signal(barrier, inc=1, device_id=sibling, device_id_type=MESH)

    def docs_half(k):
        return gp_ref.at[:, pl.ds(pl.multiple_of(k * HALF, 16), HALF), :]

    to_pair = pltpu.make_async_remote_copy(
        src_ref=docs_half(1 - c), dst_ref=sib.at[pl.ds(0, POOL)],
        send_sem=pair_sem.at[0], recv_sem=pair_sem.at[1],
        device_id=sibling, device_id_type=MESH,
    )
    mine = pltpu.make_async_copy(docs_half(c), own.at[pl.ds(0, POOL)], pair_sem.at[2])
    mine.start()
    own[POOL] = jnp.zeros((HALF, BLK), jnp.bfloat16)
    sib[POOL] = jnp.zeros((HALF, BLK), jnp.bfloat16)
    pl.semaphore_wait(barrier, 7)
    to_pair.start()
    mine.wait()
    to_pair.wait_recv()

    parts = range(3)
    started = []

    def coords(p):
        return tuple(here[axis] for axis in PARTS[p][0])

    def spread(p, sub):
        order, row, rows = PARTS[p]
        line = hop(coords(p)[1], LINES[sub])

        def one(i, carry):
            at = cell(PARTS[p], lax.div(i, 4), line, lax.rem(i, 4))
            first_block = ((at[0] * 4 + at[1]) * 4 + at[2]) * 4
            for blk in range(row // HALF, (row + rows - 1) // HALF + 1):
                low, high = max(row, blk * HALF), min(row + rows, blk * HALF + HALF)
                span = pl.ds(low - blk * HALF, high - low)
                b = first_block + blk
                acc[(*at[:3], pl.ds(low, high - low), slice(None))] = (
                    own[tables[2, b], span, :] + sib[tables[3, b], span, :]
                )
            return carry

        lax.fori_loop(0, 16, one, 0)

    def push(source, target, slot, axis, k):
        return pltpu.make_async_remote_copy(
            src_ref=acc.at[source], dst_ref=target, send_sem=send.at[slot], recv_sem=recv.at[slot],
            device_id={AXES[axis]: hop(here[axis], k)}, device_id_type=MESH,
        )

    def go(op):
        op.start()
        started.append(op)

    def third(p, sub, way, k):
        line, t = hop(coords(p)[1], LINES[sub]), coords(p)[2]
        half = 1 - way if k == 1 else way
        source = cell(PARTS[p], two(half), line, hop(t, 2 if k == 0 else NEAR[way]))
        target = across2[p].at[sub, way] if k == 0 else near2[p].at[sub, way, two(half)]
        slot = 27 + ((p * 4 + sub) * 2 + way) * 3 + k
        return push(source, target, slot, PARTS[p][0][2], NEAR[way])

    def second(p, way, k):
        _, b, t = coords(p)
        half = 1 - way if k == 1 else way
        source = cell(PARTS[p], two(half), hop(b, 2 if k == 0 else NEAR[way]), t)
        target = across1[p].at[way] if k == 0 else near1[p].at[way, two(half)]
        return push(source, target, 9 + (p * 2 + way) * 3 + k, PARTS[p][0][1], NEAR[way])

    def first(p, way):
        a, b, t = coords(p)
        source = cell(PARTS[p], hop(a, NEAR[way]), b, t)
        return push(source, near0[p].at[way], p * 3 + way, PARTS[p][0][0], NEAR[way])

    def add(at, *terms):
        total = acc[at].astype(jnp.float32)
        for term in terms:
            total = total + term.astype(jnp.float32)
        acc[at] = total.astype(jnp.bfloat16)

    def send_line(p, sub):
        spread(p, sub)
        for k in range(2):
            for way in range(2):
                go(third(p, sub, way, k))

    def pass_line(p, sub):
        line, t = hop(coords(p)[1], LINES[sub]), coords(p)[2]
        for way in range(2):
            third(p, sub, way, 0).wait_recv()
            for i in range(2):
                add(
                    cell(PARTS[p], 2 * way + i, line, hop(t, NEAR[way])),
                    across2[p][sub, way, i],
                )
            go(third(p, sub, way, 2))

    def finish_line(p, sub):
        line, t = hop(coords(p)[1], LINES[sub]), coords(p)[2]
        for way in range(2):
            third(p, sub, way, 1).wait_recv()
            third(p, sub, way, 2).wait_recv()
        for i in range(4):
            add(cell(PARTS[p], i, line, t), near2[p][sub, 0, i], near2[p][sub, 1, i])

    for p in parts:
        send_line(p, 3)
    for p in parts:
        send_line(p, 1)
    for p in parts:
        pass_line(p, 3)
        send_line(p, 2)
    for p in parts:
        pass_line(p, 1)
        send_line(p, 0)
    for p in parts:
        finish_line(p, 3)
        for way in range(2):
            go(second(p, way, 0))
    for p in parts:
        pass_line(p, 2)
    for p in parts:
        pass_line(p, 0)
    for p in parts:
        finish_line(p, 1)
        finish_line(p, 2)
        for way in range(2):
            go(second(p, way, 1))
    for p in parts:
        _, b, t = coords(p)
        for way in range(2):
            second(p, way, 0).wait_recv()
            for i in range(2):
                add(cell(PARTS[p], 2 * way + i, hop(b, NEAR[way]), t), across1[p][way, i])
            go(second(p, way, 2))
    for p in parts:
        finish_line(p, 0)
    for p in parts:
        _, b, t = coords(p)
        for way in range(2):
            second(p, way, 1).wait_recv()
            second(p, way, 2).wait_recv()
        for i in range(4):
            add(cell(PARTS[p], i, b, t), near1[p][0, i], near1[p][1, i])
        for way in (2, 0, 1):
            go(first(p, way))
    for p in parts:
        for way in range(3):
            first(p, way).wait_recv()
        add(cell(PARTS[p], *coords(p)), *(near0[p][way] for way in range(3)))

    total = acc[y, z, x]
    grad[...] = jnp.where(mask[...] > 0, total, jnp.zeros_like(total))

    def columns(k):
        return grad.at[pl.ds(pl.multiple_of(k * DOCS, 16), DOCS), :]

    def pair_grad(k, core):
        return pltpu.make_async_remote_copy(
            src_ref=columns(k), dst_ref=mine_grad.at[core],
            send_sem=pair_sem.at[3], recv_sem=pair_sem.at[4],
            device_id=sibling, device_id_type=MESH,
        )

    to_other = pair_grad(1 - c, c)
    to_other.start()
    kept = pltpu.make_async_copy(columns(c), mine_grad.at[c], pair_sem.at[5])
    kept.start()
    kept.wait()
    pair_grad(c, 1 - c).wait_recv()
    sides = [
        jnp.concatenate([mine_grad[half, pl.ds(j * HALF, HALF), :] for half in range(2)], axis=0)
        for j in range(2)
    ]
    right = jnp.concatenate(sides, axis=1)

    def out_columns(l):
        return out_ref.at[:, pl.ds(pl.multiple_of(l * 256, 256), 256)]

    def out_copy(to, origin):
        return pltpu.make_async_remote_copy(
            src_ref=pieces.at[to], dst_ref=out_columns(origin),
            send_sem=o_send.at[to], recv_sem=o_recv.at[origin],
            device_id=label_peer(to), device_id_type=MESH,
        )

    own_out = pltpu.make_async_copy(pieces.at[me], out_columns(me), pair_sem.at[6])
    for k in range(4):
        row = hop(z, k) * 8
        left = docs_ref[pl.ds(hop(z, k) * 4, 4)].reshape(256, 256)[:, :DOCS]
        pieces[pl.ds(row, 8)] = jnp.dot(
            left, right, preferred_element_type=jnp.float32
        ).astype(jnp.bfloat16).reshape(8, 32, 256)

        def deliver(o, carry):
            out_copy(row + lax.rem(x * 2 + c + o, 8), me).start()
            return carry

        lax.fori_loop(1 if k == 0 else 0, 8, deliver, 0)
        if k == 0:
            own_out.start()
    own_out.wait()

    def collect(o, carry):
        other = lax.rem(me + o, 32)
        out_copy(other, other).wait_recv()
        return carry

    def drain(o, carry):
        out_copy(lax.rem(me + o, 32), me).wait_send()
        return carry

    lax.fori_loop(1, 32, collect, 0)
    to_pair.wait_send()
    to_other.wait_send()
    for op in started:
        op.wait_send()
    lax.fori_loop(1, 32, drain, 0)


def reduce_blocks(tables, gp, mask, docs_all):
    received = [
        pltpu.VMEM((*lead, rows, BLK), jnp.bfloat16)
        for lead in ((4, 2, 2), (4, 2, 4), (2, 2), (2, 4), (3,))
        for _, _, rows in PARTS
    ]
    return pl.pallas_call(
        reduce_kernel,
        out_shape=jax.ShapeDtypeStruct((32, 8192), jnp.bfloat16),
        in_specs=[
            pl.BlockSpec(memory_space=pltpu.SMEM),
            pl.BlockSpec(memory_space=pl.ANY),
            pl.BlockSpec(memory_space=pltpu.VMEM),
            pl.BlockSpec(memory_space=pltpu.VMEM),
        ],
        out_specs=pl.BlockSpec(memory_space=pltpu.VMEM),
        scratch_shapes=[
            pltpu.VMEM((POOL + 1, HALF, BLK), jnp.bfloat16),
            pltpu.VMEM((POOL + 1, HALF, BLK), jnp.bfloat16),
            pltpu.VMEM((4, 4, 4, SHARD, BLK), jnp.bfloat16),
            pltpu.VMEM((SHARD, BLK), jnp.bfloat16),
            pltpu.VMEM((2, DOCS, BLK), jnp.bfloat16),
            pltpu.VMEM((32, 32, 256), jnp.bfloat16),
            *received,
            pltpu.SemaphoreType.DMA((7,)),
            pltpu.SemaphoreType.DMA((99,)),
            pltpu.SemaphoreType.DMA((99,)),
            pltpu.SemaphoreType.DMA((32,)),
            pltpu.SemaphoreType.DMA((32,)),
        ],
        compiler_params=pltpu.CompilerParams(
            collective_id=1, has_side_effects=True, vmem_limit_bytes=24 * MIB
        ),
        name="reduce_blocks",
    )(tables, gp, mask, docs_all)


def on_device(documents, expand_weight, sparse_weight, feature_lists, positives):
    core = lax.axis_index("label_2")
    group = lax.axis_index(AXES)
    pair = lax.dynamic_slice_in_dim(feature_lists, (group - core) * LBLK_DEV, 2 * LBLK_DEV, 0)
    pair = pair.reshape(2, LBLK_DEV * SLOTS)
    keys = jnp.where(core == 0, pair, pair[::-1]) * 512
    keys = jnp.pad(keys + jnp.arange(LBLK_DEV * SLOTS, dtype=jnp.int32)[None, :], ((0, 6), (0, 0)))
    weight = pltpu.with_memory_space_constraint(expand_weight, pltpu.HBM)
    docs_t = pltpu.with_memory_space_constraint(documents.T, pltpu.HBM)
    hid, docs_all, mask, tables = expand(keys, docs_t, weight)
    grad_sparse, gp = label_blocks(
        tables,
        (group * LBLK_DEV).astype(jnp.int32).reshape(1),
        positives.T,
        hid.reshape(FBLOCKS, DOCS, BLK),
        sparse_weight,
    )
    grad_expand = reduce_blocks(tables, gp, mask, docs_all)
    return (grad_expand, grad_sparse)


def solution(mesh):
    finer = Mesh(mesh.devices.reshape(mesh.shape["feat"], 4, 4, 2), AXES)
    return jax.shard_map(
        on_device,
        mesh=finer,
        in_specs=(P(None, LABEL), P(LABEL, "feat"), P(AXES, None, None, None), P(), P()),
        out_specs=(P(LABEL, "feat"), P(AXES, None, None, None)),
        check_vma=False,
    )
```
